32 devices in a mesh: dp: 4 (over x, core), ctx: 8 (over z, y).
Axes of the slice: x: 2, y: 2, z: 4, core: 2. Of those that a mesh axis runs over, the one named last changes fastest.
Arguments:
- query: bfloat16 [4, 1024, 2048], P('dp', 'ctx'), may hold values from -6 to 6
- keys: bfloat16 [4, 1024, 2048], P('dp', 'ctx'), may hold values from -6 to 6
- values: bfloat16 [4, 1024, 2048], P('dp', 'ctx'), may hold values from -6 to 6
- cotangent: bfloat16 [4, 1024, 2048], P('dp', 'ctx'), may hold values from -6 to 6
- long_filter: bfloat16 [1024, 2048], P('ctx'), may hold values from -1.05 to 1.05, as said below
- short_weights: float32 [3, 3, 2048], replicated, may hold values from -3 to 3
- skip: float32 [2048], replicated, may hold values from -4 to 4
- lengths: int32 [4, 16], P('dp'), may hold values from 1 to 256, 1024 in all within a row
Outputs:
- gated: bfloat16 [4, 1024, 2048], P('dp', 'ctx')
- grad_query: bfloat16 [4, 1024, 2048], P('dp', 'ctx')
- grad_keys: bfloat16 [4, 1024, 2048], P('dp', 'ctx')
- grad_values: bfloat16 [4, 1024, 2048], P('dp', 'ctx')
- grad_filter: float32 [1024, 2048], P('ctx', 'dp')
- grad_short: float32 [3, 3, 2048], replicated
- grad_skip: float32 [2048], replicated
The draws below stay inside these ranges and needn't reach their ends.
Inputs may be any that keep to these rules, and one draw needn't show every extreme that they name: Each row lists, in order, the lengths of the 16 documents packed into one sequence; they sum to 1024 and the longest is exactly 256. `long_filter`: one filter for every channel over the lags 0 .. 1023.
All inputs are finite; a program needn't handle non-finite values.
Results may differ from the reference program's by a relative error of at most 0.024.
Values may be sent and summed in bfloat16 or wider, within the bound.
No kernel may reach another device: no remote copies, remote signals or barrier semaphores. Data moves between devices by JAX's collectives and lax.ppermute only.
A program may use at most 192 MiB of HBM per device.

```python
import math
import jax
import jax.numpy as jnp
import numpy as np
from jax import lax

C = 2048
SHORT = 3
DOCS = 16
SEQ = 1024
SEQS = 4
TOKENS = 4096


def draw_long_filter(key, part):
    rate_key, noise_key = jax.random.split(key)
    lag_times = jnp.arange(SEQ, dtype=jnp.float32)[:, None]
    log_span = jax.random.uniform(rate_key, (1, C), jnp.float32, math.log(30.0), math.log(8.0 * SEQ))
    rough_part = jax.random.truncated_normal(noise_key, -4.0, 4.0, (SEQ, C), jnp.float32)
    decay_span = jnp.exp(log_span)
    scaling = jnp.sqrt(jnp.expm1(-2.0 / decay_span) / jnp.expm1(-2.0 * SEQ / decay_span))
    return (scaling * jnp.exp(-lag_times / decay_span) * rough_part).astype(jnp.bfloat16)


def block_levels(key, extent, cuts, smallest, largest):
    factor_of = 1.0
    for dim, shards_of in cuts:
        steps = jax.random.uniform(jax.random.fold_in(jax.random.fold_in(key, 6), dim), (shards_of,), jnp.float32, smallest / len(cuts), largest / len(cuts))
        factor_of = factor_of * jnp.repeat(jnp.exp(steps), extent[dim] // shards_of).reshape((-1,) + (1,) * (len(extent) - 1 - dim))
    return factor_of


def profile(number_of, total, most, slope):
    portions = [(1 << 20) // math.isqrt(standing ** slope) + 1 for standing in range(2, number_of + 1)]
    surplus, counts = total - most - (number_of - 1), [1] * (number_of - 1)
    while surplus > 0:
        free = [i for i in range(number_of - 1) if counts[i] < most]
        whole, left = sum([portions[i] for i in free]), surplus
        for i in free:
            extra = min(most - counts[i], max(1, left * portions[i] // whole), surplus)
            counts[i] = counts[i] + extra
            surplus = surplus - extra
    return np.array([most] + counts)


def ragged(own_key, count, total, reach, skew):
    if count == 2:
        one = jax.random.randint(own_key, (), max(1, total - reach), min(reach, total - 1) + 1)
        return jnp.stack([one, total - one])
    sizes = jnp.asarray(profile(count, total, reach, skew), jnp.int32)
    couples = (count - 1) // 2
    giver, taker = sizes[1:1 + 2 * couples:2], sizes[2:2 + 2 * couples:2]
    slack = jnp.minimum(giver - 1, reach - taker)
    passed = jax.random.randint(jax.random.fold_in(own_key, 1), (couples,), 0, 1 << 20) % (slack + 1)
    sizes = sizes.at[1:1 + 2 * couples:2].set(giver - passed).at[2:2 + 2 * couples:2].set(taker + passed)
    return sizes[jax.random.permutation(jax.random.fold_in(own_key, 2), count)]


def normal_values(rng, dims, deviation, most, pieces=(), kind=jnp.bfloat16):
    array = deviation * jax.random.normal(rng, dims, jnp.float32)
    if pieces:
        array = array * block_levels(rng, dims, pieces, -0.22, 0.18)
    return jnp.clip(array, -most, most).astype(kind)


def setup_inputs(seed: int = 0) -> dict:
    key_list = jax.random.split(jax.random.key(seed), 9)
    return {
        "query": normal_values(key_list[0], (SEQS, SEQ, C), 1.0, 6.0, ((0, 4), (1, 8))),
        "keys": normal_values(key_list[1], (SEQS, SEQ, C), 1.0, 6.0, ((0, 4), (1, 8))),
        "values": normal_values(key_list[2], (SEQS, SEQ, C), 1.0, 6.0, ((0, 4), (1, 8))),
        "cotangent": normal_values(key_list[3], (SEQS, SEQ, C), 1.0, 6.0, ((0, 4), (1, 8))),
        "long_filter": draw_long_filter(jax.random.fold_in(key_list[8], 71), 0),
        "short_weights": normal_values(key_list[5], (3, SHORT, C), 0.5, 3.0, (), jnp.float32),
        "skip": normal_values(key_list[6], (C,), 1.0, 4.0, (), jnp.float32),
        "lengths": jax.vmap(lambda own: ragged(own, DOCS, SEQ, SEQ // 4, 2))(jax.random.split(key_list[7], SEQS)).reshape((SEQS, DOCS)).astype(jnp.int32),
    }


def causal_conv(signal, kernel):
    length = signal.shape[0]
    spectrum = jnp.fft.rfft(signal, n=2 * length, axis=0) * jnp.fft.rfft(kernel, n=2 * length, axis=0)
    return jnp.fft.irfft(spectrum, n=2 * length, axis=0)[:length]


def causal_corr(later, earlier):
    length = later.shape[0]
    spectrum = jnp.fft.rfft(later, n=2 * length, axis=0) * jnp.conj(jnp.fft.rfft(earlier, n=2 * length, axis=0))
    return jnp.fft.irfft(spectrum, n=2 * length, axis=0)[:length]


def shifted_down(wide, offset):
    return jnp.concatenate([jnp.zeros((offset, wide.shape[1]), wide.dtype), wide[:-offset]], 0)


def shifted_up(wide, offset):
    return jnp.concatenate([wide[offset:], jnp.zeros((offset, wide.shape[1]), wide.dtype)], 0)


def short_forward(source, weights, valid):
    wide = source.astype(jnp.float32)
    summed = weights[0] * wide
    for offset in range(1, weights.shape[0]):
        summed = summed + jnp.where(valid[offset][:, None], weights[offset] * shifted_down(wide, offset), 0.0)
    return summed


def short_backward(source, grad_short, weights, valid):
    wide = source.astype(jnp.float32)
    grad_source = weights[0] * grad_short
    weight_grads = [jnp.sum(wide * grad_short, axis=0)]
    for offset in range(1, weights.shape[0]):
        masked = jnp.where(valid[offset][:, None], grad_short, 0.0)
        grad_source = grad_source + weights[offset] * shifted_up(masked, offset)
        weight_grads.append(jnp.sum(masked * shifted_down(wide, offset), axis=0))
    return grad_source, jnp.stack(weight_grads)


def sequence_pass(inputs, short_weights, filter_wide, skip):
    q_rows, k_rows, v_rows, upstream, doc_len = inputs
    seq_len = q_rows.shape[0]
    taps = short_weights.shape[1]
    position = jnp.arange(seq_len, dtype=jnp.int32)
    starts = jnp.cumsum(doc_len) - doc_len
    begin = jnp.max(jnp.where(starts[None, :] <= position[:, None], starts[None, :], 0), axis=1)
    valid = position[None, :] - jnp.arange(taps, dtype=jnp.int32)[:, None] >= begin[None, :]
    q_short = short_forward(q_rows, short_weights[0], valid).astype(jnp.bfloat16)
    k_short = short_forward(k_rows, short_weights[1], valid).astype(jnp.bfloat16)
    v_short = short_forward(v_rows, short_weights[2], valid).astype(jnp.bfloat16)
    mixed = (k_short.astype(jnp.float32) * v_short.astype(jnp.float32)).astype(jnp.bfloat16)
    mixed_wide = mixed.astype(jnp.float32)
    conv = causal_conv(mixed_wide, filter_wide) + skip * mixed_wide
    gated = (q_short.astype(jnp.float32) * conv).astype(jnp.bfloat16)
    upstream_wide = upstream.astype(jnp.float32)
    grad_conv = (upstream_wide * q_short.astype(jnp.float32)).astype(jnp.bfloat16)
    grad_wide = grad_conv.astype(jnp.float32)
    grad_qs = upstream_wide * conv
    grad_mixed = causal_corr(grad_wide, filter_wide) + skip * grad_wide
    grad_ks = grad_mixed * v_short.astype(jnp.float32)
    grad_vs = grad_mixed * k_short.astype(jnp.float32)
    grad_filter = causal_corr(grad_wide, mixed_wide)
    grad_q, short_q = short_backward(q_rows, grad_qs, short_weights[0], valid)
    grad_k, short_k = short_backward(k_rows, grad_ks, short_weights[1], valid)
    grad_v, short_v = short_backward(v_rows, grad_vs, short_weights[2], valid)
    return (gated, grad_q.astype(jnp.bfloat16), grad_k.astype(jnp.bfloat16), grad_v.astype(jnp.bfloat16),
            grad_filter, jnp.stack([short_q, short_k, short_v]), jnp.sum(grad_wide * mixed_wide, axis=0))


def reference(query, keys, values, cotangent, long_filter, short_weights, skip, lengths):
    filter_wide = long_filter.astype(jnp.float32)
    results = lax.map(lambda inputs: sequence_pass(inputs, short_weights, filter_wide, skip),
                      (query, keys, values, cotangent, lengths))
    gated, grad_query, grad_keys, grad_values, filter_part, short_part, skip_part = results
    scale = 1.0 / TOKENS
    return (gated, grad_query, grad_keys, grad_values,
            jnp.sum(filter_part, axis=0) * scale, jnp.sum(short_part, axis=0) * scale,
            jnp.sum(skip_part, axis=0) * scale)
```

```python
import math

import jax
import jax.numpy as jnp
import ml_dtypes
import numpy as np
from jax import lax
from jax.sharding import PartitionSpec as P


def shifted(x, axis, by):
    length = lax.axis_size(axis)
    pairs = [(i, i + by) for i in range(length) if 0 <= i + by < length]
    return lax.ppermute(x, axis, pairs)


def table_halves(table):
    upper = table.astype(ml_dtypes.bfloat16)
    lower = (table - upper.astype(np.float64)).astype(ml_dtypes.bfloat16)
    return jnp.asarray(upper), jnp.asarray(lower)


def split_product(form, table, data):
    upper, lower = table_halves(table)
    wide = jnp.float32
    if data.dtype == jnp.bfloat16:
        total = jnp.einsum(form, upper, data, preferred_element_type=wide)
        return total + jnp.einsum(form, lower, data, preferred_element_type=wide)
    data_upper = lax.optimization_barrier(data.astype(jnp.bfloat16))
    data_lower = (data - data_upper.astype(wide)).astype(jnp.bfloat16)
    total = jnp.einsum(form, upper, data_upper, preferred_element_type=wide)
    total = total + jnp.einsum(form, lower, data_upper, preferred_element_type=wide)
    return total + jnp.einsum(form, upper, data_lower, preferred_element_type=wide)


def factors(size):
    bits = size.bit_length() - 1
    inner = 1 << (bits // 2)
    return size // inner, inner


def twiddles(outer, inner, size):
    phase = 2.0 * np.pi * np.outer(np.arange(outer), np.arange(inner)) / size
    cosine = jnp.asarray(np.cos(phase), jnp.float32)[None, :, :, None]
    sine = jnp.asarray(np.sin(phase), jnp.float32)[None, :, :, None]
    return cosine, sine


def inner_table(inner, sign):
    phase = 2.0 * np.pi * np.outer(np.arange(inner), np.arange(inner)) / inner
    cosine, sine = np.cos(phase), sign * np.sin(phase)
    return np.block([[cosine, sine], [-sine, cosine]])


def fft_forward(signal):
    count, length, lanes = signal.shape
    size = 2 * length
    outer, inner = factors(size)
    half = outer // 2
    phase = 2.0 * np.pi * np.outer(np.arange(outer), np.arange(half)) / outer
    first = np.concatenate([np.cos(phase), -np.sin(phase)], 0)
    stage = split_product("kn,snqb->skqb", first, signal.reshape(count, half, inner, lanes))
    real_part, imag_part = stage[:, :outer], stage[:, outer:]
    cosine, sine = twiddles(outer, inner, size)
    turned = jnp.concatenate(
        [real_part * cosine + imag_part * sine, imag_part * cosine - real_part * sine], 2
    )
    return split_product("ab,skbc->skac", inner_table(inner, 1.0), turned)


def fft_inverse(spectrum, length):
    count, outer, twice, lanes = spectrum.shape
    inner = twice // 2
    size = outer * inner
    half = outer // 2
    stage = split_product("ab,skbc->skac", inner_table(inner, -1.0), spectrum)
    real_part, imag_part = stage[:, :, :inner], stage[:, :, inner:]
    cosine, sine = twiddles(outer, inner, size)
    turned = jnp.concatenate(
        [real_part * cosine - imag_part * sine, imag_part * cosine + real_part * sine], 1
    )
    phase = 2.0 * np.pi * np.outer(np.arange(half), np.arange(outer)) / outer
    last = np.concatenate([np.cos(phase), -np.sin(phase)], 1) / size
    return split_product("nk,skqb->snqb", last, turned).reshape(count, length, lanes)


def spectral_products(spectra):
    inner = spectra.shape[2] // 2
    parts = [(s[:, :inner], s[:, inner:]) for s in (spectra[0], spectra[1], spectra[2])]
    (f_re, f_im), (m_re, m_im), (g_re, g_im) = parts
    conv = jnp.concatenate([m_re * f_re - m_im * f_im, m_re * f_im + m_im * f_re], 1)
    back = jnp.concatenate([g_re * f_re + g_im * f_im, g_im * f_re - g_re * f_im], 1)
    cross = jnp.concatenate([g_re * m_re + g_im * m_im, g_im * m_re - g_re * m_im], 1)
    return jnp.stack([conv, back, cross])


def local(query, keys, values, cotangent, long_filter, short_weights, skip, lengths):
    parts = lax.axis_size("ctx")
    index = lax.axis_index("ctx")
    groups = lax.axis_size("dp")
    q_rows, k_rows, v_rows, c_rows = query[0], keys[0], values[0], cotangent[0]
    rows, chans = q_rows.shape
    taps = short_weights.shape[1]
    head = taps - 1
    seq_len = rows * parts
    lanes = chans // parts
    ext = rows + head
    doc_len = lengths[0]
    starts = jnp.cumsum(doc_len) - doc_len

    position = index * rows + jnp.arange(ext, dtype=jnp.int32)
    begin = jnp.max(jnp.where(starts[None, :] <= position[:, None], starts[None, :], 0), axis=1)
    valid = position[None, :] - jnp.arange(taps, dtype=jnp.int32)[:, None] >= begin[None, :]
    valid_after = valid & (position < seq_len)[None, :]

    prev = shifted((q_rows[rows - head :], k_rows[rows - head :], v_rows[rows - head :]), "ctx", 1)
    nxt = shifted((q_rows[:head], k_rows[:head], v_rows[:head], c_rows[:head]), "ctx", -1)
    padded = [
        jnp.concatenate([prev[i], src, nxt[i]], 0).astype(jnp.float32)
        for i, src in enumerate((q_rows, k_rows, v_rows))
    ]

    def short_forward(wide, weights):
        summed = weights[0] * wide[head : head + ext]
        for offset in range(1, taps):
            begin_at = head - offset
            summed = summed + jnp.where(
                valid[offset][:, None], weights[offset] * wide[begin_at : begin_at + ext], 0.0
            )
        return summed.astype(jnp.bfloat16).astype(jnp.float32)

    q_short = short_forward(padded[0], short_weights[0])
    k_short = short_forward(padded[1], short_weights[1])
    v_short = short_forward(padded[2], short_weights[2])
    upstream = jnp.concatenate([c_rows, nxt[3]], 0).astype(jnp.float32)
    mixed = (k_short * v_short).astype(jnp.bfloat16)
    grad_conv = (upstream * q_short).astype(jnp.bfloat16)
    mixed_wide = mixed.astype(jnp.float32)
    grad_wide = grad_conv.astype(jnp.float32)

    sent = jnp.stack([long_filter, mixed[:rows], grad_conv[:rows]])
    columns = lax.all_to_all(sent, "ctx", 2, 1, tiled=True)
    spectra = fft_forward(columns)
    raw = fft_inverse(spectral_products(spectra), seq_len).astype(jnp.bfloat16)
    raw = jnp.concatenate([raw, jnp.zeros((3, head, lanes), raw.dtype)], 1)
    blocks = jnp.stack([raw[:, j * rows : j * rows + ext] for j in range(parts)], 1)
    back = lax.all_to_all(blocks, "ctx", 1, 3, tiled=True).reshape(3, ext, chans)
    back = back.astype(jnp.float32)

    conv = back[0] + skip * mixed_wide
    gated = (q_short[:rows] * conv[:rows]).astype(jnp.bfloat16)
    grad_qs = upstream * conv
    grad_mixed = back[1] + skip * grad_wide
    grad_ks = grad_mixed * v_short
    grad_vs = grad_mixed * k_short

    def short_backward(wide, grad_short, weights):
        grad_source = weights[0] * grad_short[:rows]
        weight_grads = [jnp.sum(wide[head : head + rows] * grad_short[:rows], axis=0)]
        for offset in range(1, taps):
            later = jnp.where(
                valid_after[offset, offset : offset + rows][:, None],
                grad_short[offset : offset + rows],
                0.0,
            )
            grad_source = grad_source + weights[offset] * later
            masked = jnp.where(valid[offset, :rows][:, None], grad_short[:rows], 0.0)
            begin_at = head - offset
            weight_grads.append(jnp.sum(masked * wide[begin_at : begin_at + rows], axis=0))
        return grad_source, jnp.stack(weight_grads)

    grad_q, short_q = short_backward(padded[0], grad_qs, short_weights[0])
    grad_k, short_k = short_backward(padded[1], grad_ks, short_weights[1])
    grad_v, short_v = short_backward(padded[2], grad_vs, short_weights[2])
    skip_grad = jnp.sum(grad_wide[:rows] * mixed_wide[:rows], axis=0)
    stats = jnp.concatenate(
        [jnp.stack([short_q, short_k, short_v]).reshape(3 * taps, chans), skip_grad[None]], 0
    )
    summed = lax.psum(stats, ("dp", "ctx"))
    filter_part = lax.psum_scatter(back[2, :rows], "dp", scatter_dimension=1, tiled=True)
    scale = 1.0 / (groups * seq_len)
    return (
        gated[None],
        grad_q.astype(jnp.bfloat16)[None],
        grad_k.astype(jnp.bfloat16)[None],
        grad_v.astype(jnp.bfloat16)[None],
        filter_part * scale,
        summed[: 3 * taps].reshape(3, taps, chans) * scale,
        summed[3 * taps] * scale,
    )


def solution(mesh):
    in_specs = (
        P("dp", "ctx", None),
        P("dp", "ctx", None),
        P("dp", "ctx", None),
        P("dp", "ctx", None),
        P("ctx", None),
        P(),
        P(),
        P("dp", None),
    )
    out_specs = (
        P("dp", "ctx", None),
        P("dp", "ctx", None),
        P("dp", "ctx", None),
        P("dp", "ctx", None),
        P("ctx", "dp"),
        P(),
        P(),
    )
    return jax.shard_map(local, mesh=mesh, in_specs=in_specs, out_specs=out_specs, check_vma=False)
```

```python
import math

import jax
import jax.numpy as jnp
import ml_dtypes
import numpy as np
from jax import lax
from jax.sharding import PartitionSpec as P


def shifted(x, axis, by):
    length = lax.axis_size(axis)
    pairs = [(i, i + by) for i in range(length) if 0 <= i + by < length]
    return lax.ppermute(x, axis, pairs)


def table_halves(table):
    upper = table.astype(ml_dtypes.bfloat16)
    lower = (table - upper.astype(np.float64)).astype(ml_dtypes.bfloat16)
    return jnp.asarray(upper), jnp.asarray(lower)


def split_product(form, table, data, exact=True):
    upper, lower = table_halves(table)
    wide = jnp.float32
    if not exact:
        return jnp.einsum(form, upper, data.astype(jnp.bfloat16), preferred_element_type=wide)
    if data.dtype == jnp.bfloat16:
        total = jnp.einsum(form, upper, data, preferred_element_type=wide)
        return total + jnp.einsum(form, lower, data, preferred_element_type=wide)
    data_upper = lax.optimization_barrier(data.astype(jnp.bfloat16))
    data_lower = (data - data_upper.astype(wide)).astype(jnp.bfloat16)
    total = jnp.einsum(form, upper, data_upper, preferred_element_type=wide)
    total = total + jnp.einsum(form, lower, data_upper, preferred_element_type=wide)
    return total + jnp.einsum(form, upper, data_lower, preferred_element_type=wide)


def factors(size):
    bits = size.bit_length() - 1
    inner = 1 << (bits // 2)
    return size // inner, inner


def twiddles(outer, inner, size):
    phase = 2.0 * np.pi * np.outer(np.arange(outer), np.arange(inner)) / size
    cosine = jnp.asarray(np.cos(phase), jnp.float32)[None, :, :, None]
    sine = jnp.asarray(np.sin(phase), jnp.float32)[None, :, :, None]
    return cosine, sine


def inner_table(inner, sign):
    phase = 2.0 * np.pi * np.outer(np.arange(inner), np.arange(inner)) / inner
    cosine, sine = np.cos(phase), sign * np.sin(phase)
    return np.block([[cosine, sine], [-sine, cosine]])


def fft_forward(signal):
    count, length, lanes = signal.shape
    size = 2 * length
    outer, inner = factors(size)
    half = outer // 2
    phase = 2.0 * np.pi * np.outer(np.arange(outer), np.arange(half)) / outer
    first = np.concatenate([np.cos(phase), -np.sin(phase)], 0)
    stage = split_product("kn,snqb->skqb", first, signal.reshape(count, half, inner, lanes))
    real_part, imag_part = stage[:, :outer], stage[:, outer:]
    cosine, sine = twiddles(outer, inner, size)
    turned = jnp.concatenate(
        [real_part * cosine + imag_part * sine, imag_part * cosine - real_part * sine], 2
    )
    return split_product("ab,skbc->skac", inner_table(inner, 1.0), turned, exact=False)


def fft_inverse(spectrum, length):
    count, outer, twice, lanes = spectrum.shape
    inner = twice // 2
    size = outer * inner
    half = outer // 2
    stage = split_product("ab,skbc->skac", inner_table(inner, -1.0), spectrum, exact=False)
    real_part, imag_part = stage[:, :, :inner], stage[:, :, inner:]
    cosine, sine = twiddles(outer, inner, size)
    turned = jnp.concatenate(
        [real_part * cosine - imag_part * sine, imag_part * cosine + real_part * sine], 1
    )
    phase = 2.0 * np.pi * np.outer(np.arange(half), np.arange(outer)) / outer
    last = np.concatenate([np.cos(phase), -np.sin(phase)], 1) / size
    return split_product("nk,skqb->snqb", last, turned, exact=False).reshape(count, length, lanes)


def spectral_products(spectra):
    inner = spectra.shape[2] // 2
    parts = [(s[:, :inner], s[:, inner:]) for s in (spectra[0], spectra[1], spectra[2])]
    (f_re, f_im), (m_re, m_im), (g_re, g_im) = parts
    conv = jnp.concatenate([m_re * f_re - m_im * f_im, m_re * f_im + m_im * f_re], 1)
    back = jnp.concatenate([g_re * f_re + g_im * f_im, g_im * f_re - g_re * f_im], 1)
    cross = jnp.concatenate([g_re * m_re + g_im * m_im, g_im * m_re - g_re * m_im], 1)
    return jnp.stack([conv, back, cross])


def butterfly_sum(data, axis):
    size = lax.axis_size(axis)
    step = 1
    while step < size:
        data = data + lax.ppermute(data, axis, [(i, i ^ step) for i in range(size)])
        step *= 2
    return data


def halving_scatter(data, axis):
    size = lax.axis_size(axis)
    index = lax.axis_index(axis)
    rows, chans = data.shape
    blocks = data.reshape(rows, size, chans // size)
    step = size // 2
    while step >= 1:
        half = blocks.shape[1] // 2
        upper = (index // step) % 2 == 1
        keep = jnp.where(upper, blocks[:, half:], blocks[:, :half])
        give = jnp.where(upper, blocks[:, :half], blocks[:, half:])
        blocks = keep + lax.ppermute(give, axis, [(i, i ^ step) for i in range(size)])
        step //= 2
    return blocks.reshape(rows, chans // size)


def local(query, keys, values, cotangent, long_filter, short_weights, skip, lengths):
    parts = lax.axis_size("ctx")
    index = lax.axis_index("ctx")
    groups = lax.axis_size("dp")
    q_rows, k_rows, v_rows, c_rows = query[0], keys[0], values[0], cotangent[0]
    rows, chans = q_rows.shape
    taps = short_weights.shape[1]
    head = taps - 1
    seq_len = rows * parts
    lanes = chans // parts
    ext = rows + head
    doc_len = lengths[0]
    starts = jnp.cumsum(doc_len) - doc_len

    position = index * rows + jnp.arange(ext, dtype=jnp.int32)
    begin = jnp.max(jnp.where(starts[None, :] <= position[:, None], starts[None, :], 0), axis=1)
    valid = position[None, :] - jnp.arange(taps, dtype=jnp.int32)[:, None] >= begin[None, :]
    valid_after = valid & (position < seq_len)[None, :]

    prev = shifted(jnp.stack([a[rows - head :] for a in (q_rows, k_rows, v_rows)]), "ctx", 1)
    nxt = shifted(jnp.stack([a[:head] for a in (q_rows, k_rows, v_rows, c_rows)]), "ctx", -1)
    padded = [
        jnp.concatenate([prev[i], src, nxt[i]], 0).astype(jnp.float32)
        for i, src in enumerate((q_rows, k_rows, v_rows))
    ]

    def short_forward(wide, weights):
        summed = weights[0] * wide[head : head + ext]
        for offset in range(1, taps):
            begin_at = head - offset
            summed = summed + jnp.where(
                valid[offset][:, None], weights[offset] * wide[begin_at : begin_at + ext], 0.0
            )
        return summed.astype(jnp.bfloat16).astype(jnp.float32)

    q_short = short_forward(padded[0], short_weights[0])
    k_short = short_forward(padded[1], short_weights[1])
    v_short = short_forward(padded[2], short_weights[2])
    upstream = jnp.concatenate([c_rows, nxt[3]], 0).astype(jnp.float32)
    mixed = (k_short * v_short).astype(jnp.bfloat16)
    grad_conv = (upstream * q_short).astype(jnp.bfloat16)
    mixed_wide = mixed.astype(jnp.float32)
    grad_wide = grad_conv.astype(jnp.float32)

    sent = jnp.stack([long_filter, mixed[:rows], grad_conv[:rows]])
    columns = lax.all_to_all(sent, "ctx", 2, 1, tiled=True)
    spectra = fft_forward(columns)
    raw = fft_inverse(spectral_products(spectra), seq_len).astype(jnp.bfloat16)
    raw = jnp.concatenate([raw, jnp.zeros((3, head, lanes), raw.dtype)], 1)
    blocks = jnp.stack([raw[:, j * rows : j * rows + ext] for j in range(parts)], 1)
    back = lax.all_to_all(blocks, "ctx", 1, 3, tiled=True).reshape(3, ext, chans)
    back = back.astype(jnp.float32)

    conv = back[0] + skip * mixed_wide
    gated = (q_short[:rows] * conv[:rows]).astype(jnp.bfloat16)
    grad_qs = upstream * conv
    grad_mixed = back[1] + skip * grad_wide
    grad_ks = grad_mixed * v_short
    grad_vs = grad_mixed * k_short

    def short_backward(wide, grad_short, weights):
        grad_source = weights[0] * grad_short[:rows]
        weight_grads = [jnp.sum(wide[head : head + rows] * grad_short[:rows], axis=0)]
        for offset in range(1, taps):
            later = jnp.where(
                valid_after[offset, offset : offset + rows][:, None],
                grad_short[offset : offset + rows],
                0.0,
            )
            grad_source = grad_source + weights[offset] * later
            masked = jnp.where(valid[offset, :rows][:, None], grad_short[:rows], 0.0)
            begin_at = head - offset
            weight_grads.append(jnp.sum(masked * wide[begin_at : begin_at + rows], axis=0))
        return grad_source, jnp.stack(weight_grads)

    grad_q, short_q = short_backward(padded[0], grad_qs, short_weights[0])
    grad_k, short_k = short_backward(padded[1], grad_ks, short_weights[1])
    grad_v, short_v = short_backward(padded[2], grad_vs, short_weights[2])
    skip_grad = jnp.sum(grad_wide[:rows] * mixed_wide[:rows], axis=0)
    stats = jnp.concatenate(
        [jnp.stack([short_q, short_k, short_v]).reshape(3 * taps, chans), skip_grad[None]], 0
    )
    summed = butterfly_sum(butterfly_sum(stats, "ctx"), "dp")
    filter_part = halving_scatter(back[2, :rows], "dp")
    scale = 1.0 / (groups * seq_len)
    return (
        gated[None],
        grad_q.astype(jnp.bfloat16)[None],
        grad_k.astype(jnp.bfloat16)[None],
        grad_v.astype(jnp.bfloat16)[None],
        filter_part * scale,
        summed[: 3 * taps].reshape(3, taps, chans) * scale,
        summed[3 * taps] * scale,
    )


def solution(mesh):
    in_specs = (
        P("dp", "ctx", None),
        P("dp", "ctx", None),
        P("dp", "ctx", None),
        P("dp", "ctx", None),
        P("ctx", None),
        P(),
        P(),
        P("dp", None),
    )
    out_specs = (
        P("dp", "ctx", None),
        P("dp", "ctx", None),
        P("dp", "ctx", None),
        P("dp", "ctx", None),
        P("ctx", "dp"),
        P(),
        P(),
    )
    return jax.shard_map(local, mesh=mesh, in_specs=in_specs, out_specs=out_specs, check_vma=False)
```

```python
import math

import jax
import jax.numpy as jnp
import ml_dtypes
import numpy as np
from jax import lax
from jax.sharding import PartitionSpec as P


def shifted(x, axis, by):
    length = lax.axis_size(axis)
    pairs = [(i, i + by) for i in range(length) if 0 <= i + by < length]
    return lax.ppermute(x, axis, pairs)


def table_halves(table):
    upper = table.astype(ml_dtypes.bfloat16)
    lower = (table - upper.astype(np.float64)).astype(ml_dtypes.bfloat16)
    return jnp.asarray(upper), jnp.asarray(lower)


def split_product(form, table, data, exact=True):
    upper, lower = table_halves(table)
    wide = jnp.float32
    if not exact:
        return jnp.einsum(form, upper, data.astype(jnp.bfloat16), preferred_element_type=wide)
    if data.dtype == jnp.bfloat16:
        total = jnp.einsum(form, upper, data, preferred_element_type=wide)
        return total + jnp.einsum(form, lower, data, preferred_element_type=wide)
    data_upper = lax.optimization_barrier(data.astype(jnp.bfloat16))
    data_lower = (data - data_upper.astype(wide)).astype(jnp.bfloat16)
    total = jnp.einsum(form, upper, data_upper, preferred_element_type=wide)
    total = total + jnp.einsum(form, lower, data_upper, preferred_element_type=wide)
    return total + jnp.einsum(form, upper, data_lower, preferred_element_type=wide)


def batched_product(table, data):
    count, outer, twice, lanes = data.shape
    upper = jnp.asarray(table.astype(ml_dtypes.bfloat16))
    upper = jnp.broadcast_to(upper, (count, outer, twice, twice))
    return jnp.einsum(
        "skab,skbc->skac", upper, data.astype(jnp.bfloat16), preferred_element_type=jnp.float32
    )


def factors(size):
    bits = size.bit_length() - 1
    inner = 1 << (bits // 2)
    return size // inner, inner


def twiddles(outer, inner, size):
    phase = 2.0 * np.pi * np.outer(np.arange(outer), np.arange(inner)) / size
    cosine = jnp.asarray(np.cos(phase), jnp.float32)[None, :, :, None]
    sine = jnp.asarray(np.sin(phase), jnp.float32)[None, :, :, None]
    return cosine, sine


def inner_table(inner, sign):
    phase = 2.0 * np.pi * np.outer(np.arange(inner), np.arange(inner)) / inner
    cosine, sine = np.cos(phase), sign * np.sin(phase)
    return np.block([[cosine, sine], [-sine, cosine]])


def fft_forward(signal):
    count, length, lanes = signal.shape
    size = 2 * length
    outer, inner = factors(size)
    half = outer // 2
    phase = 2.0 * np.pi * np.outer(np.arange(outer), np.arange(half)) / outer
    first = np.concatenate([np.cos(phase), -np.sin(phase)], 0)
    stage = split_product("kn,snqb->skqb", first, signal.reshape(count, half, inner, lanes))
    real_part, imag_part = stage[:, :outer], stage[:, outer:]
    cosine, sine = twiddles(outer, inner, size)
    turned = jnp.concatenate(
        [real_part * cosine + imag_part * sine, imag_part * cosine - real_part * sine], 2
    )
    return batched_product(inner_table(inner, 1.0), turned)


def fft_inverse(spectrum, length):
    count, outer, twice, lanes = spectrum.shape
    inner = twice // 2
    size = outer * inner
    half = outer // 2
    stage = batched_product(inner_table(inner, -1.0), spectrum)
    real_part, imag_part = stage[:, :, :inner], stage[:, :, inner:]
    cosine, sine = twiddles(outer, inner, size)
    turned = jnp.concatenate(
        [real_part * cosine - imag_part * sine, imag_part * cosine + real_part * sine], 1
    )
    phase = 2.0 * np.pi * np.outer(np.arange(half), np.arange(outer)) / outer
    last = np.concatenate([np.cos(phase), -np.sin(phase)], 1) / size
    return split_product("nk,skqb->snqb", last, turned, exact=False).reshape(count, length, lanes)


def spectral_products(spectra):
    inner = spectra.shape[2] // 2
    parts = [(s[:, :inner], s[:, inner:]) for s in (spectra[0], spectra[1], spectra[2])]
    (f_re, f_im), (m_re, m_im), (g_re, g_im) = parts
    conv = jnp.concatenate([m_re * f_re - m_im * f_im, m_re * f_im + m_im * f_re], 1)
    back = jnp.concatenate([g_re * f_re + g_im * f_im, g_im * f_re - g_re * f_im], 1)
    cross = jnp.concatenate([g_re * m_re + g_im * m_im, g_im * m_re - g_re * m_im], 1)
    return jnp.stack([conv, back, cross])


def butterfly_sum(data, axis):
    size = lax.axis_size(axis)
    step = 1
    while step < size:
        data = data + lax.ppermute(data, axis, [(i, i ^ step) for i in range(size)])
        step *= 2
    return data


def halving_scatter(data, axis):
    size = lax.axis_size(axis)
    index = lax.axis_index(axis)
    rows, chans = data.shape
    blocks = data.reshape(rows, size, chans // size)
    step = size // 2
    while step >= 1:
        half = blocks.shape[1] // 2
        upper = (index // step) % 2 == 1
        keep = jnp.where(upper, blocks[:, half:], blocks[:, :half])
        give = jnp.where(upper, blocks[:, :half], blocks[:, half:])
        blocks = keep + lax.ppermute(give, axis, [(i, i ^ step) for i in range(size)])
        step //= 2
    return blocks.reshape(rows, chans // size)


def local(query, keys, values, cotangent, long_filter, short_weights, skip, lengths):
    parts = lax.axis_size("ctx")
    index = lax.axis_index("ctx")
    groups = lax.axis_size("dp")
    q_rows, k_rows, v_rows, c_rows = query[0], keys[0], values[0], cotangent[0]
    rows, chans = q_rows.shape
    taps = short_weights.shape[1]
    head = taps - 1
    seq_len = rows * parts
    lanes = chans // parts
    ext = rows + head
    doc_len = lengths[0]
    starts = jnp.cumsum(doc_len) - doc_len

    position = index * rows + jnp.arange(ext, dtype=jnp.int32)
    begin = jnp.max(jnp.where(starts[None, :] <= position[:, None], starts[None, :], 0), axis=1)
    valid = position[None, :] - jnp.arange(taps, dtype=jnp.int32)[:, None] >= begin[None, :]
    valid_after = valid & (position < seq_len)[None, :]

    prev = shifted(jnp.stack([a[rows - head :] for a in (q_rows, k_rows, v_rows)]), "ctx", 1)
    nxt = shifted(jnp.stack([a[:head] for a in (q_rows, k_rows, v_rows, c_rows)]), "ctx", -1)
    padded = [
        jnp.concatenate([prev[i], src, nxt[i]], 0).astype(jnp.float32)
        for i, src in enumerate((q_rows, k_rows, v_rows))
    ]

    def short_forward(wide, weights):
        summed = weights[0] * wide[head : head + ext]
        for offset in range(1, taps):
            begin_at = head - offset
            summed = summed + jnp.where(
                valid[offset][:, None], weights[offset] * wide[begin_at : begin_at + ext], 0.0
            )
        return summed.astype(jnp.bfloat16).astype(jnp.float32)

    q_short = short_forward(padded[0], short_weights[0])
    k_short = short_forward(padded[1], short_weights[1])
    v_short = short_forward(padded[2], short_weights[2])
    upstream = jnp.concatenate([c_rows, nxt[3]], 0).astype(jnp.float32)
    mixed = (k_short * v_short).astype(jnp.bfloat16)
    grad_conv = (upstream * q_short).astype(jnp.bfloat16)
    mixed_wide = mixed.astype(jnp.float32)
    grad_wide = grad_conv.astype(jnp.float32)

    def to_columns(data):
        count = data.shape[0]
        split = data.reshape(count, rows, parts, lanes).transpose(0, 2, 1, 3)
        moved = lax.all_to_all(split, "ctx", 1, 1, tiled=True)
        return moved.reshape(count, seq_len, lanes)

    filter_columns = to_columns(long_filter[None])
    signal_columns = to_columns(jnp.stack([mixed[:rows], grad_conv[:rows]]))
    columns = jnp.concatenate([filter_columns, signal_columns], 0)
    spectra = fft_forward(columns)
    raw = fft_inverse(spectral_products(spectra), seq_len).astype(jnp.bfloat16)
    raw = jnp.concatenate([raw, jnp.zeros((3, head, lanes), raw.dtype)], 1)
    blocks = jnp.stack([raw[:, j * rows : j * rows + ext] for j in range(parts)], 1)
    back = lax.all_to_all(blocks, "ctx", 1, 3, tiled=True).reshape(3, ext, chans)
    back = back.astype(jnp.float32)

    conv = back[0] + skip * mixed_wide
    gated = (q_short[:rows] * conv[:rows]).astype(jnp.bfloat16)
    grad_qs = upstream * conv
    grad_mixed = back[1] + skip * grad_wide
    grad_ks = grad_mixed * v_short
    grad_vs = grad_mixed * k_short

    def short_backward(wide, grad_short, weights):
        grad_source = weights[0] * grad_short[:rows]
        weight_grads = [jnp.sum(wide[head : head + rows] * grad_short[:rows], axis=0)]
        for offset in range(1, taps):
            later = jnp.where(
                valid_after[offset, offset : offset + rows][:, None],
                grad_short[offset : offset + rows],
                0.0,
            )
            grad_source = grad_source + weights[offset] * later
            masked = jnp.where(valid[offset, :rows][:, None], grad_short[:rows], 0.0)
            begin_at = head - offset
            weight_grads.append(jnp.sum(masked * wide[begin_at : begin_at + rows], axis=0))
        return grad_source, jnp.stack(weight_grads)

    grad_q, short_q = short_backward(padded[0], grad_qs, short_weights[0])
    grad_k, short_k = short_backward(padded[1], grad_ks, short_weights[1])
    grad_v, short_v = short_backward(padded[2], grad_vs, short_weights[2])
    skip_grad = jnp.sum(grad_wide[:rows] * mixed_wide[:rows], axis=0)
    stats = jnp.concatenate(
        [jnp.stack([short_q, short_k, short_v]).reshape(3 * taps, chans), skip_grad[None]], 0
    )
    summed = butterfly_sum(butterfly_sum(stats, "ctx"), "dp")
    filter_part = halving_scatter(back[2, :rows], "dp")
    scale = 1.0 / (groups * seq_len)
    return (
        gated[None],
        grad_q.astype(jnp.bfloat16)[None],
        grad_k.astype(jnp.bfloat16)[None],
        grad_v.astype(jnp.bfloat16)[None],
        filter_part * scale,
        summed[: 3 * taps].reshape(3, taps, chans) * scale,
        summed[3 * taps] * scale,
    )


def solution(mesh):
    in_specs = (
        P("dp", "ctx", None),
        P("dp", "ctx", None),
        P("dp", "ctx", None),
        P("dp", "ctx", None),
        P("ctx", None),
        P(),
        P(),
        P("dp", None),
    )
    out_specs = (
        P("dp", "ctx", None),
        P("dp", "ctx", None),
        P("dp", "ctx", None),
        P("dp", "ctx", None),
        P("ctx", "dp"),
        P(),
        P(),
    )
    return jax.shard_map(local, mesh=mesh, in_specs=in_specs, out_specs=out_specs, check_vma=False)
```

```python
import math

import jax
import jax.numpy as jnp
import ml_dtypes
import numpy as np
from jax import lax
from jax.sharding import PartitionSpec as P


def shifted(x, axis, by):
    length = lax.axis_size(axis)
    pairs = [(i, i + by) for i in range(length) if 0 <= i + by < length]
    return lax.ppermute(x, axis, pairs)


def table_halves(table):
    upper = table.astype(ml_dtypes.bfloat16)
    lower = (table - upper.astype(np.float64)).astype(ml_dtypes.bfloat16)
    return jnp.asarray(upper), jnp.asarray(lower)


def split_product(form, table, data, exact=True):
    upper, lower = table_halves(table)
    wide = jnp.float32
    if not exact:
        return jnp.einsum(form, upper, data.astype(jnp.bfloat16), preferred_element_type=wide)
    if data.dtype == jnp.bfloat16:
        total = jnp.einsum(form, upper, data, preferred_element_type=wide)
        return total + jnp.einsum(form, lower, data, preferred_element_type=wide)
    data_upper = lax.optimization_barrier(data.astype(jnp.bfloat16))
    data_lower = (data - data_upper.astype(wide)).astype(jnp.bfloat16)
    total = jnp.einsum(form, upper, data_upper, preferred_element_type=wide)
    total = total + jnp.einsum(form, lower, data_upper, preferred_element_type=wide)
    return total + jnp.einsum(form, upper, data_lower, preferred_element_type=wide)


def batched_product(table, data):
    count, outer, twice, lanes = data.shape
    upper = jnp.asarray(table.astype(ml_dtypes.bfloat16))
    upper = jnp.broadcast_to(upper, (count, outer, twice, twice))
    return jnp.einsum(
        "skab,skbc->skac", upper, data.astype(jnp.bfloat16), preferred_element_type=jnp.float32
    )


def factors(size):
    bits = size.bit_length() - 1
    inner = 1 << (bits // 2)
    return size // inner, inner


def twiddles(outer, inner, size):
    phase = 2.0 * np.pi * np.outer(np.arange(outer), np.arange(inner)) / size
    cosine = jnp.asarray(np.cos(phase), jnp.float32)[None, :, :, None]
    sine = jnp.asarray(np.sin(phase), jnp.float32)[None, :, :, None]
    return cosine, sine


def inner_table(inner, sign):
    phase = 2.0 * np.pi * np.outer(np.arange(inner), np.arange(inner)) / inner
    cosine, sine = np.cos(phase), sign * np.sin(phase)
    return np.block([[cosine, sine], [-sine, cosine]])


def fft_forward(signal):
    count, length, lanes = signal.shape
    size = 2 * length
    outer, inner = factors(size)
    half = outer // 2
    phase = 2.0 * np.pi * np.outer(np.arange(outer), np.arange(half)) / outer
    first = np.concatenate([np.cos(phase), -np.sin(phase)], 0)
    stage = split_product("kn,snqb->skqb", first, signal.reshape(count, half, inner, lanes))
    real_part, imag_part = stage[:, :outer], stage[:, outer:]
    cosine, sine = twiddles(outer, inner, size)
    turned = jnp.concatenate(
        [real_part * cosine + imag_part * sine, imag_part * cosine - real_part * sine], 2
    )
    return split_product("ab,skbc->skac", inner_table(inner, 1.0), turned, exact=False)


def fft_inverse(spectrum, length):
    count, outer, twice, lanes = spectrum.shape
    inner = twice // 2
    size = outer * inner
    half = outer // 2
    stage = split_product("ab,skbc->skac", inner_table(inner, -1.0), spectrum, exact=False)
    real_part, imag_part = stage[:, :, :inner], stage[:, :, inner:]
    cosine, sine = twiddles(outer, inner, size)
    turned = jnp.concatenate(
        [real_part * cosine - imag_part * sine, imag_part * cosine + real_part * sine], 1
    )
    phase = 2.0 * np.pi * np.outer(np.arange(half), np.arange(outer)) / outer
    last = np.concatenate([np.cos(phase), -np.sin(phase)], 1) / size
    return split_product("nk,skqb->snqb", last, turned, exact=False).reshape(count, length, lanes)


def spectral_products(spectra):
    inner = spectra.shape[2] // 2
    parts = [(s[:, :inner], s[:, inner:]) for s in (spectra[0], spectra[1], spectra[2])]
    (f_re, f_im), (m_re, m_im), (g_re, g_im) = parts
    conv = jnp.concatenate([m_re * f_re - m_im * f_im, m_re * f_im + m_im * f_re], 1)
    back = jnp.concatenate([g_re * f_re + g_im * f_im, g_im * f_re - g_re * f_im], 1)
    cross = jnp.concatenate([g_re * m_re + g_im * m_im, g_im * m_re - g_re * m_im], 1)
    return jnp.stack([conv, back, cross])


def all_sum(data, axis):
    size = lax.axis_size(axis)
    total = data
    for step in range(1, size):
        total = total + lax.ppermute(data, axis, [(i, (i + step) % size) for i in range(size)])
    return total


def halving_scatter(data, axis):
    size = lax.axis_size(axis)
    index = lax.axis_index(axis)
    rows, chans = data.shape
    blocks = data.reshape(rows, size, chans // size)
    step = size // 2
    while step >= 1:
        half = blocks.shape[1] // 2
        upper = (index // step) % 2 == 1
        keep = jnp.where(upper, blocks[:, half:], blocks[:, :half])
        give = jnp.where(upper, blocks[:, :half], blocks[:, half:])
        blocks = keep + lax.ppermute(give, axis, [(i, i ^ step) for i in range(size)])
        step //= 2
    return blocks.reshape(rows, chans // size)


def local(query, keys, values, cotangent, long_filter, short_weights, skip, lengths):
    parts = lax.axis_size("ctx")
    index = lax.axis_index("ctx")
    groups = lax.axis_size("dp")
    q_rows, k_rows, v_rows, c_rows = query[0], keys[0], values[0], cotangent[0]
    rows, chans = q_rows.shape
    taps = short_weights.shape[1]
    head = taps - 1
    seq_len = rows * parts
    lanes = chans // parts
    ext = rows + head
    doc_len = lengths[0]
    starts = jnp.cumsum(doc_len) - doc_len

    position = index * rows + jnp.arange(ext, dtype=jnp.int32)
    begin = jnp.max(jnp.where(starts[None, :] <= position[:, None], starts[None, :], 0), axis=1)
    valid = position[None, :] - jnp.arange(taps, dtype=jnp.int32)[:, None] >= begin[None, :]
    valid_after = valid & (position < seq_len)[None, :]

    prev = shifted(jnp.stack([a[rows - head :] for a in (q_rows, k_rows, v_rows)]), "ctx", 1)
    nxt = shifted(jnp.stack([a[:head] for a in (q_rows, k_rows, v_rows, c_rows)]), "ctx", -1)
    padded = [
        jnp.concatenate([prev[i], src, nxt[i]], 0).astype(jnp.float32)
        for i, src in enumerate((q_rows, k_rows, v_rows))
    ]

    def short_forward(wide, weights):
        summed = weights[0] * wide[head : head + ext]
        for offset in range(1, taps):
            begin_at = head - offset
            summed = summed + jnp.where(
                valid[offset][:, None], weights[offset] * wide[begin_at : begin_at + ext], 0.0
            )
        return summed.astype(jnp.bfloat16).astype(jnp.float32)

    q_short = short_forward(padded[0], short_weights[0])
    k_short = short_forward(padded[1], short_weights[1])
    v_short = short_forward(padded[2], short_weights[2])
    upstream = jnp.concatenate([c_rows, nxt[3]], 0).astype(jnp.float32)
    mixed = (k_short * v_short).astype(jnp.bfloat16)
    grad_conv = (upstream * q_short).astype(jnp.bfloat16)
    mixed_wide = mixed.astype(jnp.float32)
    grad_wide = grad_conv.astype(jnp.float32)

    def to_columns(data):
        count = data.shape[0]
        split = data.reshape(count, rows, parts, lanes).transpose(0, 2, 1, 3)
        moved = lax.all_to_all(split, "ctx", 1, 1, tiled=True)
        return moved.reshape(count, seq_len, lanes)

    filter_columns = to_columns(long_filter[None])
    signal_columns = to_columns(jnp.stack([mixed[:rows], grad_conv[:rows]]))
    columns = jnp.concatenate([filter_columns, signal_columns], 0)
    spectra = fft_forward(columns)
    raw = fft_inverse(spectral_products(spectra), seq_len).astype(jnp.bfloat16)
    raw = jnp.concatenate([raw, jnp.zeros((3, head, lanes), raw.dtype)], 1)
    blocks = jnp.stack([raw[:, j * rows : j * rows + ext] for j in range(parts)], 1)
    back = lax.all_to_all(blocks, "ctx", 1, 3, tiled=True).reshape(3, ext, chans)
    back = back.astype(jnp.float32)

    conv = back[0] + skip * mixed_wide
    gated = (q_short[:rows] * conv[:rows]).astype(jnp.bfloat16)
    grad_qs = upstream * conv
    grad_mixed = back[1] + skip * grad_wide
    grad_ks = grad_mixed * v_short
    grad_vs = grad_mixed * k_short

    def short_backward(wide, grad_short, weights):
        grad_source = weights[0] * grad_short[:rows]
        weight_grads = [jnp.sum(wide[head : head + rows] * grad_short[:rows], axis=0)]
        for offset in range(1, taps):
            later = jnp.where(
                valid_after[offset, offset : offset + rows][:, None],
                grad_short[offset : offset + rows],
                0.0,
            )
            grad_source = grad_source + weights[offset] * later
            masked = jnp.where(valid[offset, :rows][:, None], grad_short[:rows], 0.0)
            begin_at = head - offset
            weight_grads.append(jnp.sum(masked * wide[begin_at : begin_at + rows], axis=0))
        return grad_source, jnp.stack(weight_grads)

    grad_q, short_q = short_backward(padded[0], grad_qs, short_weights[0])
    grad_k, short_k = short_backward(padded[1], grad_ks, short_weights[1])
    grad_v, short_v = short_backward(padded[2], grad_vs, short_weights[2])
    skip_grad = jnp.sum(grad_wide[:rows] * mixed_wide[:rows], axis=0)
    stats = jnp.concatenate(
        [jnp.stack([short_q, short_k, short_v]).reshape(3 * taps, chans), skip_grad[None]], 0
    )
    summed = all_sum(all_sum(stats, "ctx"), "dp")
    filter_part = halving_scatter(back[2, :rows], "dp")
    scale = 1.0 / (groups * seq_len)
    return (
        gated[None],
        grad_q.astype(jnp.bfloat16)[None],
        grad_k.astype(jnp.bfloat16)[None],
        grad_v.astype(jnp.bfloat16)[None],
        filter_part * scale,
        summed[: 3 * taps].reshape(3, taps, chans) * scale,
        summed[3 * taps] * scale,
    )


def solution(mesh):
    in_specs = (
        P("dp", "ctx", None),
        P("dp", "ctx", None),
        P("dp", "ctx", None),
        P("dp", "ctx", None),
        P("ctx", None),
        P(),
        P(),
        P("dp", None),
    )
    out_specs = (
        P("dp", "ctx", None),
        P("dp", "ctx", None),
        P("dp", "ctx", None),
        P("dp", "ctx", None),
        P("ctx", "dp"),
        P(),
        P(),
    )
    return jax.shard_map(local, mesh=mesh, in_specs=in_specs, out_specs=out_specs, check_vma=False)
```

```python
import math

import jax
import jax.numpy as jnp
import ml_dtypes
import numpy as np
from jax import lax
from jax.sharding import PartitionSpec as P


def shifted(x, axis, by):
    length = lax.axis_size(axis)
    pairs = [(i, i + by) for i in range(length) if 0 <= i + by < length]
    return lax.ppermute(x, axis, pairs)


def table_halves(table):
    upper = table.astype(ml_dtypes.bfloat16)
    lower = (table - upper.astype(np.float64)).astype(ml_dtypes.bfloat16)
    return jnp.asarray(upper), jnp.asarray(lower)


def split_product(form, table, data, exact=True):
    upper, lower = table_halves(table)
    wide = jnp.float32
    if not exact:
        return jnp.einsum(form, upper, data.astype(jnp.bfloat16), preferred_element_type=wide)
    if data.dtype == jnp.bfloat16:
        total = jnp.einsum(form, upper, data, preferred_element_type=wide)
        return total + jnp.einsum(form, lower, data, preferred_element_type=wide)
    data_upper = lax.optimization_barrier(data.astype(jnp.bfloat16))
    data_lower = (data - data_upper.astype(wide)).astype(jnp.bfloat16)
    total = jnp.einsum(form, upper, data_upper, preferred_element_type=wide)
    total = total + jnp.einsum(form, lower, data_upper, preferred_element_type=wide)
    return total + jnp.einsum(form, upper, data_lower, preferred_element_type=wide)


def batched_product(table, data):
    count, outer, twice, lanes = data.shape
    upper = jnp.asarray(table.astype(ml_dtypes.bfloat16))
    upper = jnp.broadcast_to(upper, (count, outer, twice, twice))
    return jnp.einsum(
        "skab,skbc->skac", upper, data.astype(jnp.bfloat16), preferred_element_type=jnp.float32
    )


def factors(size):
    bits = size.bit_length() - 1
    inner = 1 << (bits // 2)
    return size // inner, inner


def twiddles(outer, inner, size):
    phase = 2.0 * np.pi * np.outer(np.arange(outer), np.arange(inner)) / size
    cosine = jnp.asarray(np.cos(phase), jnp.float32)[None, :, :, None]
    sine = jnp.asarray(np.sin(phase), jnp.float32)[None, :, :, None]
    return cosine, sine


def inner_table(inner, sign):
    phase = 2.0 * np.pi * np.outer(np.arange(inner), np.arange(inner)) / inner
    cosine, sine = np.cos(phase), sign * np.sin(phase)
    return np.block([[cosine, sine], [-sine, cosine]])


def fft_forward(signal):
    count, length, lanes = signal.shape
    size = 2 * length
    outer, inner = factors(size)
    half = outer // 2
    phase = 2.0 * np.pi * np.outer(np.arange(outer), np.arange(half)) / outer
    first = np.concatenate([np.cos(phase), -np.sin(phase)], 0)
    stage = split_product("kn,snqb->skqb", first, signal.reshape(count, half, inner, lanes))
    real_part, imag_part = stage[:, :outer], stage[:, outer:]
    cosine, sine = twiddles(outer, inner, size)
    turned = jnp.concatenate(
        [real_part * cosine + imag_part * sine, imag_part * cosine - real_part * sine], 2
    )
    return split_product("ab,skbc->skac", inner_table(inner, 1.0), turned, exact=False)


def fft_inverse(spectrum, length):
    count, outer, twice, lanes = spectrum.shape
    inner = twice // 2
    size = outer * inner
    half = outer // 2
    stage = split_product("ab,skbc->skac", inner_table(inner, -1.0), spectrum, exact=False)
    real_part, imag_part = stage[:, :, :inner], stage[:, :, inner:]
    cosine, sine = twiddles(outer, inner, size)
    turned = jnp.concatenate(
        [real_part * cosine - imag_part * sine, imag_part * cosine + real_part * sine], 1
    )
    phase = 2.0 * np.pi * np.outer(np.arange(half), np.arange(outer)) / outer
    last = np.concatenate([np.cos(phase), -np.sin(phase)], 1) / size
    return split_product("nk,skqb->snqb", last, turned, exact=False).reshape(count, length, lanes)


def spectral_products(spectra):
    inner = spectra.shape[2] // 2
    parts = [(s[:, :inner], s[:, inner:]) for s in (spectra[0], spectra[1], spectra[2])]
    (f_re, f_im), (m_re, m_im), (g_re, g_im) = parts
    conv = jnp.concatenate([m_re * f_re - m_im * f_im, m_re * f_im + m_im * f_re], 1)
    back = jnp.concatenate([g_re * f_re + g_im * f_im, g_im * f_re - g_re * f_im], 1)
    cross = jnp.concatenate([g_re * m_re + g_im * m_im, g_im * m_re - g_re * m_im], 1)
    return jnp.stack([conv, back, cross])


def all_sum(data, axis):
    size = lax.axis_size(axis)
    total = data
    for step in range(1, size):
        total = total + lax.ppermute(data, axis, [(i, (i + step) % size) for i in range(size)])
    return total


def halving_scatter(data, axis):
    size = lax.axis_size(axis)
    index = lax.axis_index(axis)
    rows, chans = data.shape
    blocks = data.reshape(rows, size, chans // size)
    step = size // 2
    while step >= 1:
        half = blocks.shape[1] // 2
        upper = (index // step) % 2 == 1
        keep = jnp.where(upper, blocks[:, half:], blocks[:, :half])
        give = jnp.where(upper, blocks[:, :half], blocks[:, half:])
        blocks = keep + lax.ppermute(give, axis, [(i, i ^ step) for i in range(size)])
        step //= 2
    return blocks.reshape(rows, chans // size)


def local(query, keys, values, cotangent, long_filter, short_weights, skip, lengths):
    parts = lax.axis_size("ctx")
    index = lax.axis_index("ctx")
    groups = lax.axis_size("dp")
    q_rows, k_rows, v_rows, c_rows = query[0], keys[0], values[0], cotangent[0]
    rows, chans = q_rows.shape
    taps = short_weights.shape[1]
    head = taps - 1
    seq_len = rows * parts
    lanes = chans // parts
    ext = rows + head
    doc_len = lengths[0]
    starts = jnp.cumsum(doc_len) - doc_len

    position = index * rows + jnp.arange(ext, dtype=jnp.int32)
    begin = jnp.max(jnp.where(starts[None, :] <= position[:, None], starts[None, :], 0), axis=1)
    valid = position[None, :] - jnp.arange(taps, dtype=jnp.int32)[:, None] >= begin[None, :]
    valid_after = valid & (position < seq_len)[None, :]

    prev = shifted(jnp.stack([a[rows - head :] for a in (q_rows, k_rows, v_rows)]), "ctx", 1)
    nxt = shifted(jnp.stack([a[:head] for a in (q_rows, k_rows, v_rows, c_rows)]), "ctx", -1)
    padded = [
        jnp.concatenate([prev[i], src, nxt[i]], 0).astype(jnp.float32)
        for i, src in enumerate((q_rows, k_rows, v_rows))
    ]

    def short_forward(wide, weights):
        summed = weights[0] * wide[head : head + ext]
        for offset in range(1, taps):
            begin_at = head - offset
            summed = summed + jnp.where(
                valid[offset][:, None], weights[offset] * wide[begin_at : begin_at + ext], 0.0
            )
        return summed.astype(jnp.bfloat16).astype(jnp.float32)

    q_short = short_forward(padded[0], short_weights[0])
    k_short = short_forward(padded[1], short_weights[1])
    v_short = short_forward(padded[2], short_weights[2])
    upstream = jnp.concatenate([c_rows, nxt[3]], 0).astype(jnp.float32)
    mixed = (k_short * v_short).astype(jnp.bfloat16)
    grad_conv = (upstream * q_short).astype(jnp.bfloat16)
    mixed_wide = mixed.astype(jnp.float32)
    grad_wide = grad_conv.astype(jnp.float32)

    chunks = 2 if lanes % 2 == 0 else 1
    width = lanes // chunks

    def to_columns(data, part):
        count = data.shape[0]
        split = data.reshape(count, rows, parts, chunks, width)[:, :, :, part]
        moved = lax.all_to_all(split.transpose(0, 2, 1, 3), "ctx", 1, 1, tiled=True)
        return moved.reshape(count, seq_len, width)

    signals = jnp.stack([mixed[:rows], grad_conv[:rows]])
    returned = []
    for part in range(chunks):
        columns = jnp.concatenate(
            [to_columns(long_filter[None], part), to_columns(signals, part)], 0
        )
        spectra = fft_forward(columns)
        raw = fft_inverse(spectral_products(spectra), seq_len).astype(jnp.bfloat16)
        raw = jnp.concatenate([raw, jnp.zeros((3, head, width), raw.dtype)], 1)
        blocks = jnp.stack([raw[:, j * rows : j * rows + ext] for j in range(parts)], 1)
        returned.append(lax.all_to_all(blocks, "ctx", 1, 1, tiled=True))
    back = jnp.stack(returned, 3).transpose(0, 2, 1, 3, 4).reshape(3, ext, chans)
    back = back.astype(jnp.float32)

    conv = back[0] + skip * mixed_wide
    gated = (q_short[:rows] * conv[:rows]).astype(jnp.bfloat16)
    grad_qs = upstream * conv
    grad_mixed = back[1] + skip * grad_wide
    grad_ks = grad_mixed * v_short
    grad_vs = grad_mixed * k_short

    def short_backward(wide, grad_short, weights):
        grad_source = weights[0] * grad_short[:rows]
        weight_grads = [jnp.sum(wide[head : head + rows] * grad_short[:rows], axis=0)]
        for offset in range(1, taps):
            later = jnp.where(
                valid_after[offset, offset : offset + rows][:, None],
                grad_short[offset : offset + rows],
                0.0,
            )
            grad_source = grad_source + weights[offset] * later
            masked = jnp.where(valid[offset, :rows][:, None], grad_short[:rows], 0.0)
            begin_at = head - offset
            weight_grads.append(jnp.sum(masked * wide[begin_at : begin_at + rows], axis=0))
        return grad_source, jnp.stack(weight_grads)

    grad_q, short_q = short_backward(padded[0], grad_qs, short_weights[0])
    grad_k, short_k = short_backward(padded[1], grad_ks, short_weights[1])
    grad_v, short_v = short_backward(padded[2], grad_vs, short_weights[2])
    skip_grad = jnp.sum(grad_wide[:rows] * mixed_wide[:rows], axis=0)
    stats = jnp.concatenate(
        [jnp.stack([short_q, short_k, short_v]).reshape(3 * taps, chans), skip_grad[None]], 0
    )
    summed = all_sum(all_sum(stats, "ctx"), "dp")
    filter_part = halving_scatter(back[2, :rows], "dp")
    scale = 1.0 / (groups * seq_len)
    return (
        gated[None],
        grad_q.astype(jnp.bfloat16)[None],
        grad_k.astype(jnp.bfloat16)[None],
        grad_v.astype(jnp.bfloat16)[None],
        filter_part * scale,
        summed[: 3 * taps].reshape(3, taps, chans) * scale,
        summed[3 * taps] * scale,
    )


def solution(mesh):
    in_specs = (
        P("dp", "ctx", None),
        P("dp", "ctx", None),
        P("dp", "ctx", None),
        P("dp", "ctx", None),
        P("ctx", None),
        P(),
        P(),
        P("dp", None),
    )
    out_specs = (
        P("dp", "ctx", None),
        P("dp", "ctx", None),
        P("dp", "ctx", None),
        P("dp", "ctx", None),
        P("ctx", "dp"),
        P(),
        P(),
    )
    return jax.shard_map(local, mesh=mesh, in_specs=in_specs, out_specs=out_specs, check_vma=False)
```

```python
import math

import jax
import jax.numpy as jnp
import ml_dtypes
import numpy as np
from jax import lax
from jax.sharding import PartitionSpec as P


def shifted(x, axis, by):
    length = lax.axis_size(axis)
    pairs = [(i, i + by) for i in range(length) if 0 <= i + by < length]
    return lax.ppermute(x, axis, pairs)


def table_halves(table):
    upper = table.astype(ml_dtypes.bfloat16)
    lower = (table - upper.astype(np.float64)).astype(ml_dtypes.bfloat16)
    return jnp.asarray(upper), jnp.asarray(lower)


def split_product(form, table, data, exact=True):
    upper, lower = table_halves(table)
    wide = jnp.float32
    if not exact:
        return jnp.einsum(form, upper, data.astype(jnp.bfloat16), preferred_element_type=wide)
    if data.dtype == jnp.bfloat16:
        total = jnp.einsum(form, upper, data, preferred_element_type=wide)
        return total + jnp.einsum(form, lower, data, preferred_element_type=wide)
    data_upper = lax.optimization_barrier(data.astype(jnp.bfloat16))
    data_lower = (data - data_upper.astype(wide)).astype(jnp.bfloat16)
    total = jnp.einsum(form, upper, data_upper, preferred_element_type=wide)
    total = total + jnp.einsum(form, lower, data_upper, preferred_element_type=wide)
    return total + jnp.einsum(form, upper, data_lower, preferred_element_type=wide)


def batched_product(table, data):
    count, outer, twice, lanes = data.shape
    upper = jnp.asarray(table.astype(ml_dtypes.bfloat16))
    upper = jnp.broadcast_to(upper, (count, outer, twice, twice))
    return jnp.einsum(
        "skab,skbc->skac", upper, data.astype(jnp.bfloat16), preferred_element_type=jnp.float32
    )


def factors(size):
    bits = size.bit_length() - 1
    inner = 1 << (bits // 2)
    return size // inner, inner


def twiddles(outer, inner, size):
    phase = 2.0 * np.pi * np.outer(np.arange(outer), np.arange(inner)) / size
    cosine = jnp.asarray(np.cos(phase), jnp.float32)[None, :, :, None]
    sine = jnp.asarray(np.sin(phase), jnp.float32)[None, :, :, None]
    return cosine, sine


def inner_table(inner, sign):
    phase = 2.0 * np.pi * np.outer(np.arange(inner), np.arange(inner)) / inner
    cosine, sine = np.cos(phase), sign * np.sin(phase)
    return np.block([[cosine, sine], [-sine, cosine]])


def fft_forward(signal):
    count, length, lanes = signal.shape
    size = 2 * length
    outer, inner = factors(size)
    half = outer // 2
    phase = 2.0 * np.pi * np.outer(np.arange(outer), np.arange(half)) / outer
    first = np.concatenate([np.cos(phase), -np.sin(phase)], 0)
    stage = split_product("kn,snqb->skqb", first, signal.reshape(count, half, inner, lanes))
    real_part, imag_part = stage[:, :outer], stage[:, outer:]
    cosine, sine = twiddles(outer, inner, size)
    turned = jnp.concatenate(
        [real_part * cosine + imag_part * sine, imag_part * cosine - real_part * sine], 2
    )
    return split_product("ab,skbc->skac", inner_table(inner, 1.0), turned, exact=False)


def fft_inverse(spectrum, length):
    count, outer, twice, lanes = spectrum.shape
    inner = twice // 2
    size = outer * inner
    half = outer // 2
    stage = split_product("ab,skbc->skac", inner_table(inner, -1.0), spectrum, exact=False)
    real_part, imag_part = stage[:, :, :inner], stage[:, :, inner:]
    cosine, sine = twiddles(outer, inner, size)
    turned = jnp.concatenate(
        [real_part * cosine - imag_part * sine, imag_part * cosine + real_part * sine], 1
    )
    phase = 2.0 * np.pi * np.outer(np.arange(half), np.arange(outer)) / outer
    last = np.concatenate([np.cos(phase), -np.sin(phase)], 1) / size
    return split_product("nk,skqb->snqb", last, turned, exact=False).reshape(count, length, lanes)


def spectral_products(spectra):
    inner = spectra.shape[2] // 2
    parts = [(s[:, :inner], s[:, inner:]) for s in (spectra[0], spectra[1], spectra[2])]
    (f_re, f_im), (m_re, m_im), (g_re, g_im) = parts
    conv = jnp.concatenate([m_re * f_re - m_im * f_im, m_re * f_im + m_im * f_re], 1)
    back = jnp.concatenate([g_re * f_re + g_im * f_im, g_im * f_re - g_re * f_im], 1)
    cross = jnp.concatenate([g_re * m_re + g_im * m_im, g_im * m_re - g_re * m_im], 1)
    return jnp.stack([conv, back, cross])


def all_sum(data, axis):
    size = lax.axis_size(axis)
    total = data
    for step in range(1, size):
        total = total + lax.ppermute(data, axis, [(i, (i + step) % size) for i in range(size)])
    return total


def halving_scatter(data, axis):
    size = lax.axis_size(axis)
    index = lax.axis_index(axis)
    rows, chans = data.shape
    blocks = data.reshape(rows, size, chans // size)
    step = size // 2
    while step >= 1:
        half = blocks.shape[1] // 2
        upper = (index // step) % 2 == 1
        keep = jnp.where(upper, blocks[:, half:], blocks[:, :half])
        give = jnp.where(upper, blocks[:, :half], blocks[:, half:])
        blocks = keep + lax.ppermute(give, axis, [(i, i ^ step) for i in range(size)])
        step //= 2
    return blocks.reshape(rows, chans // size)


def local(query, keys, values, cotangent, long_filter, short_weights, skip, lengths):
    parts = lax.axis_size("ctx")
    index = lax.axis_index("ctx")
    groups = lax.axis_size("dp")
    q_rows, k_rows, v_rows, c_rows = query[0], keys[0], values[0], cotangent[0]
    rows, chans = q_rows.shape
    taps = short_weights.shape[1]
    head = taps - 1
    seq_len = rows * parts
    lanes = chans // parts
    ext = rows + head
    doc_len = lengths[0]
    starts = jnp.cumsum(doc_len) - doc_len

    position = index * rows + jnp.arange(ext, dtype=jnp.int32)
    begin = jnp.max(jnp.where(starts[None, :] <= position[:, None], starts[None, :], 0), axis=1)
    valid = position[None, :] - jnp.arange(taps, dtype=jnp.int32)[:, None] >= begin[None, :]
    valid_after = valid & (position < seq_len)[None, :]

    prev = shifted(jnp.stack([a[rows - head :] for a in (q_rows, k_rows, v_rows)]), "ctx", 1)
    nxt = shifted(jnp.stack([a[:head] for a in (q_rows, k_rows, v_rows, c_rows)]), "ctx", -1)
    padded = [
        jnp.concatenate([prev[i], src, nxt[i]], 0).astype(jnp.float32)
        for i, src in enumerate((q_rows, k_rows, v_rows))
    ]

    def short_forward(wide, weights):
        summed = weights[0] * wide[head : head + ext]
        for offset in range(1, taps):
            begin_at = head - offset
            summed = summed + jnp.where(
                valid[offset][:, None], weights[offset] * wide[begin_at : begin_at + ext], 0.0
            )
        return summed.astype(jnp.bfloat16).astype(jnp.float32)

    q_short = short_forward(padded[0], short_weights[0])
    k_short = short_forward(padded[1], short_weights[1])
    v_short = short_forward(padded[2], short_weights[2])
    upstream = jnp.concatenate([c_rows, nxt[3]], 0).astype(jnp.float32)
    mixed = (k_short * v_short).astype(jnp.bfloat16)
    grad_conv = (upstream * q_short).astype(jnp.bfloat16)
    mixed_wide = mixed.astype(jnp.float32)
    grad_wide = grad_conv.astype(jnp.float32)

    chunks = 2 if lanes % 2 == 0 else 1
    width = lanes // chunks

    def to_columns(data):
        count = data.shape[0]
        split = data.reshape(count, rows, parts, lanes).transpose(0, 2, 1, 3)
        moved = lax.all_to_all(split, "ctx", 1, 1, tiled=True)
        return moved.reshape(count, seq_len, chunks, width)

    all_columns = jnp.concatenate(
        [to_columns(long_filter[None]), to_columns(jnp.stack([mixed[:rows], grad_conv[:rows]]))], 0
    )
    returned = []
    for part in range(chunks):
        columns = all_columns[:, :, part]
        spectra = fft_forward(columns)
        raw = fft_inverse(spectral_products(spectra), seq_len).astype(jnp.bfloat16)
        raw = jnp.concatenate([raw, jnp.zeros((3, head, width), raw.dtype)], 1)
        blocks = jnp.stack([raw[:, j * rows : j * rows + ext] for j in range(parts)], 1)
        returned.append(lax.all_to_all(blocks, "ctx", 1, 1, tiled=True))
    back = jnp.stack(returned, 3).transpose(0, 2, 1, 3, 4).reshape(3, ext, chans)
    back = back.astype(jnp.float32)

    conv = back[0] + skip * mixed_wide
    gated = (q_short[:rows] * conv[:rows]).astype(jnp.bfloat16)
    grad_qs = upstream * conv
    grad_mixed = back[1] + skip * grad_wide
    grad_ks = grad_mixed * v_short
    grad_vs = grad_mixed * k_short

    def weight_grads(wide, grad_short):
        sums = [jnp.sum(wide[head : head + rows] * grad_short[:rows], axis=0)]
        for offset in range(1, taps):
            masked = jnp.where(valid[offset, :rows][:, None], grad_short[:rows], 0.0)
            begin_at = head - offset
            sums.append(jnp.sum(masked * wide[begin_at : begin_at + rows], axis=0))
        return jnp.stack(sums)

    def short_backward(grad_short, weights):
        grad_source = weights[0] * grad_short[:rows]
        for offset in range(1, taps):
            later = jnp.where(
                valid_after[offset, offset : offset + rows][:, None],
                grad_short[offset : offset + rows],
                0.0,
            )
            grad_source = grad_source + weights[offset] * later
        return grad_source

    grads = (grad_qs, grad_ks, grad_vs)
    short_part = [weight_grads(padded[i], grads[i]) for i in range(3)]
    skip_grad = jnp.sum(grad_wide[:rows] * mixed_wide[:rows], axis=0)
    stats = jnp.concatenate([jnp.stack(short_part).reshape(3 * taps, chans), skip_grad[None]], 0)
    grads, stats = lax.optimization_barrier((grads, stats))
    summed = all_sum(all_sum(stats, "ctx"), "dp")
    grad_q = short_backward(grads[0], short_weights[0])
    grad_k = short_backward(grads[1], short_weights[1])
    grad_v = short_backward(grads[2], short_weights[2])
    filter_part = halving_scatter(back[2, :rows], "dp")
    scale = 1.0 / (groups * seq_len)
    return (
        gated[None],
        grad_q.astype(jnp.bfloat16)[None],
        grad_k.astype(jnp.bfloat16)[None],
        grad_v.astype(jnp.bfloat16)[None],
        filter_part * scale,
        summed[: 3 * taps].reshape(3, taps, chans) * scale,
        summed[3 * taps] * scale,
    )


def solution(mesh):
    in_specs = (
        P("dp", "ctx", None),
        P("dp", "ctx", None),
        P("dp", "ctx", None),
        P("dp", "ctx", None),
        P("ctx", None),
        P(),
        P(),
        P("dp", None),
    )
    out_specs = (
        P("dp", "ctx", None),
        P("dp", "ctx", None),
        P("dp", "ctx", None),
        P("dp", "ctx", None),
        P("ctx", "dp"),
        P(),
        P(),
    )
    return jax.shard_map(local, mesh=mesh, in_specs=in_specs, out_specs=out_specs, check_vma=False)
```

```python
import math

import jax
import jax.numpy as jnp
import ml_dtypes
import numpy as np
from jax import lax
from jax.experimental import pallas as pl
from jax.experimental.pallas import tpu as pltpu
from jax.sharding import PartitionSpec as P


def shifted(x, axis, by):
    length = lax.axis_size(axis)
    pairs = [(i, i + by) for i in range(length) if 0 <= i + by < length]
    return lax.ppermute(x, axis, pairs)


def table_halves(table):
    upper = table.astype(ml_dtypes.bfloat16)
    lower = (table - upper.astype(np.float64)).astype(ml_dtypes.bfloat16)
    return jnp.asarray(upper), jnp.asarray(lower)


def split_product(form, table, data, exact=True):
    upper, lower = table_halves(table)
    wide = jnp.float32
    if not exact:
        return jnp.einsum(form, upper, data.astype(jnp.bfloat16), preferred_element_type=wide)
    if data.dtype == jnp.bfloat16:
        total = jnp.einsum(form, upper, data, preferred_element_type=wide)
        return total + jnp.einsum(form, lower, data, preferred_element_type=wide)
    data_upper = lax.optimization_barrier(data.astype(jnp.bfloat16))
    data_lower = (data - data_upper.astype(wide)).astype(jnp.bfloat16)
    total = jnp.einsum(form, upper, data_upper, preferred_element_type=wide)
    total = total + jnp.einsum(form, lower, data_upper, preferred_element_type=wide)
    return total + jnp.einsum(form, upper, data_lower, preferred_element_type=wide)


def batched_product(table, data):
    count, outer, twice, lanes = data.shape
    upper = jnp.asarray(table.astype(ml_dtypes.bfloat16))
    upper = jnp.broadcast_to(upper, (count, outer, twice, twice))
    return jnp.einsum(
        "skab,skbc->skac", upper, data.astype(jnp.bfloat16), preferred_element_type=jnp.float32
    )


def factors(size):
    bits = size.bit_length() - 1
    inner = 1 << (bits // 2)
    return size // inner, inner


def twiddles(outer, inner, size):
    phase = 2.0 * np.pi * np.outer(np.arange(outer), np.arange(inner)) / size
    cosine = jnp.asarray(np.cos(phase), jnp.float32)[None, :, :, None]
    sine = jnp.asarray(np.sin(phase), jnp.float32)[None, :, :, None]
    return cosine, sine


def inner_table(inner, sign):
    phase = 2.0 * np.pi * np.outer(np.arange(inner), np.arange(inner)) / inner
    cosine, sine = np.cos(phase), sign * np.sin(phase)
    return np.block([[cosine, sine], [-sine, cosine]])


def fft_forward(signal):
    count, length, lanes = signal.shape
    size = 2 * length
    outer, inner = factors(size)
    half = outer // 2
    phase = 2.0 * np.pi * np.outer(np.arange(outer), np.arange(half)) / outer
    first = np.concatenate([np.cos(phase), -np.sin(phase)], 0)
    stage = split_product("kn,snqb->skqb", first, signal.reshape(count, half, inner, lanes))
    real_part, imag_part = stage[:, :outer], stage[:, outer:]
    cosine, sine = twiddles(outer, inner, size)
    turned = jnp.concatenate(
        [real_part * cosine + imag_part * sine, imag_part * cosine - real_part * sine], 2
    )
    return split_product("ab,skbc->skac", inner_table(inner, 1.0), turned, exact=False)


def fft_inverse(spectrum, length):
    count, outer, twice, lanes = spectrum.shape
    inner = twice // 2
    size = outer * inner
    half = outer // 2
    stage = split_product("ab,skbc->skac", inner_table(inner, -1.0), spectrum, exact=False)
    real_part, imag_part = stage[:, :, :inner], stage[:, :, inner:]
    cosine, sine = twiddles(outer, inner, size)
    turned = jnp.concatenate(
        [real_part * cosine - imag_part * sine, imag_part * cosine + real_part * sine], 1
    )
    phase = 2.0 * np.pi * np.outer(np.arange(half), np.arange(outer)) / outer
    last = np.concatenate([np.cos(phase), -np.sin(phase)], 1) / size
    return split_product("nk,skqb->snqb", last, turned, exact=False).reshape(count, length, lanes)


def spectral_products(spectra):
    inner = spectra.shape[2] // 2
    parts = [(s[:, :inner], s[:, inner:]) for s in (spectra[0], spectra[1], spectra[2])]
    (f_re, f_im), (m_re, m_im), (g_re, g_im) = parts
    conv = jnp.concatenate([m_re * f_re - m_im * f_im, m_re * f_im + m_im * f_re], 1)
    back = jnp.concatenate([g_re * f_re + g_im * f_im, g_im * f_re - g_re * f_im], 1)
    cross = jnp.concatenate([g_re * m_re + g_im * m_im, g_im * m_re - g_re * m_im], 1)
    return jnp.stack([conv, back, cross])


def all_sum(data, axis):
    size = lax.axis_size(axis)
    total = data
    for step in range(1, size):
        total = total + lax.ppermute(data, axis, [(i, (i + step) % size) for i in range(size)])
    return total


def halving_scatter(data, axis):
    size = lax.axis_size(axis)
    index = lax.axis_index(axis)
    rows, chans = data.shape
    blocks = data.reshape(rows, size, chans // size)
    step = size // 2
    while step >= 1:
        half = blocks.shape[1] // 2
        upper = (index // step) % 2 == 1
        keep = jnp.where(upper, blocks[:, half:], blocks[:, :half])
        give = jnp.where(upper, blocks[:, :half], blocks[:, half:])
        blocks = keep + lax.ppermute(give, axis, [(i, i ^ step) for i in range(size)])
        step //= 2
    return blocks.reshape(rows, chans // size)


def epilogue_kernel(conv_ref, back_ref, src_ref, up_ref, mask_ref, w_ref, skip_ref, out_ref, stats_ref):
    wide, narrow = jnp.float32, jnp.bfloat16
    taps = w_ref.shape[1]
    head = taps - 1
    frame = src_ref.shape[1]
    rows = out_ref.shape[1]

    def mask(i):
        return mask_ref[i] > 0.5

    def down(x, by):
        return pltpu.roll(x, by, 0) if by else x

    def lift(x, by):
        return pltpu.roll(x, frame - by, 0) if by else x

    sources = [src_ref[i].astype(wide) for i in range(3)]
    weights = w_ref[...]
    shorts = []
    for i in range(3):
        total = weights[i, 0:1] * sources[i]
        for off in range(1, taps):
            total = total + jnp.where(mask(off), weights[i, off : off + 1] * down(sources[i], off), 0.0)
        shorts.append(total.astype(narrow).astype(wide))
    q_short, k_short, v_short = shorts
    upstream = up_ref[...].astype(wide)
    skip = skip_ref[...]
    mixed = (k_short * v_short).astype(narrow).astype(wide)
    grad_conv = (upstream * q_short).astype(narrow).astype(wide)
    conv = conv_ref[...].astype(wide) + skip * mixed
    grad_mixed = back_ref[...].astype(wide) + skip * grad_conv
    own = mask(2 * taps)
    out_ref[0] = lift(q_short * conv, head)[:rows].astype(narrow)
    grads = [upstream * conv, grad_mixed * v_short, grad_mixed * k_short]
    stats = []
    for i in range(3):
        grad = grads[i]
        acc = weights[i, 0:1] * grad
        stats.append(jnp.sum(jnp.where(own, sources[i] * grad, 0.0), axis=0, keepdims=True))
        for off in range(1, taps):
            later = lift(jnp.where(mask(taps + off), grad, 0.0), off)
            acc = acc + weights[i, off : off + 1] * later
            lagged = jnp.where(own & mask(off), down(sources[i], off) * grad, 0.0)
            stats.append(jnp.sum(lagged, axis=0, keepdims=True))
        out_ref[1 + i] = lift(acc, head)[:rows].astype(narrow)
    stats.append(jnp.sum(jnp.where(own, grad_conv * mixed, 0.0), axis=0, keepdims=True))
    width = stats[0].shape[1]
    stats.append(jnp.zeros((stats_ref.shape[0] - len(stats), width), wide))
    stats_ref[...] = jnp.concatenate(stats, 0)


def epilogue(back, sources, upstream, masks, short_weights, skip, rows):
    _, frame, chans = back.shape
    taps = short_weights.shape[1]
    block = 256 if chans % 256 == 0 else chans
    grid = (chans // block,)
    stat_rows = 16
    return pl.pallas_call(
        epilogue_kernel,
        grid=grid,
        in_specs=[
            pl.BlockSpec((None, frame, block), lambda c: (0, 0, c)),
            pl.BlockSpec((None, frame, block), lambda c: (1, 0, c)),
            pl.BlockSpec((3, frame, block), lambda c: (0, 0, c)),
            pl.BlockSpec((frame, block), lambda c: (0, c)),
            pl.BlockSpec(masks.shape, lambda c: (0, 0, 0)),
            pl.BlockSpec((3, taps, block), lambda c: (0, 0, c)),
            pl.BlockSpec((1, block), lambda c: (0, c)),
        ],
        out_specs=[
            pl.BlockSpec((4, rows, block), lambda c: (0, 0, c)),
            pl.BlockSpec((stat_rows, block), lambda c: (0, c)),
        ],
        out_shape=[
            jax.ShapeDtypeStruct((4, rows, chans), jnp.bfloat16),
            jax.ShapeDtypeStruct((stat_rows, chans), jnp.float32),
        ],
    )(back, back, sources, upstream, masks, short_weights, skip[None])


def local(query, keys, values, cotangent, long_filter, short_weights, skip, lengths):
    parts = lax.axis_size("ctx")
    index = lax.axis_index("ctx")
    groups = lax.axis_size("dp")
    q_rows, k_rows, v_rows, c_rows = query[0], keys[0], values[0], cotangent[0]
    rows, chans = q_rows.shape
    taps = short_weights.shape[1]
    head = taps - 1
    seq_len = rows * parts
    lanes = chans // parts
    ext = rows + head
    frame = -(-(rows + 2 * head) // 8) * 8
    doc_len = lengths[0]
    starts = jnp.cumsum(doc_len) - doc_len

    position = index * rows + jnp.arange(ext, dtype=jnp.int32)
    begin = jnp.max(jnp.where(starts[None, :] <= position[:, None], starts[None, :], 0), axis=1)
    valid = position[None, :] - jnp.arange(taps, dtype=jnp.int32)[:, None] >= begin[None, :]
    valid_after = valid & (position < seq_len)[None, :]

    prev = shifted(jnp.stack([a[rows - head :] for a in (q_rows, k_rows, v_rows)]), "ctx", 1)
    nxt = shifted(jnp.stack([a[:head] for a in (q_rows, k_rows, v_rows, c_rows)]), "ctx", -1)
    padded = [
        jnp.concatenate([prev[i], src, nxt[i]], 0).astype(jnp.float32)
        for i, src in enumerate((q_rows, k_rows, v_rows))
    ]

    def short_forward(wide, weights):
        summed = weights[0] * wide[head : head + ext]
        for offset in range(1, taps):
            begin_at = head - offset
            summed = summed + jnp.where(
                valid[offset][:, None], weights[offset] * wide[begin_at : begin_at + ext], 0.0
            )
        return summed.astype(jnp.bfloat16).astype(jnp.float32)

    q_short = short_forward(padded[0], short_weights[0])
    k_short = short_forward(padded[1], short_weights[1])
    v_short = short_forward(padded[2], short_weights[2])
    upstream = jnp.concatenate([c_rows, nxt[3]], 0).astype(jnp.float32)
    mixed = (k_short * v_short).astype(jnp.bfloat16)
    grad_conv = (upstream * q_short).astype(jnp.bfloat16)
    mixed_wide = mixed.astype(jnp.float32)
    grad_wide = grad_conv.astype(jnp.float32)

    chunks = 2 if lanes % 2 == 0 else 1
    width = lanes // chunks

    def to_columns(data):
        count = data.shape[0]
        split = data.reshape(count, rows, parts, lanes).transpose(0, 2, 1, 3)
        moved = lax.all_to_all(split, "ctx", 1, 1, tiled=True)
        return moved.reshape(count, seq_len, chunks, width)

    all_columns = jnp.concatenate(
        [to_columns(long_filter[None]), to_columns(jnp.stack([mixed[:rows], grad_conv[:rows]]))], 0
    )
    returned = []
    for part in range(chunks):
        columns = all_columns[:, :, part]
        spectra = fft_forward(columns)
        raw = fft_inverse(spectral_products(spectra), seq_len).astype(jnp.bfloat16)
        raw = jnp.concatenate(
            [jnp.zeros((3, head, width), raw.dtype), raw, jnp.zeros((3, frame - rows - head, width), raw.dtype)], 1
        )
        blocks = jnp.stack([raw[:, j * rows : j * rows + frame] for j in range(parts)], 1)
        returned.append(lax.all_to_all(blocks, "ctx", 1, 1, tiled=True))
    back = jnp.stack(returned, 3).transpose(0, 2, 1, 3, 4).reshape(3, frame, chans)

    spot = index * rows - head + jnp.arange(frame, dtype=jnp.int32)
    spot_begin = jnp.max(jnp.where(starts[None, :] <= spot[:, None], starts[None, :], 0), axis=1)
    spot_valid = spot[None, :] - jnp.arange(taps, dtype=jnp.int32)[:, None] >= spot_begin[None, :]
    spot_after = spot_valid & ((spot >= 0) & (spot < seq_len))[None, :]
    spot_own = ((spot >= index * rows) & (spot < index * rows + rows))[None, :]
    masks = jnp.concatenate([spot_valid, spot_after, spot_own], 0).astype(jnp.float32)
    masks = jnp.concatenate([masks, jnp.zeros(((-masks.shape[0]) % 8, frame), jnp.float32)], 0)
    tail = frame - rows - 2 * head
    sources = jnp.stack([
        jnp.concatenate([prev[i], src, nxt[i], jnp.zeros((tail, chans), src.dtype)], 0)
        for i, src in enumerate((q_rows, k_rows, v_rows))
    ])
    framed_up = jnp.concatenate(
        [jnp.zeros((head, chans), c_rows.dtype), c_rows, nxt[3], jnp.zeros((tail, chans), c_rows.dtype)], 0
    )
    outs, stats = epilogue(back, sources, framed_up, masks[:, :, None], short_weights, skip, rows)
    summed = all_sum(all_sum(stats[: 3 * taps + 1], "ctx"), "dp")
    gated, grad_q, grad_k, grad_v = outs[0], outs[1], outs[2], outs[3]
    filter_part = halving_scatter(back[2, head : head + rows].astype(jnp.float32), "dp")
    scale = 1.0 / (groups * seq_len)
    return (
        gated[None],
        grad_q.astype(jnp.bfloat16)[None],
        grad_k.astype(jnp.bfloat16)[None],
        grad_v.astype(jnp.bfloat16)[None],
        filter_part * scale,
        summed[: 3 * taps].reshape(3, taps, chans) * scale,
        summed[3 * taps] * scale,
    )


def solution(mesh):
    in_specs = (
        P("dp", "ctx", None),
        P("dp", "ctx", None),
        P("dp", "ctx", None),
        P("dp", "ctx", None),
        P("ctx", None),
        P(),
        P(),
        P("dp", None),
    )
    out_specs = (
        P("dp", "ctx", None),
        P("dp", "ctx", None),
        P("dp", "ctx", None),
        P("dp", "ctx", None),
        P("ctx", "dp"),
        P(),
        P(),
    )
    return jax.shard_map(local, mesh=mesh, in_specs=in_specs, out_specs=out_specs, check_vma=False)
```

```python
import math

import jax
import jax.numpy as jnp
import ml_dtypes
import numpy as np
from jax import lax
from jax.experimental import pallas as pl
from jax.experimental.pallas import tpu as pltpu
from jax.sharding import PartitionSpec as P


def shifted(x, axis, by):
    length = lax.axis_size(axis)
    pairs = [(i, i + by) for i in range(length) if 0 <= i + by < length]
    return lax.ppermute(x, axis, pairs)


def table_halves(table):
    upper = table.astype(ml_dtypes.bfloat16)
    lower = (table - upper.astype(np.float64)).astype(ml_dtypes.bfloat16)
    return jnp.asarray(upper), jnp.asarray(lower)


def split_product(form, table, data, exact=True):
    upper, lower = table_halves(table)
    wide = jnp.float32
    if not exact:
        return jnp.einsum(form, upper, data.astype(jnp.bfloat16), preferred_element_type=wide)
    if data.dtype == jnp.bfloat16:
        total = jnp.einsum(form, upper, data, preferred_element_type=wide)
        return total + jnp.einsum(form, lower, data, preferred_element_type=wide)
    data_upper = lax.optimization_barrier(data.astype(jnp.bfloat16))
    data_lower = (data - data_upper.astype(wide)).astype(jnp.bfloat16)
    total = jnp.einsum(form, upper, data_upper, preferred_element_type=wide)
    total = total + jnp.einsum(form, lower, data_upper, preferred_element_type=wide)
    return total + jnp.einsum(form, upper, data_lower, preferred_element_type=wide)


def batched_product(table, data):
    count, outer, twice, lanes = data.shape
    upper = jnp.asarray(table.astype(ml_dtypes.bfloat16))
    upper = jnp.broadcast_to(upper, (count, outer, twice, twice))
    return jnp.einsum(
        "skab,skbc->skac", upper, data.astype(jnp.bfloat16), preferred_element_type=jnp.float32
    )


def factors(size):
    bits = size.bit_length() - 1
    inner = 1 << (bits // 2)
    return size // inner, inner


def twiddles(outer, inner, size):
    phase = 2.0 * np.pi * np.outer(np.arange(outer), np.arange(inner)) / size
    cosine = jnp.asarray(np.cos(phase), jnp.float32)[None, :, :, None]
    sine = jnp.asarray(np.sin(phase), jnp.float32)[None, :, :, None]
    return cosine, sine


def inner_table(inner, sign):
    phase = 2.0 * np.pi * np.outer(np.arange(inner), np.arange(inner)) / inner
    cosine, sine = np.cos(phase), sign * np.sin(phase)
    return np.block([[cosine, sine], [-sine, cosine]])


def fft_forward(signal):
    count, length, lanes = signal.shape
    size = 2 * length
    outer, inner = factors(size)
    half = outer // 2
    phase = 2.0 * np.pi * np.outer(np.arange(outer), np.arange(half)) / outer
    first = np.concatenate([np.cos(phase), -np.sin(phase)], 0)
    stage = split_product("kn,snqb->skqb", first, signal.reshape(count, half, inner, lanes))
    real_part, imag_part = stage[:, :outer], stage[:, outer:]
    cosine, sine = twiddles(outer, inner, size)
    turned = jnp.concatenate(
        [real_part * cosine + imag_part * sine, imag_part * cosine - real_part * sine], 2
    )
    return split_product("ab,skbc->skac", inner_table(inner, 1.0), turned, exact=False)


def fft_inverse(spectrum, length):
    count, outer, twice, lanes = spectrum.shape
    inner = twice // 2
    size = outer * inner
    half = outer // 2
    stage = split_product("ab,skbc->skac", inner_table(inner, -1.0), spectrum, exact=False)
    real_part, imag_part = stage[:, :, :inner], stage[:, :, inner:]
    cosine, sine = twiddles(outer, inner, size)
    turned = jnp.concatenate(
        [real_part * cosine - imag_part * sine, imag_part * cosine + real_part * sine], 1
    )
    phase = 2.0 * np.pi * np.outer(np.arange(half), np.arange(outer)) / outer
    last = np.concatenate([np.cos(phase), -np.sin(phase)], 1) / size
    return split_product("nk,skqb->snqb", last, turned, exact=False).reshape(count, length, lanes)


def spectral_products(spectra):
    inner = spectra.shape[2] // 2
    parts = [(s[:, :inner], s[:, inner:]) for s in (spectra[0], spectra[1], spectra[2])]
    (f_re, f_im), (m_re, m_im), (g_re, g_im) = parts
    conv = jnp.concatenate([m_re * f_re - m_im * f_im, m_re * f_im + m_im * f_re], 1)
    back = jnp.concatenate([g_re * f_re + g_im * f_im, g_im * f_re - g_re * f_im], 1)
    cross = jnp.concatenate([g_re * m_re + g_im * m_im, g_im * m_re - g_re * m_im], 1)
    return jnp.stack([conv, back, cross])


def all_sum(data, axis):
    size = lax.axis_size(axis)
    total = data
    for step in range(1, size):
        total = total + lax.ppermute(data, axis, [(i, (i + step) % size) for i in range(size)])
    return total


def mesh_sum(data, axes):
    count = 1
    for axis in axes:
        count *= lax.axis_size(axis)
    rows, chans = data.shape
    pieces = data.reshape(rows, count, chans // count).transpose(1, 0, 2)
    mine = jnp.sum(lax.all_to_all(pieces, axes, 0, 0, tiled=True), axis=0)
    spread = jnp.broadcast_to(mine[None], (count,) + mine.shape)
    gathered = lax.all_to_all(spread, axes, 0, 0, tiled=True)
    return gathered.transpose(1, 0, 2).reshape(rows, chans)


def halving_scatter(data, axis):
    size = lax.axis_size(axis)
    index = lax.axis_index(axis)
    rows, chans = data.shape
    blocks = data.reshape(rows, size, chans // size)
    step = size // 2
    while step >= 1:
        half = blocks.shape[1] // 2
        upper = (index // step) % 2 == 1
        keep = jnp.where(upper, blocks[:, half:], blocks[:, :half])
        give = jnp.where(upper, blocks[:, :half], blocks[:, half:])
        blocks = keep + lax.ppermute(give, axis, [(i, i ^ step) for i in range(size)])
        step //= 2
    return blocks.reshape(rows, chans // size)


def epilogue_kernel(conv_ref, back_ref, src_ref, up_ref, mask_ref, w_ref, skip_ref, out_ref, stats_ref):
    wide, narrow = jnp.float32, jnp.bfloat16
    taps = w_ref.shape[1]
    head = taps - 1
    frame = src_ref.shape[1]
    rows = out_ref.shape[1]

    def mask(i):
        return mask_ref[i] > 0.5

    def down(x, by):
        return pltpu.roll(x, by, 0) if by else x

    def lift(x, by):
        return pltpu.roll(x, frame - by, 0) if by else x

    sources = [src_ref[i].astype(wide) for i in range(3)]
    weights = w_ref[...]
    shorts = []
    for i in range(3):
        total = weights[i, 0:1] * sources[i]
        for off in range(1, taps):
            total = total + jnp.where(mask(off), weights[i, off : off + 1] * down(sources[i], off), 0.0)
        shorts.append(total.astype(narrow).astype(wide))
    q_short, k_short, v_short = shorts
    upstream = up_ref[...].astype(wide)
    skip = skip_ref[...]
    mixed = (k_short * v_short).astype(narrow).astype(wide)
    grad_conv = (upstream * q_short).astype(narrow).astype(wide)
    conv = conv_ref[...].astype(wide) + skip * mixed
    grad_mixed = back_ref[...].astype(wide) + skip * grad_conv
    own = mask(2 * taps)
    out_ref[0] = lift(q_short * conv, head)[:rows].astype(narrow)
    grads = [upstream * conv, grad_mixed * v_short, grad_mixed * k_short]
    stats = []
    for i in range(3):
        grad = grads[i]
        acc = weights[i, 0:1] * grad
        stats.append(jnp.sum(jnp.where(own, sources[i] * grad, 0.0), axis=0, keepdims=True))
        for off in range(1, taps):
            later = lift(jnp.where(mask(taps + off), grad, 0.0), off)
            acc = acc + weights[i, off : off + 1] * later
            lagged = jnp.where(own & mask(off), down(sources[i], off) * grad, 0.0)
            stats.append(jnp.sum(lagged, axis=0, keepdims=True))
        out_ref[1 + i] = lift(acc, head)[:rows].astype(narrow)
    stats.append(jnp.sum(jnp.where(own, grad_conv * mixed, 0.0), axis=0, keepdims=True))
    width = stats[0].shape[1]
    stats.append(jnp.zeros((stats_ref.shape[0] - len(stats), width), wide))
    stats_ref[...] = jnp.concatenate(stats, 0)


def epilogue(back, sources, upstream, masks, short_weights, skip, rows):
    _, frame, chans = back.shape
    taps = short_weights.shape[1]
    block = 256 if chans % 256 == 0 else chans
    grid = (chans // block,)
    stat_rows = 16
    return pl.pallas_call(
        epilogue_kernel,
        grid=grid,
        in_specs=[
            pl.BlockSpec((None, frame, block), lambda c: (0, 0, c)),
            pl.BlockSpec((None, frame, block), lambda c: (1, 0, c)),
            pl.BlockSpec((3, frame, block), lambda c: (0, 0, c)),
            pl.BlockSpec((frame, block), lambda c: (0, c)),
            pl.BlockSpec(masks.shape, lambda c: (0, 0, 0)),
            pl.BlockSpec((3, taps, block), lambda c: (0, 0, c)),
            pl.BlockSpec((1, block), lambda c: (0, c)),
        ],
        out_specs=[
            pl.BlockSpec((4, rows, block), lambda c: (0, 0, c)),
            pl.BlockSpec((stat_rows, block), lambda c: (0, c)),
        ],
        out_shape=[
            jax.ShapeDtypeStruct((4, rows, chans), jnp.bfloat16),
            jax.ShapeDtypeStruct((stat_rows, chans), jnp.float32),
        ],
    )(back, back, sources, upstream, masks, short_weights, skip[None])


def local(query, keys, values, cotangent, long_filter, short_weights, skip, lengths):
    parts = lax.axis_size("ctx")
    index = lax.axis_index("ctx")
    groups = lax.axis_size("dp")
    q_rows, k_rows, v_rows, c_rows = query[0], keys[0], values[0], cotangent[0]
    rows, chans = q_rows.shape
    taps = short_weights.shape[1]
    head = taps - 1
    seq_len = rows * parts
    lanes = chans // parts
    ext = rows + head
    frame = -(-(rows + 2 * head) // 8) * 8
    doc_len = lengths[0]
    starts = jnp.cumsum(doc_len) - doc_len

    position = index * rows + jnp.arange(ext, dtype=jnp.int32)
    begin = jnp.max(jnp.where(starts[None, :] <= position[:, None], starts[None, :], 0), axis=1)
    valid = position[None, :] - jnp.arange(taps, dtype=jnp.int32)[:, None] >= begin[None, :]
    valid_after = valid & (position < seq_len)[None, :]

    prev = shifted(jnp.stack([a[rows - head :] for a in (q_rows, k_rows, v_rows)]), "ctx", 1)
    nxt = shifted(jnp.stack([a[:head] for a in (q_rows, k_rows, v_rows, c_rows)]), "ctx", -1)
    padded = [
        jnp.concatenate([prev[i], src, nxt[i]], 0).astype(jnp.float32)
        for i, src in enumerate((q_rows, k_rows, v_rows))
    ]

    def short_forward(wide, weights):
        summed = weights[0] * wide[head : head + ext]
        for offset in range(1, taps):
            begin_at = head - offset
            summed = summed + jnp.where(
                valid[offset][:, None], weights[offset] * wide[begin_at : begin_at + ext], 0.0
            )
        return summed.astype(jnp.bfloat16).astype(jnp.float32)

    q_short = short_forward(padded[0], short_weights[0])
    k_short = short_forward(padded[1], short_weights[1])
    v_short = short_forward(padded[2], short_weights[2])
    upstream = jnp.concatenate([c_rows, nxt[3]], 0).astype(jnp.float32)
    mixed = (k_short * v_short).astype(jnp.bfloat16)
    grad_conv = (upstream * q_short).astype(jnp.bfloat16)
    mixed_wide = mixed.astype(jnp.float32)
    grad_wide = grad_conv.astype(jnp.float32)

    chunks = 2 if lanes % 2 == 0 else 1
    width = lanes // chunks

    def to_columns(data):
        count = data.shape[0]
        split = data.reshape(count, rows, parts, lanes).transpose(0, 2, 1, 3)
        moved = lax.all_to_all(split, "ctx", 1, 1, tiled=True)
        return moved.reshape(count, seq_len, chunks, width)

    all_columns = to_columns(jnp.stack([long_filter, mixed[:rows], grad_conv[:rows]]))
    returned = []
    for part in range(chunks):
        columns = all_columns[:, :, part]
        spectra = fft_forward(columns)
        raw = fft_inverse(spectral_products(spectra), seq_len).astype(jnp.bfloat16)
        raw = jnp.concatenate(
            [jnp.zeros((3, head, width), raw.dtype), raw, jnp.zeros((3, frame - rows - head, width), raw.dtype)], 1
        )
        blocks = jnp.stack([raw[:, j * rows : j * rows + frame] for j in range(parts)], 1)
        returned.append(lax.all_to_all(blocks, "ctx", 1, 1, tiled=True))
    back = jnp.stack(returned, 3).transpose(0, 2, 1, 3, 4).reshape(3, frame, chans)

    spot = index * rows - head + jnp.arange(frame, dtype=jnp.int32)
    spot_begin = jnp.max(jnp.where(starts[None, :] <= spot[:, None], starts[None, :], 0), axis=1)
    spot_valid = spot[None, :] - jnp.arange(taps, dtype=jnp.int32)[:, None] >= spot_begin[None, :]
    spot_after = spot_valid & ((spot >= 0) & (spot < seq_len))[None, :]
    spot_own = ((spot >= index * rows) & (spot < index * rows + rows))[None, :]
    masks = jnp.concatenate([spot_valid, spot_after, spot_own], 0).astype(jnp.float32)
    masks = jnp.concatenate([masks, jnp.zeros(((-masks.shape[0]) % 8, frame), jnp.float32)], 0)
    tail = frame - rows - 2 * head
    sources = jnp.stack([
        jnp.concatenate([prev[i], src, nxt[i], jnp.zeros((tail, chans), src.dtype)], 0)
        for i, src in enumerate((q_rows, k_rows, v_rows))
    ])
    framed_up = jnp.concatenate(
        [jnp.zeros((head, chans), c_rows.dtype), c_rows, nxt[3], jnp.zeros((tail, chans), c_rows.dtype)], 0
    )
    outs, stats = epilogue(back, sources, framed_up, masks[:, :, None], short_weights, skip, rows)
    summed = mesh_sum(stats[: 3 * taps + 1], ("dp", "ctx"))
    gated, grad_q, grad_k, grad_v = outs[0], outs[1], outs[2], outs[3]
    filter_part = halving_scatter(back[2, head : head + rows].astype(jnp.float32), "dp")
    scale = 1.0 / (groups * seq_len)
    return (
        gated[None],
        grad_q.astype(jnp.bfloat16)[None],
        grad_k.astype(jnp.bfloat16)[None],
        grad_v.astype(jnp.bfloat16)[None],
        filter_part * scale,
        summed[: 3 * taps].reshape(3, taps, chans) * scale,
        summed[3 * taps] * scale,
    )


def solution(mesh):
    in_specs = (
        P("dp", "ctx", None),
        P("dp", "ctx", None),
        P("dp", "ctx", None),
        P("dp", "ctx", None),
        P("ctx", None),
        P(),
        P(),
        P("dp", None),
    )
    out_specs = (
        P("dp", "ctx", None),
        P("dp", "ctx", None),
        P("dp", "ctx", None),
        P("dp", "ctx", None),
        P("ctx", "dp"),
        P(),
        P(),
    )
    return jax.shard_map(local, mesh=mesh, in_specs=in_specs, out_specs=out_specs, check_vma=False)
```

```python
import math

import jax
import jax.numpy as jnp
import ml_dtypes
import numpy as np
from jax import lax
from jax.experimental import pallas as pl
from jax.experimental.pallas import tpu as pltpu
from jax.sharding import PartitionSpec as P


def shifted(x, axis, by):
    length = lax.axis_size(axis)
    pairs = [(i, i + by) for i in range(length) if 0 <= i + by < length]
    return lax.ppermute(x, axis, pairs)


def table_halves(table):
    upper = table.astype(ml_dtypes.bfloat16)
    lower = (table - upper.astype(np.float64)).astype(ml_dtypes.bfloat16)
    return jnp.asarray(upper), jnp.asarray(lower)


def split_product(form, table, data, exact=True):
    upper, lower = table_halves(table)
    wide = jnp.float32
    if not exact:
        return jnp.einsum(form, upper, data.astype(jnp.bfloat16), preferred_element_type=wide)
    if data.dtype == jnp.bfloat16:
        total = jnp.einsum(form, upper, data, preferred_element_type=wide)
        return total + jnp.einsum(form, lower, data, preferred_element_type=wide)
    data_upper = lax.optimization_barrier(data.astype(jnp.bfloat16))
    data_lower = (data - data_upper.astype(wide)).astype(jnp.bfloat16)
    total = jnp.einsum(form, upper, data_upper, preferred_element_type=wide)
    total = total + jnp.einsum(form, lower, data_upper, preferred_element_type=wide)
    return total + jnp.einsum(form, upper, data_lower, preferred_element_type=wide)


def batched_product(table, data):
    count, outer, twice, lanes = data.shape
    upper = jnp.asarray(table.astype(ml_dtypes.bfloat16))
    upper = jnp.broadcast_to(upper, (count, outer, twice, twice))
    return jnp.einsum(
        "skab,skbc->skac", upper, data.astype(jnp.bfloat16), preferred_element_type=jnp.float32
    )


def factors(size):
    bits = size.bit_length() - 1
    inner = 1 << (bits // 2)
    return size // inner, inner


def twiddles(outer, inner, size):
    phase = 2.0 * np.pi * np.outer(np.arange(outer), np.arange(inner)) / size
    cosine = jnp.asarray(np.cos(phase), jnp.float32)[None, :, :, None]
    sine = jnp.asarray(np.sin(phase), jnp.float32)[None, :, :, None]
    return cosine, sine


def inner_table(inner, sign):
    phase = 2.0 * np.pi * np.outer(np.arange(inner), np.arange(inner)) / inner
    cosine, sine = np.cos(phase), sign * np.sin(phase)
    return np.block([[cosine, sine], [-sine, cosine]])


def fft_forward(signal):
    count, length, lanes = signal.shape
    size = 2 * length
    outer, inner = factors(size)
    half = outer // 2
    phase = 2.0 * np.pi * np.outer(np.arange(outer), np.arange(half)) / outer
    first = np.concatenate([np.cos(phase), -np.sin(phase)], 0)
    blocks = signal.reshape(count, half, inner, lanes).transpose(1, 0, 2, 3)
    stage = split_product("kn,nsqb->ksqb", first, blocks)
    real_part, imag_part = stage[:outer], stage[outer:]
    cosine, sine = twiddles(outer, inner, size)
    cosine, sine = cosine.transpose(1, 0, 2, 3), sine.transpose(1, 0, 2, 3)
    turned = jnp.stack(
        [real_part * cosine + imag_part * sine, imag_part * cosine - real_part * sine]
    ).astype(jnp.bfloat16)
    turned = turned.transpose(0, 3, 2, 1, 4).reshape(2 * inner, count, outer, lanes)
    return split_product("ab,bskc->askc", inner_table(inner, 1.0), turned, exact=False)


def fft_inverse(spectrum, length):
    twice, count, outer, lanes = spectrum.shape
    inner = twice // 2
    size = outer * inner
    half = outer // 2
    stage = split_product("ab,bskc->askc", inner_table(inner, -1.0), spectrum, exact=False)
    real_part, imag_part = stage[:inner], stage[inner:]
    cosine, sine = twiddles(outer, inner, size)
    cosine, sine = cosine.transpose(2, 0, 1, 3), sine.transpose(2, 0, 1, 3)
    turned = jnp.stack(
        [real_part * cosine - imag_part * sine, imag_part * cosine + real_part * sine]
    ).astype(jnp.bfloat16)
    turned = turned.transpose(0, 3, 2, 1, 4).reshape(2 * outer, count, inner, lanes)
    phase = 2.0 * np.pi * np.outer(np.arange(half), np.arange(outer)) / outer
    last = np.concatenate([np.cos(phase), -np.sin(phase)], 1) / size
    result = split_product("nk,ksqb->nsqb", last, turned, exact=False)
    return result.transpose(1, 0, 2, 3).reshape(count, length, lanes)


def spectral_products(spectra):
    inner = spectra.shape[0] // 2
    parts = [(spectra[:inner, i], spectra[inner:, i]) for i in range(3)]
    (f_re, f_im), (m_re, m_im), (g_re, g_im) = parts
    conv = jnp.concatenate([m_re * f_re - m_im * f_im, m_re * f_im + m_im * f_re], 0)
    back = jnp.concatenate([g_re * f_re + g_im * f_im, g_im * f_re - g_re * f_im], 0)
    cross = jnp.concatenate([g_re * m_re + g_im * m_im, g_im * m_re - g_re * m_im], 0)
    return jnp.stack([conv, back, cross], 1)


def all_sum(data, axis):
    size = lax.axis_size(axis)
    total = data
    for step in range(1, size):
        total = total + lax.ppermute(data, axis, [(i, (i + step) % size) for i in range(size)])
    return total


def mesh_sum(data, axes):
    count = 1
    for axis in axes:
        count *= lax.axis_size(axis)
    rows, chans = data.shape
    pieces = data.reshape(rows, count, chans // count).transpose(1, 0, 2)
    mine = jnp.sum(lax.all_to_all(pieces, axes, 0, 0, tiled=True), axis=0)
    spread = jnp.broadcast_to(mine[None], (count,) + mine.shape)
    gathered = lax.all_to_all(spread, axes, 0, 0, tiled=True)
    return gathered.transpose(1, 0, 2).reshape(rows, chans)


def halving_scatter(data, axis):
    size = lax.axis_size(axis)
    index = lax.axis_index(axis)
    rows, chans = data.shape
    blocks = data.reshape(rows, size, chans // size)
    step = size // 2
    while step >= 1:
        half = blocks.shape[1] // 2
        upper = (index // step) % 2 == 1
        keep = jnp.where(upper, blocks[:, half:], blocks[:, :half])
        give = jnp.where(upper, blocks[:, :half], blocks[:, half:])
        blocks = keep + lax.ppermute(give, axis, [(i, i ^ step) for i in range(size)])
        step //= 2
    return blocks.reshape(rows, chans // size)


def epilogue_kernel(conv_ref, back_ref, src_ref, up_ref, mask_ref, w_ref, skip_ref, out_ref, stats_ref):
    wide, narrow = jnp.float32, jnp.bfloat16
    taps = w_ref.shape[1]
    head = taps - 1
    frame = src_ref.shape[1]
    rows = out_ref.shape[1]

    def mask(i):
        return mask_ref[i] > 0.5

    def down(x, by):
        return pltpu.roll(x, by, 0) if by else x

    def lift(x, by):
        return pltpu.roll(x, frame - by, 0) if by else x

    sources = [src_ref[i].astype(wide) for i in range(3)]
    weights = w_ref[...]
    shorts = []
    for i in range(3):
        total = weights[i, 0:1] * sources[i]
        for off in range(1, taps):
            total = total + jnp.where(mask(off), weights[i, off : off + 1] * down(sources[i], off), 0.0)
        shorts.append(total.astype(narrow).astype(wide))
    q_short, k_short, v_short = shorts
    upstream = up_ref[...].astype(wide)
    skip = skip_ref[...]
    mixed = (k_short * v_short).astype(narrow).astype(wide)
    grad_conv = (upstream * q_short).astype(narrow).astype(wide)
    conv = conv_ref[...].astype(wide) + skip * mixed
    grad_mixed = back_ref[...].astype(wide) + skip * grad_conv
    own = mask(2 * taps)
    out_ref[0] = lift(q_short * conv, head)[:rows].astype(narrow)
    grads = [upstream * conv, grad_mixed * v_short, grad_mixed * k_short]
    stats = []
    for i in range(3):
        grad = grads[i]
        acc = weights[i, 0:1] * grad
        stats.append(jnp.sum(jnp.where(own, sources[i] * grad, 0.0), axis=0, keepdims=True))
        for off in range(1, taps):
            later = lift(jnp.where(mask(taps + off), grad, 0.0), off)
            acc = acc + weights[i, off : off + 1] * later
            lagged = jnp.where(own & mask(off), down(sources[i], off) * grad, 0.0)
            stats.append(jnp.sum(lagged, axis=0, keepdims=True))
        out_ref[1 + i] = lift(acc, head)[:rows].astype(narrow)
    stats.append(jnp.sum(jnp.where(own, grad_conv * mixed, 0.0), axis=0, keepdims=True))
    width = stats[0].shape[1]
    stats.append(jnp.zeros((stats_ref.shape[0] - len(stats), width), wide))
    stats_ref[...] = jnp.concatenate(stats, 0)


def epilogue(back, sources, upstream, masks, short_weights, skip, rows):
    _, frame, chans = back.shape
    taps = short_weights.shape[1]
    block = 256 if chans % 256 == 0 else chans
    grid = (chans // block,)
    stat_rows = 16
    return pl.pallas_call(
        epilogue_kernel,
        grid=grid,
        in_specs=[
            pl.BlockSpec((None, frame, block), lambda c: (0, 0, c)),
            pl.BlockSpec((None, frame, block), lambda c: (1, 0, c)),
            pl.BlockSpec((3, frame, block), lambda c: (0, 0, c)),
            pl.BlockSpec((frame, block), lambda c: (0, c)),
            pl.BlockSpec(masks.shape, lambda c: (0, 0, 0)),
            pl.BlockSpec((3, taps, block), lambda c: (0, 0, c)),
            pl.BlockSpec((1, block), lambda c: (0, c)),
        ],
        out_specs=[
            pl.BlockSpec((4, rows, block), lambda c: (0, 0, c)),
            pl.BlockSpec((stat_rows, block), lambda c: (0, c)),
        ],
        out_shape=[
            jax.ShapeDtypeStruct((4, rows, chans), jnp.bfloat16),
            jax.ShapeDtypeStruct((stat_rows, chans), jnp.float32),
        ],
    )(back, back, sources, upstream, masks, short_weights, skip[None])


def local(query, keys, values, cotangent, long_filter, short_weights, skip, lengths):
    parts = lax.axis_size("ctx")
    index = lax.axis_index("ctx")
    groups = lax.axis_size("dp")
    q_rows, k_rows, v_rows, c_rows = query[0], keys[0], values[0], cotangent[0]
    rows, chans = q_rows.shape
    taps = short_weights.shape[1]
    head = taps - 1
    seq_len = rows * parts
    lanes = chans // parts
    ext = rows + head
    frame = -(-(rows + 2 * head) // 8) * 8
    doc_len = lengths[0]
    starts = jnp.cumsum(doc_len) - doc_len

    position = index * rows + jnp.arange(ext, dtype=jnp.int32)
    begin = jnp.max(jnp.where(starts[None, :] <= position[:, None], starts[None, :], 0), axis=1)
    valid = position[None, :] - jnp.arange(taps, dtype=jnp.int32)[:, None] >= begin[None, :]
    valid_after = valid & (position < seq_len)[None, :]

    prev = shifted(jnp.stack([a[rows - head :] for a in (q_rows, k_rows, v_rows)]), "ctx", 1)
    nxt = shifted(jnp.stack([a[:head] for a in (q_rows, k_rows, v_rows, c_rows)]), "ctx", -1)
    padded = [
        jnp.concatenate([prev[i], src, nxt[i]], 0).astype(jnp.float32)
        for i, src in enumerate((q_rows, k_rows, v_rows))
    ]

    def short_forward(wide, weights):
        summed = weights[0] * wide[head : head + ext]
        for offset in range(1, taps):
            begin_at = head - offset
            summed = summed + jnp.where(
                valid[offset][:, None], weights[offset] * wide[begin_at : begin_at + ext], 0.0
            )
        return summed.astype(jnp.bfloat16).astype(jnp.float32)

    q_short = short_forward(padded[0], short_weights[0])
    k_short = short_forward(padded[1], short_weights[1])
    v_short = short_forward(padded[2], short_weights[2])
    upstream = jnp.concatenate([c_rows, nxt[3]], 0).astype(jnp.float32)
    mixed = (k_short * v_short).astype(jnp.bfloat16)
    grad_conv = (upstream * q_short).astype(jnp.bfloat16)
    mixed_wide = mixed.astype(jnp.float32)
    grad_wide = grad_conv.astype(jnp.float32)

    chunks = 2 if lanes % 2 == 0 else 1
    width = lanes // chunks

    def to_columns(data):
        count = data.shape[0]
        split = data.reshape(count, rows, parts, lanes).transpose(0, 2, 1, 3)
        moved = lax.all_to_all(split, "ctx", 1, 1, tiled=True)
        return moved.reshape(count, seq_len, chunks, width)

    all_columns = to_columns(jnp.stack([long_filter, mixed[:rows], grad_conv[:rows]]))
    returned = []
    for part in range(chunks):
        columns = all_columns[:, :, part]
        spectra = fft_forward(columns)
        raw = fft_inverse(spectral_products(spectra), seq_len).astype(jnp.bfloat16)
        raw = jnp.concatenate(
            [jnp.zeros((3, head, width), raw.dtype), raw, jnp.zeros((3, frame - rows - head, width), raw.dtype)], 1
        )
        blocks = jnp.stack([raw[:, j * rows : j * rows + frame] for j in range(parts)], 1)
        returned.append(lax.all_to_all(blocks, "ctx", 1, 1, tiled=True))
    back = jnp.stack(returned, 3).transpose(0, 2, 1, 3, 4).reshape(3, frame, chans)

    spot = index * rows - head + jnp.arange(frame, dtype=jnp.int32)
    spot_begin = jnp.max(jnp.where(starts[None, :] <= spot[:, None], starts[None, :], 0), axis=1)
    spot_valid = spot[None, :] - jnp.arange(taps, dtype=jnp.int32)[:, None] >= spot_begin[None, :]
    spot_after = spot_valid & ((spot >= 0) & (spot < seq_len))[None, :]
    spot_own = ((spot >= index * rows) & (spot < index * rows + rows))[None, :]
    masks = jnp.concatenate([spot_valid, spot_after, spot_own], 0).astype(jnp.float32)
    masks = jnp.concatenate([masks, jnp.zeros(((-masks.shape[0]) % 8, frame), jnp.float32)], 0)
    tail = frame - rows - 2 * head
    sources = jnp.stack([
        jnp.concatenate([prev[i], src, nxt[i], jnp.zeros((tail, chans), src.dtype)], 0)
        for i, src in enumerate((q_rows, k_rows, v_rows))
    ])
    framed_up = jnp.concatenate(
        [jnp.zeros((head, chans), c_rows.dtype), c_rows, nxt[3], jnp.zeros((tail, chans), c_rows.dtype)], 0
    )
    outs, stats = epilogue(back, sources, framed_up, masks[:, :, None], short_weights, skip, rows)
    summed = mesh_sum(stats[: 3 * taps + 1], ("dp", "ctx"))
    gated, grad_q, grad_k, grad_v = outs[0], outs[1], outs[2], outs[3]
    filter_part = halving_scatter(back[2, head : head + rows].astype(jnp.float32), "dp")
    scale = 1.0 / (groups * seq_len)
    return (
        gated[None],
        grad_q.astype(jnp.bfloat16)[None],
        grad_k.astype(jnp.bfloat16)[None],
        grad_v.astype(jnp.bfloat16)[None],
        filter_part * scale,
        summed[: 3 * taps].reshape(3, taps, chans) * scale,
        summed[3 * taps] * scale,
    )


def solution(mesh):
    in_specs = (
        P("dp", "ctx", None),
        P("dp", "ctx", None),
        P("dp", "ctx", None),
        P("dp", "ctx", None),
        P("ctx", None),
        P(),
        P(),
        P("dp", None),
    )
    out_specs = (
        P("dp", "ctx", None),
        P("dp", "ctx", None),
        P("dp", "ctx", None),
        P("dp", "ctx", None),
        P("ctx", "dp"),
        P(),
        P(),
    )
    return jax.shard_map(local, mesh=mesh, in_specs=in_specs, out_specs=out_specs, check_vma=False)
```

```python
import math

import jax
import jax.numpy as jnp
import ml_dtypes
import numpy as np
from jax import lax
from jax.experimental import pallas as pl
from jax.experimental.pallas import tpu as pltpu
from jax.sharding import PartitionSpec as P


def shifted(x, axis, by):
    length = lax.axis_size(axis)
    pairs = [(i, i + by) for i in range(length) if 0 <= i + by < length]
    return lax.ppermute(x, axis, pairs)


def table_halves(table):
    upper = table.astype(ml_dtypes.bfloat16)
    lower = (table - upper.astype(np.float64)).astype(ml_dtypes.bfloat16)
    return jnp.asarray(upper), jnp.asarray(lower)


def split_product(form, table, data, exact=True):
    upper, lower = table_halves(table)
    wide = jnp.float32
    if not exact:
        return jnp.einsum(form, upper, data.astype(jnp.bfloat16), preferred_element_type=wide)
    if data.dtype == jnp.bfloat16:
        total = jnp.einsum(form, upper, data, preferred_element_type=wide)
        return total + jnp.einsum(form, lower, data, preferred_element_type=wide)
    data_upper = lax.optimization_barrier(data.astype(jnp.bfloat16))
    data_lower = (data - data_upper.astype(wide)).astype(jnp.bfloat16)
    total = jnp.einsum(form, upper, data_upper, preferred_element_type=wide)
    total = total + jnp.einsum(form, lower, data_upper, preferred_element_type=wide)
    return total + jnp.einsum(form, upper, data_lower, preferred_element_type=wide)


def batched_product(table, data):
    count, outer, twice, lanes = data.shape
    upper = jnp.asarray(table.astype(ml_dtypes.bfloat16))
    upper = jnp.broadcast_to(upper, (count, outer, twice, twice))
    return jnp.einsum(
        "skab,skbc->skac", upper, data.astype(jnp.bfloat16), preferred_element_type=jnp.float32
    )


def factors(size):
    bits = size.bit_length() - 1
    inner = 1 << (bits // 2)
    return size // inner, inner


def twiddles(outer, inner, size):
    phase = 2.0 * np.pi * np.outer(np.arange(outer), np.arange(inner)) / size
    cosine = jnp.asarray(np.cos(phase), jnp.float32)[None, :, :, None]
    sine = jnp.asarray(np.sin(phase), jnp.float32)[None, :, :, None]
    return cosine, sine


def inner_table(inner, sign):
    phase = 2.0 * np.pi * np.outer(np.arange(inner), np.arange(inner)) / inner
    cosine, sine = np.cos(phase), sign * np.sin(phase)
    return np.block([[cosine, sine], [-sine, cosine]])


def fft_forward(signal):
    count, length, lanes = signal.shape
    size = 2 * length
    outer, inner = factors(size)
    half = outer // 2
    phase = 2.0 * np.pi * np.outer(np.arange(outer), np.arange(half)) / outer
    first = np.concatenate([np.cos(phase), -np.sin(phase)], 0)
    blocks = signal.reshape(count, half, inner, lanes).transpose(1, 0, 2, 3)
    stage = split_product("kn,nsqb->ksqb", first, blocks)
    real_part, imag_part = stage[:outer], stage[outer:]
    cosine, sine = twiddles(outer, inner, size)
    cosine, sine = cosine.transpose(1, 0, 2, 3), sine.transpose(1, 0, 2, 3)
    turned = jnp.stack(
        [real_part * cosine + imag_part * sine, imag_part * cosine - real_part * sine]
    ).astype(jnp.bfloat16)
    turned = turned.transpose(0, 3, 2, 1, 4).reshape(2 * inner, count, outer, lanes)
    return split_product("ab,bskc->askc", inner_table(inner, 1.0), turned, exact=False)


def fft_inverse(spectrum, length):
    twice, count, outer, lanes = spectrum.shape
    inner = twice // 2
    size = outer * inner
    half = outer // 2
    stage = split_product("ab,bskc->askc", inner_table(inner, -1.0), spectrum, exact=False)
    real_part, imag_part = stage[:inner], stage[inner:]
    cosine, sine = twiddles(outer, inner, size)
    cosine, sine = cosine.transpose(2, 0, 1, 3), sine.transpose(2, 0, 1, 3)
    turned = jnp.stack(
        [real_part * cosine - imag_part * sine, imag_part * cosine + real_part * sine]
    ).astype(jnp.bfloat16)
    turned = turned.transpose(0, 3, 2, 1, 4).reshape(2 * outer, count, inner, lanes)
    phase = 2.0 * np.pi * np.outer(np.arange(half), np.arange(outer)) / outer
    last = np.concatenate([np.cos(phase), -np.sin(phase)], 1) / size
    result = split_product("nk,ksqb->nsqb", last, turned, exact=False)
    return result.transpose(1, 0, 2, 3).reshape(count, length, lanes)


def spectral_products(spectra):
    inner = spectra.shape[0] // 2
    parts = [(spectra[:inner, i], spectra[inner:, i]) for i in range(3)]
    (f_re, f_im), (m_re, m_im), (g_re, g_im) = parts
    conv = jnp.concatenate([m_re * f_re - m_im * f_im, m_re * f_im + m_im * f_re], 0)
    back = jnp.concatenate([g_re * f_re + g_im * f_im, g_im * f_re - g_re * f_im], 0)
    cross = jnp.concatenate([g_re * m_re + g_im * m_im, g_im * m_re - g_re * m_im], 0)
    return jnp.stack([conv, back, cross], 1)


def all_sum(data, axis):
    size = lax.axis_size(axis)
    total = data
    for step in range(1, size):
        total = total + lax.ppermute(data, axis, [(i, (i + step) % size) for i in range(size)])
    return total


def mesh_sum(data, axes):
    count = 1
    for axis in axes:
        count *= lax.axis_size(axis)
    rows, chans = data.shape
    pieces = data.reshape(rows, count, chans // count).transpose(1, 0, 2)
    mine = jnp.sum(lax.all_to_all(pieces, axes, 0, 0, tiled=True), axis=0)
    spread = jnp.broadcast_to(mine[None], (count,) + mine.shape)
    gathered = lax.all_to_all(spread, axes, 0, 0, tiled=True)
    return gathered.transpose(1, 0, 2).reshape(rows, chans)


def halving_scatter(data, axis):
    size = lax.axis_size(axis)
    index = lax.axis_index(axis)
    rows, chans = data.shape
    blocks = data.reshape(rows, size, chans // size)
    step = size // 2
    while step >= 1:
        half = blocks.shape[1] // 2
        upper = (index // step) % 2 == 1
        keep = jnp.where(upper, blocks[:, half:], blocks[:, :half])
        give = jnp.where(upper, blocks[:, :half], blocks[:, half:])
        blocks = keep + lax.ppermute(give, axis, [(i, i ^ step) for i in range(size)])
        step //= 2
    return blocks.reshape(rows, chans // size)


def epilogue_kernel(conv_ref, back_ref, src_ref, up_ref, mask_ref, w_ref, skip_ref, out_ref, stats_ref):
    wide, narrow = jnp.float32, jnp.bfloat16
    taps = w_ref.shape[1]
    head = taps - 1
    frame = src_ref.shape[1]
    rows = out_ref.shape[1]

    def mask(i):
        return mask_ref[i] > 0.5

    def down(x, by):
        return pltpu.roll(x, by, 0) if by else x

    def lift(x, by):
        return pltpu.roll(x, frame - by, 0) if by else x

    sources = [src_ref[i].astype(wide) for i in range(3)]
    weights = w_ref[...]
    shorts = []
    for i in range(3):
        total = weights[i, 0:1] * sources[i]
        for off in range(1, taps):
            total = total + jnp.where(mask(off), weights[i, off : off + 1] * down(sources[i], off), 0.0)
        shorts.append(total.astype(narrow).astype(wide))
    q_short, k_short, v_short = shorts
    upstream = up_ref[...].astype(wide)
    skip = skip_ref[...]
    mixed = (k_short * v_short).astype(narrow).astype(wide)
    grad_conv = (upstream * q_short).astype(narrow).astype(wide)
    conv = conv_ref[...].astype(wide) + skip * mixed
    grad_mixed = back_ref[...].astype(wide) + skip * grad_conv
    own = mask(2 * taps)
    out_ref[0] = lift(q_short * conv, head)[:rows].astype(narrow)
    grads = [upstream * conv, grad_mixed * v_short, grad_mixed * k_short]
    stats = []
    for i in range(3):
        grad = grads[i]
        acc = weights[i, 0:1] * grad
        stats.append(jnp.sum(jnp.where(own, sources[i] * grad, 0.0), axis=0, keepdims=True))
        for off in range(1, taps):
            later = lift(jnp.where(mask(taps + off), grad, 0.0), off)
            acc = acc + weights[i, off : off + 1] * later
            lagged = jnp.where(own & mask(off), down(sources[i], off) * grad, 0.0)
            stats.append(jnp.sum(lagged, axis=0, keepdims=True))
        out_ref[1 + i] = lift(acc, head)[:rows].astype(narrow)
    stats.append(jnp.sum(jnp.where(own, grad_conv * mixed, 0.0), axis=0, keepdims=True))
    width = stats[0].shape[1]
    stats.append(jnp.zeros((stats_ref.shape[0] - len(stats), width), wide))
    stats_ref[...] = jnp.concatenate(stats, 0)


def epilogue(back, sources, upstream, masks, short_weights, skip, rows):
    _, frame, chans = back.shape
    taps = short_weights.shape[1]
    block = 256 if chans % 256 == 0 else chans
    grid = (chans // block,)
    stat_rows = 16
    return pl.pallas_call(
        epilogue_kernel,
        grid=grid,
        in_specs=[
            pl.BlockSpec((None, frame, block), lambda c: (0, 0, c)),
            pl.BlockSpec((None, frame, block), lambda c: (1, 0, c)),
            pl.BlockSpec((3, frame, block), lambda c: (0, 0, c)),
            pl.BlockSpec((frame, block), lambda c: (0, c)),
            pl.BlockSpec(masks.shape, lambda c: (0, 0, 0)),
            pl.BlockSpec((3, taps, block), lambda c: (0, 0, c)),
            pl.BlockSpec((1, block), lambda c: (0, c)),
        ],
        out_specs=[
            pl.BlockSpec((4, rows, block), lambda c: (0, 0, c)),
            pl.BlockSpec((stat_rows, block), lambda c: (0, c)),
        ],
        out_shape=[
            jax.ShapeDtypeStruct((4, rows, chans), jnp.bfloat16),
            jax.ShapeDtypeStruct((stat_rows, chans), jnp.float32),
        ],
    )(back, back, sources, upstream, masks, short_weights, skip[None])


def local(query, keys, values, cotangent, long_filter, short_weights, skip, lengths):
    parts = lax.axis_size("ctx")
    index = lax.axis_index("ctx")
    groups = lax.axis_size("dp")
    q_rows, k_rows, v_rows, c_rows = query[0], keys[0], values[0], cotangent[0]
    rows, chans = q_rows.shape
    taps = short_weights.shape[1]
    head = taps - 1
    seq_len = rows * parts
    lanes = chans // parts
    ext = rows + head
    frame = -(-(rows + 2 * head) // 8) * 8
    doc_len = lengths[0]
    starts = jnp.cumsum(doc_len) - doc_len

    position = index * rows + jnp.arange(ext, dtype=jnp.int32)
    begin = jnp.max(jnp.where(starts[None, :] <= position[:, None], starts[None, :], 0), axis=1)
    valid = position[None, :] - jnp.arange(taps, dtype=jnp.int32)[:, None] >= begin[None, :]
    valid_after = valid & (position < seq_len)[None, :]

    prev = shifted(jnp.stack([a[rows - head :] for a in (q_rows, k_rows, v_rows)]), "ctx", 1)
    nxt = shifted(jnp.stack([a[:head] for a in (q_rows, k_rows, v_rows, c_rows)]), "ctx", -1)
    padded = [
        jnp.concatenate([prev[i], src, nxt[i]], 0).astype(jnp.float32)
        for i, src in enumerate((q_rows, k_rows, v_rows))
    ]

    def short_forward(wide, weights):
        summed = weights[0] * wide[head : head + ext]
        for offset in range(1, taps):
            begin_at = head - offset
            summed = summed + jnp.where(
                valid[offset][:, None], weights[offset] * wide[begin_at : begin_at + ext], 0.0
            )
        return summed.astype(jnp.bfloat16).astype(jnp.float32)

    q_short = short_forward(padded[0], short_weights[0])
    k_short = short_forward(padded[1], short_weights[1])
    v_short = short_forward(padded[2], short_weights[2])
    upstream = jnp.concatenate([c_rows, nxt[3]], 0).astype(jnp.float32)
    mixed = (k_short * v_short).astype(jnp.bfloat16)
    grad_conv = (upstream * q_short).astype(jnp.bfloat16)
    mixed_wide = mixed.astype(jnp.float32)
    grad_wide = grad_conv.astype(jnp.float32)

    chunks = 2 if lanes % 2 == 0 else 1
    width = lanes // chunks

    def to_columns(data, part):
        count = data.shape[0]
        split = data.reshape(count, rows, parts, chunks, width)[:, :, :, part]
        moved = lax.all_to_all(split.transpose(0, 2, 1, 3), "ctx", 1, 1, tiled=True)
        return moved.reshape(count, seq_len, width)

    sent = jnp.stack([long_filter, mixed[:rows], grad_conv[:rows]])
    returned = []
    previous = None
    for part in range(chunks):
        columns = to_columns(sent, part)
        if previous is not None:
            columns, previous = lax.optimization_barrier((columns, previous))
            returned.append(lax.all_to_all(previous, "ctx", 1, 1, tiled=True))
        spectra = fft_forward(columns)
        raw = fft_inverse(spectral_products(spectra), seq_len).astype(jnp.bfloat16)
        raw = jnp.concatenate(
            [jnp.zeros((3, head, width), raw.dtype), raw, jnp.zeros((3, frame - rows - head, width), raw.dtype)], 1
        )
        blocks = jnp.stack([raw[:, j * rows : j * rows + frame] for j in range(parts)], 1)
        previous = blocks
    returned.append(lax.all_to_all(previous, "ctx", 1, 1, tiled=True))
    back = jnp.stack(returned, 3).transpose(0, 2, 1, 3, 4).reshape(3, frame, chans)

    spot = index * rows - head + jnp.arange(frame, dtype=jnp.int32)
    spot_begin = jnp.max(jnp.where(starts[None, :] <= spot[:, None], starts[None, :], 0), axis=1)
    spot_valid = spot[None, :] - jnp.arange(taps, dtype=jnp.int32)[:, None] >= spot_begin[None, :]
    spot_after = spot_valid & ((spot >= 0) & (spot < seq_len))[None, :]
    spot_own = ((spot >= index * rows) & (spot < index * rows + rows))[None, :]
    masks = jnp.concatenate([spot_valid, spot_after, spot_own], 0).astype(jnp.float32)
    masks = jnp.concatenate([masks, jnp.zeros(((-masks.shape[0]) % 8, frame), jnp.float32)], 0)
    tail = frame - rows - 2 * head
    sources = jnp.stack([
        jnp.concatenate([prev[i], src, nxt[i], jnp.zeros((tail, chans), src.dtype)], 0)
        for i, src in enumerate((q_rows, k_rows, v_rows))
    ])
    framed_up = jnp.concatenate(
        [jnp.zeros((head, chans), c_rows.dtype), c_rows, nxt[3], jnp.zeros((tail, chans), c_rows.dtype)], 0
    )
    outs, stats = epilogue(back, sources, framed_up, masks[:, :, None], short_weights, skip, rows)
    summed = mesh_sum(stats[: 3 * taps + 1], ("dp", "ctx"))
    gated, grad_q, grad_k, grad_v = outs[0], outs[1], outs[2], outs[3]
    filter_part = halving_scatter(back[2, head : head + rows].astype(jnp.float32), "dp")
    scale = 1.0 / (groups * seq_len)
    return (
        gated[None],
        grad_q.astype(jnp.bfloat16)[None],
        grad_k.astype(jnp.bfloat16)[None],
        grad_v.astype(jnp.bfloat16)[None],
        filter_part * scale,
        summed[: 3 * taps].reshape(3, taps, chans) * scale,
        summed[3 * taps] * scale,
    )


def solution(mesh):
    in_specs = (
        P("dp", "ctx", None),
        P("dp", "ctx", None),
        P("dp", "ctx", None),
        P("dp", "ctx", None),
        P("ctx", None),
        P(),
        P(),
        P("dp", None),
    )
    out_specs = (
        P("dp", "ctx", None),
        P("dp", "ctx", None),
        P("dp", "ctx", None),
        P("dp", "ctx", None),
        P("ctx", "dp"),
        P(),
        P(),
    )
    return jax.shard_map(local, mesh=mesh, in_specs=in_specs, out_specs=out_specs, check_vma=False)
```

```python
import math

import jax
import jax.numpy as jnp
import ml_dtypes
import numpy as np
from jax import lax
from jax.experimental import pallas as pl
from jax.experimental.pallas import tpu as pltpu
from jax.sharding import PartitionSpec as P


def shifted(x, axis, by):
    length = lax.axis_size(axis)
    pairs = [(i, i + by) for i in range(length) if 0 <= i + by < length]
    return lax.ppermute(x, axis, pairs)


def table_halves(table):
    upper = table.astype(ml_dtypes.bfloat16)
    lower = (table - upper.astype(np.float64)).astype(ml_dtypes.bfloat16)
    return jnp.asarray(upper), jnp.asarray(lower)


def split_product(form, table, data, exact=True):
    upper, lower = table_halves(table)
    wide = jnp.float32
    if not exact:
        return jnp.einsum(form, upper, data.astype(jnp.bfloat16), preferred_element_type=wide)
    if data.dtype == jnp.bfloat16:
        total = jnp.einsum(form, upper, data, preferred_element_type=wide)
        return total + jnp.einsum(form, lower, data, preferred_element_type=wide)
    data_upper = lax.optimization_barrier(data.astype(jnp.bfloat16))
    data_lower = (data - data_upper.astype(wide)).astype(jnp.bfloat16)
    total = jnp.einsum(form, upper, data_upper, preferred_element_type=wide)
    total = total + jnp.einsum(form, lower, data_upper, preferred_element_type=wide)
    return total + jnp.einsum(form, upper, data_lower, preferred_element_type=wide)


def batched_product(table, data):
    count, outer, twice, lanes = data.shape
    upper = jnp.asarray(table.astype(ml_dtypes.bfloat16))
    upper = jnp.broadcast_to(upper, (count, outer, twice, twice))
    return jnp.einsum(
        "skab,skbc->skac", upper, data.astype(jnp.bfloat16), preferred_element_type=jnp.float32
    )


def factors(size):
    bits = size.bit_length() - 1
    inner = 1 << (bits // 2)
    return size // inner, inner


def twiddles(outer, inner, size):
    phase = 2.0 * np.pi * np.outer(np.arange(outer), np.arange(inner)) / size
    cosine = jnp.asarray(np.cos(phase), jnp.float32)[None, :, :, None]
    sine = jnp.asarray(np.sin(phase), jnp.float32)[None, :, :, None]
    return cosine, sine


def inner_table(inner, sign):
    phase = 2.0 * np.pi * np.outer(np.arange(inner), np.arange(inner)) / inner
    cosine, sine = np.cos(phase), sign * np.sin(phase)
    return np.block([[cosine, sine], [-sine, cosine]])


def fft_forward(signal):
    count, length, lanes = signal.shape
    size = 2 * length
    outer, inner = factors(size)
    half = outer // 2
    phase = 2.0 * np.pi * np.outer(np.arange(outer), np.arange(half)) / outer
    first = np.concatenate([np.cos(phase), -np.sin(phase)], 0)
    blocks = signal.reshape(count, half, inner, lanes).transpose(1, 0, 2, 3)
    stage = split_product("kn,nsqb->ksqb", first, blocks)
    real_part, imag_part = stage[:outer], stage[outer:]
    cosine, sine = twiddles(outer, inner, size)
    cosine, sine = cosine.transpose(1, 0, 2, 3), sine.transpose(1, 0, 2, 3)
    turned = jnp.stack(
        [real_part * cosine + imag_part * sine, imag_part * cosine - real_part * sine]
    ).astype(jnp.bfloat16)
    turned = turned.transpose(0, 3, 2, 1, 4).reshape(2 * inner, count, outer, lanes)
    return split_product("ab,bskc->askc", inner_table(inner, 1.0), turned, exact=False)


def fft_inverse(spectrum, length):
    twice, count, outer, lanes = spectrum.shape
    inner = twice // 2
    size = outer * inner
    half = outer // 2
    stage = split_product("ab,bskc->askc", inner_table(inner, -1.0), spectrum, exact=False)
    real_part, imag_part = stage[:inner], stage[inner:]
    cosine, sine = twiddles(outer, inner, size)
    cosine, sine = cosine.transpose(2, 0, 1, 3), sine.transpose(2, 0, 1, 3)
    turned = jnp.stack(
        [real_part * cosine - imag_part * sine, imag_part * cosine + real_part * sine]
    ).astype(jnp.bfloat16)
    turned = turned.transpose(0, 3, 2, 1, 4).reshape(2 * outer, count, inner, lanes)
    phase = 2.0 * np.pi * np.outer(np.arange(half), np.arange(outer)) / outer
    last = np.concatenate([np.cos(phase), -np.sin(phase)], 1) / size
    result = split_product("nk,ksqb->nsqb", last, turned, exact=False)
    return result.transpose(1, 0, 2, 3).reshape(count, length, lanes)


def spectral_products(spectra):
    inner = spectra.shape[0] // 2
    parts = [(spectra[:inner, i], spectra[inner:, i]) for i in range(3)]
    (f_re, f_im), (m_re, m_im), (g_re, g_im) = parts
    conv = jnp.concatenate([m_re * f_re - m_im * f_im, m_re * f_im + m_im * f_re], 0)
    back = jnp.concatenate([g_re * f_re + g_im * f_im, g_im * f_re - g_re * f_im], 0)
    cross = jnp.concatenate([g_re * m_re + g_im * m_im, g_im * m_re - g_re * m_im], 0)
    return jnp.stack([conv, back, cross], 1)


def all_sum(data, axis):
    size = lax.axis_size(axis)
    total = data
    for step in range(1, size):
        total = total + lax.ppermute(data, axis, [(i, (i + step) % size) for i in range(size)])
    return total


def mesh_sum(data, axes):
    count = 1
    for axis in axes:
        count *= lax.axis_size(axis)
    rows, chans = data.shape
    pieces = data.reshape(rows, count, chans // count).transpose(1, 0, 2)
    mine = jnp.sum(lax.all_to_all(pieces, axes, 0, 0, tiled=True), axis=0)
    spread = jnp.broadcast_to(mine[None], (count,) + mine.shape)
    gathered = lax.all_to_all(spread, axes, 0, 0, tiled=True)
    return gathered.transpose(1, 0, 2).reshape(rows, chans)


def halving_scatter(data, axis):
    size = lax.axis_size(axis)
    index = lax.axis_index(axis)
    rows, chans = data.shape
    blocks = data.reshape(rows, size, chans // size)
    step = size // 2
    while step >= 1:
        half = blocks.shape[1] // 2
        upper = (index // step) % 2 == 1
        keep = jnp.where(upper, blocks[:, half:], blocks[:, :half])
        give = jnp.where(upper, blocks[:, :half], blocks[:, half:])
        blocks = keep + lax.ppermute(give, axis, [(i, i ^ step) for i in range(size)])
        step //= 2
    return blocks.reshape(rows, chans // size)


def epilogue_kernel(conv_ref, back_ref, src_ref, up_ref, mask_ref, w_ref, skip_ref, out_ref, stats_ref):
    wide, narrow = jnp.float32, jnp.bfloat16
    taps = w_ref.shape[1]
    head = taps - 1
    frame = src_ref.shape[1]
    rows = out_ref.shape[1]

    def mask(i):
        return mask_ref[i] > 0.5

    def down(x, by):
        return pltpu.roll(x, by, 0) if by else x

    def lift(x, by):
        return pltpu.roll(x, frame - by, 0) if by else x

    sources = [src_ref[i].astype(wide) for i in range(3)]
    weights = w_ref[...]
    shorts = []
    for i in range(3):
        total = weights[i, 0:1] * sources[i]
        for off in range(1, taps):
            total = total + jnp.where(mask(off), weights[i, off : off + 1] * down(sources[i], off), 0.0)
        shorts.append(total.astype(narrow).astype(wide))
    q_short, k_short, v_short = shorts
    upstream = up_ref[...].astype(wide)
    skip = skip_ref[...]
    mixed = (k_short * v_short).astype(narrow).astype(wide)
    grad_conv = (upstream * q_short).astype(narrow).astype(wide)
    conv = conv_ref[...].astype(wide) + skip * mixed
    grad_mixed = back_ref[...].astype(wide) + skip * grad_conv
    own = mask(2 * taps)
    out_ref[0] = lift(q_short * conv, head)[:rows].astype(narrow)
    grads = [upstream * conv, grad_mixed * v_short, grad_mixed * k_short]
    stats = []
    for i in range(3):
        grad = grads[i]
        acc = weights[i, 0:1] * grad
        stats.append(jnp.sum(jnp.where(own, sources[i] * grad, 0.0), axis=0, keepdims=True))
        for off in range(1, taps):
            later = lift(jnp.where(mask(taps + off), grad, 0.0), off)
            acc = acc + weights[i, off : off + 1] * later
            lagged = jnp.where(own & mask(off), down(sources[i], off) * grad, 0.0)
            stats.append(jnp.sum(lagged, axis=0, keepdims=True))
        out_ref[1 + i] = lift(acc, head)[:rows].astype(narrow)
    stats.append(jnp.sum(jnp.where(own, grad_conv * mixed, 0.0), axis=0, keepdims=True))
    width = stats[0].shape[1]
    stats.append(jnp.zeros((stats_ref.shape[0] - len(stats), width), wide))
    stats_ref[...] = jnp.concatenate(stats, 0)


def epilogue(back, sources, upstream, masks, short_weights, skip, rows):
    _, frame, chans = back.shape
    taps = short_weights.shape[1]
    block = 256 if chans % 256 == 0 else chans
    grid = (chans // block,)
    stat_rows = 16
    return pl.pallas_call(
        epilogue_kernel,
        grid=grid,
        in_specs=[
            pl.BlockSpec((None, frame, block), lambda c: (0, 0, c)),
            pl.BlockSpec((None, frame, block), lambda c: (1, 0, c)),
            pl.BlockSpec((3, frame, block), lambda c: (0, 0, c)),
            pl.BlockSpec((frame, block), lambda c: (0, c)),
            pl.BlockSpec(masks.shape, lambda c: (0, 0, 0)),
            pl.BlockSpec((3, taps, block), lambda c: (0, 0, c)),
            pl.BlockSpec((1, block), lambda c: (0, c)),
        ],
        out_specs=[
            pl.BlockSpec((4, rows, block), lambda c: (0, 0, c)),
            pl.BlockSpec((stat_rows, block), lambda c: (0, c)),
        ],
        out_shape=[
            jax.ShapeDtypeStruct((4, rows, chans), jnp.bfloat16),
            jax.ShapeDtypeStruct((stat_rows, chans), jnp.float32),
        ],
    )(back, back, sources, upstream, masks, short_weights, skip[None])


def local(query, keys, values, cotangent, long_filter, short_weights, skip, lengths):
    parts = lax.axis_size("ctx")
    index = lax.axis_index("ctx")
    groups = lax.axis_size("dp")
    q_rows, k_rows, v_rows, c_rows = query[0], keys[0], values[0], cotangent[0]
    rows, chans = q_rows.shape
    taps = short_weights.shape[1]
    head = taps - 1
    seq_len = rows * parts
    lanes = chans // parts
    ext = rows + head
    frame = -(-(rows + 2 * head) // 8) * 8
    doc_len = lengths[0]
    starts = jnp.cumsum(doc_len) - doc_len

    position = index * rows + jnp.arange(ext, dtype=jnp.int32)
    begin = jnp.max(jnp.where(starts[None, :] <= position[:, None], starts[None, :], 0), axis=1)
    valid = position[None, :] - jnp.arange(taps, dtype=jnp.int32)[:, None] >= begin[None, :]
    valid_after = valid & (position < seq_len)[None, :]

    prev = shifted(jnp.stack([a[rows - head :] for a in (q_rows, k_rows, v_rows)]), "ctx", 1)
    nxt = shifted(jnp.stack([a[:head] for a in (q_rows, k_rows, v_rows, c_rows)]), "ctx", -1)
    padded = [
        jnp.concatenate([prev[i], src, nxt[i]], 0).astype(jnp.float32)
        for i, src in enumerate((q_rows, k_rows, v_rows))
    ]

    def short_forward(wide, weights):
        summed = weights[0] * wide[head : head + ext]
        for offset in range(1, taps):
            begin_at = head - offset
            summed = summed + jnp.where(
                valid[offset][:, None], weights[offset] * wide[begin_at : begin_at + ext], 0.0
            )
        return summed.astype(jnp.bfloat16).astype(jnp.float32)

    q_short = short_forward(padded[0], short_weights[0])
    k_short = short_forward(padded[1], short_weights[1])
    v_short = short_forward(padded[2], short_weights[2])
    upstream = jnp.concatenate([c_rows, nxt[3]], 0).astype(jnp.float32)
    mixed = (k_short * v_short).astype(jnp.bfloat16)
    grad_conv = (upstream * q_short).astype(jnp.bfloat16)
    mixed_wide = mixed.astype(jnp.float32)
    grad_wide = grad_conv.astype(jnp.float32)

    chunks = 2 if lanes % 2 == 0 else 1
    width = lanes // chunks

    def to_columns(data, part):
        count = data.shape[0]
        split = data.reshape(count, rows, parts, chunks, width)[:, :, :, part]
        moved = lax.all_to_all(split.transpose(0, 2, 1, 3), "ctx", 1, 1, tiled=True)
        return moved.reshape(count, seq_len, width)

    sent = jnp.stack([long_filter, mixed[:rows], grad_conv[:rows]])
    returned = []
    previous = None
    for part in range(chunks):
        columns = to_columns(sent, part)
        if previous is not None:
            columns, previous = lax.optimization_barrier((columns, previous))
            returned.append(lax.all_to_all(previous, "ctx", 1, 1, tiled=True))
        spectra = fft_forward(columns)
        if returned:
            spectra, returned[-1] = lax.optimization_barrier((spectra, returned[-1]))
        raw = fft_inverse(spectral_products(spectra), seq_len).astype(jnp.bfloat16)
        raw = jnp.concatenate(
            [jnp.zeros((3, head, width), raw.dtype), raw, jnp.zeros((3, frame - rows - head, width), raw.dtype)], 1
        )
        blocks = jnp.stack([raw[:, j * rows : j * rows + frame] for j in range(parts)], 1)
        previous = blocks
    returned.append(lax.all_to_all(previous, "ctx", 1, 1, tiled=True))
    back = jnp.stack(returned, 3).transpose(0, 2, 1, 3, 4).reshape(3, frame, chans)

    spot = index * rows - head + jnp.arange(frame, dtype=jnp.int32)
    spot_begin = jnp.max(jnp.where(starts[None, :] <= spot[:, None], starts[None, :], 0), axis=1)
    spot_valid = spot[None, :] - jnp.arange(taps, dtype=jnp.int32)[:, None] >= spot_begin[None, :]
    spot_after = spot_valid & ((spot >= 0) & (spot < seq_len))[None, :]
    spot_own = ((spot >= index * rows) & (spot < index * rows + rows))[None, :]
    masks = jnp.concatenate([spot_valid, spot_after, spot_own], 0).astype(jnp.float32)
    masks = jnp.concatenate([masks, jnp.zeros(((-masks.shape[0]) % 8, frame), jnp.float32)], 0)
    tail = frame - rows - 2 * head
    sources = jnp.stack([
        jnp.concatenate([prev[i], src, nxt[i], jnp.zeros((tail, chans), src.dtype)], 0)
        for i, src in enumerate((q_rows, k_rows, v_rows))
    ])
    framed_up = jnp.concatenate(
        [jnp.zeros((head, chans), c_rows.dtype), c_rows, nxt[3], jnp.zeros((tail, chans), c_rows.dtype)], 0
    )
    outs, stats = epilogue(back, sources, framed_up, masks[:, :, None], short_weights, skip, rows)
    summed = mesh_sum(stats[: 3 * taps + 1], ("dp", "ctx"))
    gated, grad_q, grad_k, grad_v = outs[0], outs[1], outs[2], outs[3]
    filter_part = halving_scatter(back[2, head : head + rows].astype(jnp.float32), "dp")
    scale = 1.0 / (groups * seq_len)
    return (
        gated[None],
        grad_q.astype(jnp.bfloat16)[None],
        grad_k.astype(jnp.bfloat16)[None],
        grad_v.astype(jnp.bfloat16)[None],
        filter_part * scale,
        summed[: 3 * taps].reshape(3, taps, chans) * scale,
        summed[3 * taps] * scale,
    )


def solution(mesh):
    in_specs = (
        P("dp", "ctx", None),
        P("dp", "ctx", None),
        P("dp", "ctx", None),
        P("dp", "ctx", None),
        P("ctx", None),
        P(),
        P(),
        P("dp", None),
    )
    out_specs = (
        P("dp", "ctx", None),
        P("dp", "ctx", None),
        P("dp", "ctx", None),
        P("dp", "ctx", None),
        P("ctx", "dp"),
        P(),
        P(),
    )
    return jax.shard_map(local, mesh=mesh, in_specs=in_specs, out_specs=out_specs, check_vma=False)
```

```python
import math

import jax
import jax.numpy as jnp
import ml_dtypes
import numpy as np
from jax import lax
from jax.experimental import pallas as pl
from jax.experimental.pallas import tpu as pltpu
from jax.sharding import PartitionSpec as P


def shifted(x, axis, by):
    length = lax.axis_size(axis)
    pairs = [(i, i + by) for i in range(length) if 0 <= i + by < length]
    return lax.ppermute(x, axis, pairs)


def table_halves(table):
    upper = table.astype(ml_dtypes.bfloat16)
    lower = (table - upper.astype(np.float64)).astype(ml_dtypes.bfloat16)
    return jnp.asarray(upper), jnp.asarray(lower)


def split_product(form, table, data, exact=True):
    upper, lower = table_halves(table)
    wide = jnp.float32
    if not exact:
        return jnp.einsum(form, upper, data.astype(jnp.bfloat16), preferred_element_type=wide)
    if data.dtype == jnp.bfloat16:
        total = jnp.einsum(form, upper, data, preferred_element_type=wide)
        return total + jnp.einsum(form, lower, data, preferred_element_type=wide)
    data_upper = lax.optimization_barrier(data.astype(jnp.bfloat16))
    data_lower = (data - data_upper.astype(wide)).astype(jnp.bfloat16)
    total = jnp.einsum(form, upper, data_upper, preferred_element_type=wide)
    total = total + jnp.einsum(form, lower, data_upper, preferred_element_type=wide)
    return total + jnp.einsum(form, upper, data_lower, preferred_element_type=wide)


def batched_product(table, data):
    count, outer, twice, lanes = data.shape
    upper = jnp.asarray(table.astype(ml_dtypes.bfloat16))
    upper = jnp.broadcast_to(upper, (count, outer, twice, twice))
    return jnp.einsum(
        "skab,skbc->skac", upper, data.astype(jnp.bfloat16), preferred_element_type=jnp.float32
    )


def factors(size):
    bits = size.bit_length() - 1
    inner = 1 << (bits // 2)
    return size // inner, inner


def twiddles(outer, inner, size):
    phase = 2.0 * np.pi * np.outer(np.arange(outer), np.arange(inner)) / size
    cosine = jnp.asarray(np.cos(phase), jnp.float32)[None, :, :, None]
    sine = jnp.asarray(np.sin(phase), jnp.float32)[None, :, :, None]
    return cosine, sine


def inner_table(inner, sign):
    phase = 2.0 * np.pi * np.outer(np.arange(inner), np.arange(inner)) / inner
    cosine, sine = np.cos(phase), sign * np.sin(phase)
    return np.block([[cosine, sine], [-sine, cosine]])


def fft_forward(signal):
    count, length, lanes = signal.shape
    size = 2 * length
    outer, inner = factors(size)
    half = outer // 2
    phase = 2.0 * np.pi * np.outer(np.arange(outer), np.arange(half)) / outer
    first = np.concatenate([np.cos(phase), -np.sin(phase)], 0)
    blocks = signal.reshape(count, half, inner, lanes).transpose(1, 0, 2, 3)
    stage = split_product("kn,nsqb->ksqb", first, blocks)
    real_part, imag_part = stage[:outer], stage[outer:]
    cosine, sine = twiddles(outer, inner, size)
    cosine, sine = cosine.transpose(1, 0, 2, 3), sine.transpose(1, 0, 2, 3)
    turned = jnp.stack(
        [real_part * cosine + imag_part * sine, imag_part * cosine - real_part * sine]
    ).astype(jnp.bfloat16)
    turned = turned.transpose(0, 3, 2, 1, 4).reshape(2 * inner, count, outer, lanes)
    return split_product("ab,bskc->askc", inner_table(inner, 1.0), turned, exact=False)


def fft_inverse(spectrum, length):
    twice, count, outer, lanes = spectrum.shape
    inner = twice // 2
    size = outer * inner
    half = outer // 2
    stage = split_product("ab,bskc->askc", inner_table(inner, -1.0), spectrum, exact=False)
    real_part, imag_part = stage[:inner], stage[inner:]
    cosine, sine = twiddles(outer, inner, size)
    cosine, sine = cosine.transpose(2, 0, 1, 3), sine.transpose(2, 0, 1, 3)
    turned = jnp.stack(
        [real_part * cosine - imag_part * sine, imag_part * cosine + real_part * sine]
    ).astype(jnp.bfloat16)
    turned = turned.transpose(0, 3, 2, 1, 4).reshape(2 * outer, count, inner, lanes)
    phase = 2.0 * np.pi * np.outer(np.arange(half), np.arange(outer)) / outer
    last = np.concatenate([np.cos(phase), -np.sin(phase)], 1) / size
    result = split_product("nk,ksqb->nsqb", last, turned, exact=False)
    return result.transpose(1, 0, 2, 3).reshape(count, length, lanes)


def spectral_products(spectra):
    inner = spectra.shape[0] // 2
    parts = [(spectra[:inner, i], spectra[inner:, i]) for i in range(3)]
    (f_re, f_im), (m_re, m_im), (g_re, g_im) = parts
    conv = jnp.concatenate([m_re * f_re - m_im * f_im, m_re * f_im + m_im * f_re], 0)
    back = jnp.concatenate([g_re * f_re + g_im * f_im, g_im * f_re - g_re * f_im], 0)
    cross = jnp.concatenate([g_re * m_re + g_im * m_im, g_im * m_re - g_re * m_im], 0)
    return jnp.stack([conv, back, cross], 1)


def all_sum(data, axis):
    size = lax.axis_size(axis)
    total = data
    for step in range(1, size):
        total = total + lax.ppermute(data, axis, [(i, (i + step) % size) for i in range(size)])
    return total


def mesh_sum(data, axes):
    count = 1
    for axis in axes:
        count *= lax.axis_size(axis)
    rows, chans = data.shape
    pieces = data.reshape(rows, count, chans // count).transpose(1, 0, 2)
    mine = jnp.sum(lax.all_to_all(pieces, axes, 0, 0, tiled=True), axis=0)
    spread = jnp.broadcast_to(mine[None], (count,) + mine.shape)
    gathered = lax.all_to_all(spread, axes, 0, 0, tiled=True)
    return gathered.transpose(1, 0, 2).reshape(rows, chans)


def halving_scatter(data, axis):
    size = lax.axis_size(axis)
    index = lax.axis_index(axis)
    rows, chans = data.shape
    blocks = data.reshape(rows, size, chans // size)
    step = size // 2
    while step >= 1:
        half = blocks.shape[1] // 2
        upper = (index // step) % 2 == 1
        keep = jnp.where(upper, blocks[:, half:], blocks[:, :half])
        give = jnp.where(upper, blocks[:, :half], blocks[:, half:])
        blocks = keep + lax.ppermute(give, axis, [(i, i ^ step) for i in range(size)])
        step //= 2
    return blocks.reshape(rows, chans // size)


def epilogue_kernel(conv_ref, back_ref, src_ref, up_ref, mask_ref, w_ref, skip_ref, out_ref, stats_ref):
    wide, narrow = jnp.float32, jnp.bfloat16
    taps = w_ref.shape[1]
    head = taps - 1
    frame = src_ref.shape[1]
    rows = out_ref.shape[1]

    def mask(i):
        return mask_ref[i] > 0.5

    def down(x, by):
        return pltpu.roll(x, by, 0) if by else x

    def lift(x, by):
        return pltpu.roll(x, frame - by, 0) if by else x

    sources = [src_ref[i].astype(wide) for i in range(3)]
    weights = w_ref[...]
    shorts = []
    for i in range(3):
        total = weights[i, 0:1] * sources[i]
        for off in range(1, taps):
            total = total + jnp.where(mask(off), weights[i, off : off + 1] * down(sources[i], off), 0.0)
        shorts.append(total.astype(narrow).astype(wide))
    q_short, k_short, v_short = shorts
    upstream = up_ref[...].astype(wide)
    skip = skip_ref[...]
    mixed = (k_short * v_short).astype(narrow).astype(wide)
    grad_conv = (upstream * q_short).astype(narrow).astype(wide)
    conv = conv_ref[...].astype(wide) + skip * mixed
    grad_mixed = back_ref[...].astype(wide) + skip * grad_conv
    own = mask(2 * taps)
    out_ref[0] = lift(q_short * conv, head)[:rows].astype(narrow)
    grads = [upstream * conv, grad_mixed * v_short, grad_mixed * k_short]
    stats = []
    for i in range(3):
        grad = grads[i]
        acc = weights[i, 0:1] * grad
        stats.append(jnp.sum(jnp.where(own, sources[i] * grad, 0.0), axis=0, keepdims=True))
        for off in range(1, taps):
            later = lift(jnp.where(mask(taps + off), grad, 0.0), off)
            acc = acc + weights[i, off : off + 1] * later
            lagged = jnp.where(own & mask(off), down(sources[i], off) * grad, 0.0)
            stats.append(jnp.sum(lagged, axis=0, keepdims=True))
        out_ref[1 + i] = lift(acc, head)[:rows].astype(narrow)
    stats.append(jnp.sum(jnp.where(own, grad_conv * mixed, 0.0), axis=0, keepdims=True))
    width = stats[0].shape[1]
    stats.append(jnp.zeros((stats_ref.shape[0] - len(stats), width), wide))
    stats_ref[...] = jnp.concatenate(stats, 0)


def epilogue(back, sources, upstream, masks, short_weights, skip, rows):
    _, frame, chans = back.shape
    taps = short_weights.shape[1]
    block = 256 if chans % 256 == 0 else chans
    grid = (chans // block,)
    stat_rows = 16
    return pl.pallas_call(
        epilogue_kernel,
        grid=grid,
        in_specs=[
            pl.BlockSpec((None, frame, block), lambda c: (0, 0, c)),
            pl.BlockSpec((None, frame, block), lambda c: (1, 0, c)),
            pl.BlockSpec((3, frame, block), lambda c: (0, 0, c)),
            pl.BlockSpec((frame, block), lambda c: (0, c)),
            pl.BlockSpec(masks.shape, lambda c: (0, 0, 0)),
            pl.BlockSpec((3, taps, block), lambda c: (0, 0, c)),
            pl.BlockSpec((1, block), lambda c: (0, c)),
        ],
        out_specs=[
            pl.BlockSpec((4, rows, block), lambda c: (0, 0, c)),
            pl.BlockSpec((stat_rows, block), lambda c: (0, c)),
        ],
        out_shape=[
            jax.ShapeDtypeStruct((4, rows, chans), jnp.bfloat16),
            jax.ShapeDtypeStruct((stat_rows, chans), jnp.float32),
        ],
    )(back, back, sources, upstream, masks, short_weights, skip[None])


def local(query, keys, values, cotangent, long_filter, short_weights, skip, lengths):
    parts = lax.axis_size("ctx")
    index = lax.axis_index("ctx")
    groups = lax.axis_size("dp")
    q_rows, k_rows, v_rows, c_rows = query[0], keys[0], values[0], cotangent[0]
    rows, chans = q_rows.shape
    taps = short_weights.shape[1]
    head = taps - 1
    seq_len = rows * parts
    lanes = chans // parts
    ext = rows + head
    frame = -(-(rows + 2 * head) // 8) * 8
    doc_len = lengths[0]
    starts = jnp.cumsum(doc_len) - doc_len

    position = index * rows + jnp.arange(ext, dtype=jnp.int32)
    begin = jnp.max(jnp.where(starts[None, :] <= position[:, None], starts[None, :], 0), axis=1)
    valid = position[None, :] - jnp.arange(taps, dtype=jnp.int32)[:, None] >= begin[None, :]
    valid_after = valid & (position < seq_len)[None, :]

    prev = shifted(jnp.stack([a[rows - head :] for a in (q_rows, k_rows, v_rows)]), "ctx", 1)
    nxt = shifted(jnp.stack([a[:head] for a in (q_rows, k_rows, v_rows, c_rows)]), "ctx", -1)
    padded = [
        jnp.concatenate([prev[i], src, nxt[i]], 0).astype(jnp.float32)
        for i, src in enumerate((q_rows, k_rows, v_rows))
    ]

    def short_forward(wide, weights):
        summed = weights[0] * wide[head : head + ext]
        for offset in range(1, taps):
            begin_at = head - offset
            summed = summed + jnp.where(
                valid[offset][:, None], weights[offset] * wide[begin_at : begin_at + ext], 0.0
            )
        return summed.astype(jnp.bfloat16).astype(jnp.float32)

    q_short = short_forward(padded[0], short_weights[0])
    k_short = short_forward(padded[1], short_weights[1])
    v_short = short_forward(padded[2], short_weights[2])
    upstream = jnp.concatenate([c_rows, nxt[3]], 0).astype(jnp.float32)
    mixed = (k_short * v_short).astype(jnp.bfloat16)
    grad_conv = (upstream * q_short).astype(jnp.bfloat16)
    mixed_wide = mixed.astype(jnp.float32)
    grad_wide = grad_conv.astype(jnp.float32)

    chunks = 2 if lanes % 2 == 0 else 1
    width = lanes // chunks

    def to_columns(data, part):
        count = data.shape[0]
        split = data.reshape(count, rows, parts, chunks, width)[:, :, :, part]
        moved = lax.all_to_all(split.transpose(0, 2, 1, 3), "ctx", 1, 1, tiled=True)
        return moved.reshape(count, seq_len, width)

    spread = long_filter.reshape(1, rows, parts, lanes).transpose(0, 2, 1, 3)
    filter_columns = lax.all_to_all(spread, "ctx", 1, 1, tiled=True)
    filter_columns = filter_columns.reshape(1, seq_len, chunks, width)
    sent = jnp.stack([mixed[:rows], grad_conv[:rows]])
    returned = []
    previous = None
    for part in range(chunks):
        columns = jnp.concatenate([filter_columns[:, :, part], to_columns(sent, part)], 0)
        if previous is not None:
            columns, previous = lax.optimization_barrier((columns, previous))
            returned.append(lax.all_to_all(previous, "ctx", 1, 1, tiled=True))
        spectra = fft_forward(columns)
        raw = fft_inverse(spectral_products(spectra), seq_len).astype(jnp.bfloat16)
        raw = jnp.concatenate(
            [jnp.zeros((3, head, width), raw.dtype), raw, jnp.zeros((3, frame - rows - head, width), raw.dtype)], 1
        )
        blocks = jnp.stack([raw[:, j * rows : j * rows + frame] for j in range(parts)], 1)
        previous = blocks
    returned.append(lax.all_to_all(previous, "ctx", 1, 1, tiled=True))
    back = jnp.stack(returned, 3).transpose(0, 2, 1, 3, 4).reshape(3, frame, chans)

    spot = index * rows - head + jnp.arange(frame, dtype=jnp.int32)
    spot_begin = jnp.max(jnp.where(starts[None, :] <= spot[:, None], starts[None, :], 0), axis=1)
    spot_valid = spot[None, :] - jnp.arange(taps, dtype=jnp.int32)[:, None] >= spot_begin[None, :]
    spot_after = spot_valid & ((spot >= 0) & (spot < seq_len))[None, :]
    spot_own = ((spot >= index * rows) & (spot < index * rows + rows))[None, :]
    masks = jnp.concatenate([spot_valid, spot_after, spot_own], 0).astype(jnp.float32)
    masks = jnp.concatenate([masks, jnp.zeros(((-masks.shape[0]) % 8, frame), jnp.float32)], 0)
    tail = frame - rows - 2 * head
    sources = jnp.stack([
        jnp.concatenate([prev[i], src, nxt[i], jnp.zeros((tail, chans), src.dtype)], 0)
        for i, src in enumerate((q_rows, k_rows, v_rows))
    ])
    framed_up = jnp.concatenate(
        [jnp.zeros((head, chans), c_rows.dtype), c_rows, nxt[3], jnp.zeros((tail, chans), c_rows.dtype)], 0
    )
    outs, stats = epilogue(back, sources, framed_up, masks[:, :, None], short_weights, skip, rows)
    summed = mesh_sum(stats[: 3 * taps + 1], ("dp", "ctx"))
    gated, grad_q, grad_k, grad_v = outs[0], outs[1], outs[2], outs[3]
    filter_part = halving_scatter(back[2, head : head + rows].astype(jnp.float32), "dp")
    scale = 1.0 / (groups * seq_len)
    return (
        gated[None],
        grad_q.astype(jnp.bfloat16)[None],
        grad_k.astype(jnp.bfloat16)[None],
        grad_v.astype(jnp.bfloat16)[None],
        filter_part * scale,
        summed[: 3 * taps].reshape(3, taps, chans) * scale,
        summed[3 * taps] * scale,
    )


def solution(mesh):
    in_specs = (
        P("dp", "ctx", None),
        P("dp", "ctx", None),
        P("dp", "ctx", None),
        P("dp", "ctx", None),
        P("ctx", None),
        P(),
        P(),
        P("dp", None),
    )
    out_specs = (
        P("dp", "ctx", None),
        P("dp", "ctx", None),
        P("dp", "ctx", None),
        P("dp", "ctx", None),
        P("ctx", "dp"),
        P(),
        P(),
    )
    return jax.shard_map(local, mesh=mesh, in_specs=in_specs, out_specs=out_specs, check_vma=False)
```

```python
import math

import jax
import jax.numpy as jnp
import ml_dtypes
import numpy as np
from jax import lax
from jax.experimental import pallas as pl
from jax.experimental.pallas import tpu as pltpu
from jax.sharding import PartitionSpec as P


def shifted(x, axis, by):
    length = lax.axis_size(axis)
    pairs = [(i, i + by) for i in range(length) if 0 <= i + by < length]
    return lax.ppermute(x, axis, pairs)


def table_halves(table):
    upper = table.astype(ml_dtypes.bfloat16)
    lower = (table - upper.astype(np.float64)).astype(ml_dtypes.bfloat16)
    return jnp.asarray(upper), jnp.asarray(lower)


def split_product(form, table, data, exact=True):
    upper, lower = table_halves(table)
    wide = jnp.float32
    if not exact:
        return jnp.einsum(form, upper, data.astype(jnp.bfloat16), preferred_element_type=wide)
    if data.dtype == jnp.bfloat16:
        total = jnp.einsum(form, upper, data, preferred_element_type=wide)
        return total + jnp.einsum(form, lower, data, preferred_element_type=wide)
    data_upper = lax.optimization_barrier(data.astype(jnp.bfloat16))
    data_lower = (data - data_upper.astype(wide)).astype(jnp.bfloat16)
    total = jnp.einsum(form, upper, data_upper, preferred_element_type=wide)
    total = total + jnp.einsum(form, lower, data_upper, preferred_element_type=wide)
    return total + jnp.einsum(form, upper, data_lower, preferred_element_type=wide)


def batched_product(table, data):
    count, outer, twice, lanes = data.shape
    upper = jnp.asarray(table.astype(ml_dtypes.bfloat16))
    upper = jnp.broadcast_to(upper, (count, outer, twice, twice))
    return jnp.einsum(
        "skab,skbc->skac", upper, data.astype(jnp.bfloat16), preferred_element_type=jnp.float32
    )


def factors(size):
    bits = size.bit_length() - 1
    inner = 1 << (bits // 2)
    return size // inner, inner


def twiddles(outer, inner, size):
    phase = 2.0 * np.pi * np.outer(np.arange(outer), np.arange(inner)) / size
    cosine = jnp.asarray(np.cos(phase), jnp.float32)[None, :, :, None]
    sine = jnp.asarray(np.sin(phase), jnp.float32)[None, :, :, None]
    return cosine, sine


def inner_table(inner, sign):
    phase = 2.0 * np.pi * np.outer(np.arange(inner), np.arange(inner)) / inner
    cosine, sine = np.cos(phase), sign * np.sin(phase)
    return np.block([[cosine, sine], [-sine, cosine]])


def fft_forward(signal):
    count, length, lanes = signal.shape
    size = 2 * length
    outer, inner = factors(size)
    half = outer // 2
    phase = 2.0 * np.pi * np.outer(np.arange(outer), np.arange(half)) / outer
    first = np.concatenate([np.cos(phase), -np.sin(phase)], 0)
    blocks = signal.reshape(count, half, inner, lanes).transpose(1, 0, 2, 3)
    stage = split_product("kn,nsqb->ksqb", first, blocks)
    real_part, imag_part = stage[:outer], stage[outer:]
    cosine, sine = twiddles(outer, inner, size)
    cosine, sine = cosine.transpose(1, 0, 2, 3), sine.transpose(1, 0, 2, 3)
    turned = jnp.stack(
        [real_part * cosine + imag_part * sine, imag_part * cosine - real_part * sine]
    ).astype(jnp.bfloat16)
    turned = turned.transpose(0, 3, 2, 1, 4).reshape(2 * inner, count, outer, lanes)
    return split_product("ab,bskc->askc", inner_table(inner, 1.0), turned, exact=False)


def fft_inverse(spectrum, length):
    twice, count, outer, lanes = spectrum.shape
    inner = twice // 2
    size = outer * inner
    half = outer // 2
    stage = split_product("ab,bskc->askc", inner_table(inner, -1.0), spectrum, exact=False)
    real_part, imag_part = stage[:inner], stage[inner:]
    cosine, sine = twiddles(outer, inner, size)
    cosine, sine = cosine.transpose(2, 0, 1, 3), sine.transpose(2, 0, 1, 3)
    turned = jnp.stack(
        [real_part * cosine - imag_part * sine, imag_part * cosine + real_part * sine]
    ).astype(jnp.bfloat16)
    turned = turned.transpose(0, 3, 2, 1, 4).reshape(2 * outer, count, inner, lanes)
    phase = 2.0 * np.pi * np.outer(np.arange(half), np.arange(outer)) / outer
    last = np.concatenate([np.cos(phase), -np.sin(phase)], 1) / size
    result = split_product("nk,ksqb->nsqb", last, turned, exact=False)
    return result.transpose(1, 0, 2, 3).reshape(count, length, lanes)


def spectral_products(spectra):
    inner = spectra.shape[0] // 2
    parts = [(spectra[:inner, i], spectra[inner:, i]) for i in range(3)]
    (f_re, f_im), (m_re, m_im), (g_re, g_im) = parts
    conv = jnp.concatenate([m_re * f_re - m_im * f_im, m_re * f_im + m_im * f_re], 0)
    back = jnp.concatenate([g_re * f_re + g_im * f_im, g_im * f_re - g_re * f_im], 0)
    cross = jnp.concatenate([g_re * m_re + g_im * m_im, g_im * m_re - g_re * m_im], 0)
    return jnp.stack([conv, back, cross], 1)


def all_sum(data, axis):
    size = lax.axis_size(axis)
    total = data
    for step in range(1, size):
        total = total + lax.ppermute(data, axis, [(i, (i + step) % size) for i in range(size)])
    return total


def mesh_sum(data, axes):
    count = 1
    for axis in axes:
        count *= lax.axis_size(axis)
    rows, chans = data.shape
    pieces = data.reshape(rows, count, chans // count).transpose(1, 0, 2)
    mine = jnp.sum(lax.all_to_all(pieces, axes, 0, 0, tiled=True), axis=0)
    spread = jnp.broadcast_to(mine[None], (count,) + mine.shape)
    gathered = lax.all_to_all(spread, axes, 0, 0, tiled=True)
    return gathered.transpose(1, 0, 2).reshape(rows, chans)


def halving_rows(data, axis):
    size = lax.axis_size(axis)
    index = lax.axis_index(axis)
    blocks = data.reshape(size, data.shape[0] // size, data.shape[1])
    step = size // 2
    while step >= 1:
        half = blocks.shape[0] // 2
        upper = (index // step) % 2 == 1
        keep = jnp.where(upper, blocks[half:], blocks[:half])
        give = jnp.where(upper, blocks[:half], blocks[half:])
        blocks = keep + lax.ppermute(give, axis, [(i, i ^ step) for i in range(size)])
        step //= 2
    return blocks.reshape(-1, data.shape[1])


def route_filter_grad(block, rows):
    parts = lax.axis_size("ctx")
    groups = lax.axis_size("dp")
    ratio = parts // groups
    pieces = block.reshape(ratio, rows, block.shape[1])
    columns = []
    for lane_block in range(ratio):
        total = None
        for piece in range(ratio):
            pairs = [
                (sd * parts + sc, (sc // ratio) * parts + sd * ratio + piece)
                for sd in range(groups)
                for sc in range(lane_block, parts, ratio)
            ]
            got = lax.ppermute(pieces[piece], ("dp", "ctx"), pairs)
            total = got if total is None else total + got
        columns.append(total)
    return jnp.concatenate(columns, 1)


def halving_scatter(data, axis):
    size = lax.axis_size(axis)
    index = lax.axis_index(axis)
    rows, chans = data.shape
    blocks = data.reshape(rows, size, chans // size)
    step = size // 2
    while step >= 1:
        half = blocks.shape[1] // 2
        upper = (index // step) % 2 == 1
        keep = jnp.where(upper, blocks[:, half:], blocks[:, :half])
        give = jnp.where(upper, blocks[:, :half], blocks[:, half:])
        blocks = keep + lax.ppermute(give, axis, [(i, i ^ step) for i in range(size)])
        step //= 2
    return blocks.reshape(rows, chans // size)


def epilogue_kernel(conv_ref, back_ref, src_ref, up_ref, mask_ref, w_ref, skip_ref, out_ref, stats_ref):
    wide, narrow = jnp.float32, jnp.bfloat16
    taps = w_ref.shape[1]
    head = taps - 1
    frame = src_ref.shape[1]
    rows = out_ref.shape[1]

    def mask(i):
        return mask_ref[i] > 0.5

    def down(x, by):
        return pltpu.roll(x, by, 0) if by else x

    def lift(x, by):
        return pltpu.roll(x, frame - by, 0) if by else x

    sources = [src_ref[i].astype(wide) for i in range(3)]
    weights = w_ref[...]
    shorts = []
    for i in range(3):
        total = weights[i, 0:1] * sources[i]
        for off in range(1, taps):
            total = total + jnp.where(mask(off), weights[i, off : off + 1] * down(sources[i], off), 0.0)
        shorts.append(total.astype(narrow).astype(wide))
    q_short, k_short, v_short = shorts
    upstream = up_ref[...].astype(wide)
    skip = skip_ref[...]
    mixed = (k_short * v_short).astype(narrow).astype(wide)
    grad_conv = (upstream * q_short).astype(narrow).astype(wide)
    conv = conv_ref[...].astype(wide) + skip * mixed
    grad_mixed = back_ref[...].astype(wide) + skip * grad_conv
    own = mask(2 * taps)
    out_ref[0] = lift(q_short * conv, head)[:rows].astype(narrow)
    grads = [upstream * conv, grad_mixed * v_short, grad_mixed * k_short]
    stats = []
    for i in range(3):
        grad = grads[i]
        acc = weights[i, 0:1] * grad
        stats.append(jnp.sum(jnp.where(own, sources[i] * grad, 0.0), axis=0, keepdims=True))
        for off in range(1, taps):
            later = lift(jnp.where(mask(taps + off), grad, 0.0), off)
            acc = acc + weights[i, off : off + 1] * later
            lagged = jnp.where(own & mask(off), down(sources[i], off) * grad, 0.0)
            stats.append(jnp.sum(lagged, axis=0, keepdims=True))
        out_ref[1 + i] = lift(acc, head)[:rows].astype(narrow)
    stats.append(jnp.sum(jnp.where(own, grad_conv * mixed, 0.0), axis=0, keepdims=True))
    width = stats[0].shape[1]
    stats.append(jnp.zeros((stats_ref.shape[0] - len(stats), width), wide))
    stats_ref[...] = jnp.concatenate(stats, 0)


def epilogue(back, sources, upstream, masks, short_weights, skip, rows):
    _, frame, chans = back.shape
    taps = short_weights.shape[1]
    block = 256 if chans % 256 == 0 else chans
    grid = (chans // block,)
    stat_rows = 16
    return pl.pallas_call(
        epilogue_kernel,
        grid=grid,
        in_specs=[
            pl.BlockSpec((None, frame, block), lambda c: (0, 0, c)),
            pl.BlockSpec((None, frame, block), lambda c: (1, 0, c)),
            pl.BlockSpec((3, frame, block), lambda c: (0, 0, c)),
            pl.BlockSpec((frame, block), lambda c: (0, c)),
            pl.BlockSpec(masks.shape, lambda c: (0, 0, 0)),
            pl.BlockSpec((3, taps, block), lambda c: (0, 0, c)),
            pl.BlockSpec((1, block), lambda c: (0, c)),
        ],
        out_specs=[
            pl.BlockSpec((4, rows, block), lambda c: (0, 0, c)),
            pl.BlockSpec((stat_rows, block), lambda c: (0, c)),
        ],
        out_shape=[
            jax.ShapeDtypeStruct((4, rows, chans), jnp.bfloat16),
            jax.ShapeDtypeStruct((stat_rows, chans), jnp.float32),
        ],
    )(back, back, sources, upstream, masks, short_weights, skip[None])


def local(query, keys, values, cotangent, long_filter, short_weights, skip, lengths):
    parts = lax.axis_size("ctx")
    index = lax.axis_index("ctx")
    groups = lax.axis_size("dp")
    q_rows, k_rows, v_rows, c_rows = query[0], keys[0], values[0], cotangent[0]
    rows, chans = q_rows.shape
    taps = short_weights.shape[1]
    head = taps - 1
    seq_len = rows * parts
    lanes = chans // parts
    ext = rows + head
    frame = -(-(rows + 2 * head) // 8) * 8
    doc_len = lengths[0]
    starts = jnp.cumsum(doc_len) - doc_len

    position = index * rows + jnp.arange(ext, dtype=jnp.int32)
    begin = jnp.max(jnp.where(starts[None, :] <= position[:, None], starts[None, :], 0), axis=1)
    valid = position[None, :] - jnp.arange(taps, dtype=jnp.int32)[:, None] >= begin[None, :]
    valid_after = valid & (position < seq_len)[None, :]

    prev = shifted(jnp.stack([a[rows - head :] for a in (q_rows, k_rows, v_rows)]), "ctx", 1)
    nxt = shifted(jnp.stack([a[:head] for a in (q_rows, k_rows, v_rows, c_rows)]), "ctx", -1)
    padded = [
        jnp.concatenate([prev[i], src, nxt[i]], 0).astype(jnp.float32)
        for i, src in enumerate((q_rows, k_rows, v_rows))
    ]

    def short_forward(wide, weights):
        summed = weights[0] * wide[head : head + ext]
        for offset in range(1, taps):
            begin_at = head - offset
            summed = summed + jnp.where(
                valid[offset][:, None], weights[offset] * wide[begin_at : begin_at + ext], 0.0
            )
        return summed.astype(jnp.bfloat16).astype(jnp.float32)

    q_short = short_forward(padded[0], short_weights[0])
    k_short = short_forward(padded[1], short_weights[1])
    v_short = short_forward(padded[2], short_weights[2])
    upstream = jnp.concatenate([c_rows, nxt[3]], 0).astype(jnp.float32)
    mixed = (k_short * v_short).astype(jnp.bfloat16)
    grad_conv = (upstream * q_short).astype(jnp.bfloat16)
    mixed_wide = mixed.astype(jnp.float32)
    grad_wide = grad_conv.astype(jnp.float32)

    chunks = 2 if lanes % 2 == 0 else 1
    width = lanes // chunks

    def to_columns(data, part):
        count = data.shape[0]
        split = data.reshape(count, rows, parts, chunks, width)[:, :, :, part]
        moved = lax.all_to_all(split.transpose(0, 2, 1, 3), "ctx", 1, 1, tiled=True)
        return moved.reshape(count, seq_len, width)

    sent = jnp.stack([long_filter, mixed[:rows], grad_conv[:rows]])
    returned = []
    lagged_parts = []
    previous = None
    for part in range(chunks):
        columns = to_columns(sent, part)
        if previous is not None:
            columns, previous = lax.optimization_barrier((columns, previous))
            returned.append(lax.all_to_all(previous, "ctx", 1, 1, tiled=True))
        spectra = fft_forward(columns)
        raw = fft_inverse(spectral_products(spectra), seq_len)
        lagged_parts.append(raw[2])
        raw = raw[:2].astype(jnp.bfloat16)
        raw = jnp.concatenate(
            [jnp.zeros((2, head, width), raw.dtype), raw, jnp.zeros((2, frame - rows - head, width), raw.dtype)], 1
        )
        blocks = jnp.stack([raw[:, j * rows : j * rows + frame] for j in range(parts)], 1)
        previous = blocks
    returned.append(lax.all_to_all(previous, "ctx", 1, 1, tiled=True))
    back = jnp.stack(returned, 3).transpose(0, 2, 1, 3, 4).reshape(2, frame, chans)
    lagged = halving_rows(jnp.concatenate(lagged_parts, 1), "dp")
    filter_part = route_filter_grad(lagged, rows)

    spot = index * rows - head + jnp.arange(frame, dtype=jnp.int32)
    spot_begin = jnp.max(jnp.where(starts[None, :] <= spot[:, None], starts[None, :], 0), axis=1)
    spot_valid = spot[None, :] - jnp.arange(taps, dtype=jnp.int32)[:, None] >= spot_begin[None, :]
    spot_after = spot_valid & ((spot >= 0) & (spot < seq_len))[None, :]
    spot_own = ((spot >= index * rows) & (spot < index * rows + rows))[None, :]
    masks = jnp.concatenate([spot_valid, spot_after, spot_own], 0).astype(jnp.float32)
    masks = jnp.concatenate([masks, jnp.zeros(((-masks.shape[0]) % 8, frame), jnp.float32)], 0)
    tail = frame - rows - 2 * head
    sources = jnp.stack([
        jnp.concatenate([prev[i], src, nxt[i], jnp.zeros((tail, chans), src.dtype)], 0)
        for i, src in enumerate((q_rows, k_rows, v_rows))
    ])
    framed_up = jnp.concatenate(
        [jnp.zeros((head, chans), c_rows.dtype), c_rows, nxt[3], jnp.zeros((tail, chans), c_rows.dtype)], 0
    )
    outs, stats = epilogue(back, sources, framed_up, masks[:, :, None], short_weights, skip, rows)
    summed = mesh_sum(stats[: 3 * taps + 1], ("dp", "ctx"))
    gated, grad_q, grad_k, grad_v = outs[0], outs[1], outs[2], outs[3]
    scale = 1.0 / (groups * seq_len)
    return (
        gated[None],
        grad_q.astype(jnp.bfloat16)[None],
        grad_k.astype(jnp.bfloat16)[None],
        grad_v.astype(jnp.bfloat16)[None],
        filter_part * scale,
        summed[: 3 * taps].reshape(3, taps, chans) * scale,
        summed[3 * taps] * scale,
    )


def solution(mesh):
    in_specs = (
        P("dp", "ctx", None),
        P("dp", "ctx", None),
        P("dp", "ctx", None),
        P("dp", "ctx", None),
        P("ctx", None),
        P(),
        P(),
        P("dp", None),
    )
    out_specs = (
        P("dp", "ctx", None),
        P("dp", "ctx", None),
        P("dp", "ctx", None),
        P("dp", "ctx", None),
        P("ctx", "dp"),
        P(),
        P(),
    )
    return jax.shard_map(local, mesh=mesh, in_specs=in_specs, out_specs=out_specs, check_vma=False)
```

```python
import functools
import math

import jax
import jax.numpy as jnp
import ml_dtypes
import numpy as np
from jax import lax
from jax.experimental import pallas as pl
from jax.experimental.pallas import tpu as pltpu
from jax.sharding import PartitionSpec as P


def shifted(x, axis, by):
    length = lax.axis_size(axis)
    pairs = [(i, i + by) for i in range(length) if 0 <= i + by < length]
    return lax.ppermute(x, axis, pairs)


def table_halves(table):
    upper = table.astype(ml_dtypes.bfloat16)
    lower = (table - upper.astype(np.float64)).astype(ml_dtypes.bfloat16)
    return jnp.asarray(upper), jnp.asarray(lower)


def split_product(form, table, data, exact=True):
    upper, lower = table_halves(table)
    wide = jnp.float32
    if not exact:
        return jnp.einsum(form, upper, data.astype(jnp.bfloat16), preferred_element_type=wide)
    if data.dtype == jnp.bfloat16:
        total = jnp.einsum(form, upper, data, preferred_element_type=wide)
        return total + jnp.einsum(form, lower, data, preferred_element_type=wide)
    data_upper = lax.optimization_barrier(data.astype(jnp.bfloat16))
    data_lower = (data - data_upper.astype(wide)).astype(jnp.bfloat16)
    total = jnp.einsum(form, upper, data_upper, preferred_element_type=wide)
    total = total + jnp.einsum(form, lower, data_upper, preferred_element_type=wide)
    return total + jnp.einsum(form, upper, data_lower, preferred_element_type=wide)


def batched_product(table, data):
    count, outer, twice, lanes = data.shape
    upper = jnp.asarray(table.astype(ml_dtypes.bfloat16))
    upper = jnp.broadcast_to(upper, (count, outer, twice, twice))
    return jnp.einsum(
        "skab,skbc->skac", upper, data.astype(jnp.bfloat16), preferred_element_type=jnp.float32
    )


def factors(size):
    bits = size.bit_length() - 1
    inner = 1 << (bits // 2)
    return size // inner, inner


def twiddles(outer, inner, size):
    phase = 2.0 * np.pi * np.outer(np.arange(outer), np.arange(inner)) / size
    cosine = jnp.asarray(np.cos(phase), jnp.float32)[None, :, :, None]
    sine = jnp.asarray(np.sin(phase), jnp.float32)[None, :, :, None]
    return cosine, sine


def inner_table(inner, sign):
    phase = 2.0 * np.pi * np.outer(np.arange(inner), np.arange(inner)) / inner
    cosine, sine = np.cos(phase), sign * np.sin(phase)
    return np.block([[cosine, sine], [-sine, cosine]])


def fft_forward(signal):
    count, length, lanes = signal.shape
    size = 2 * length
    outer, inner = factors(size)
    half = outer // 2
    phase = 2.0 * np.pi * np.outer(np.arange(outer), np.arange(half)) / outer
    first = np.concatenate([np.cos(phase), -np.sin(phase)], 0)
    blocks = signal.reshape(count, half, inner, lanes).transpose(1, 0, 2, 3)
    stage = split_product("kn,nsqb->ksqb", first, blocks)
    real_part, imag_part = stage[:outer], stage[outer:]
    cosine, sine = twiddles(outer, inner, size)
    cosine, sine = cosine.transpose(1, 0, 2, 3), sine.transpose(1, 0, 2, 3)
    turned = jnp.stack(
        [real_part * cosine + imag_part * sine, imag_part * cosine - real_part * sine]
    ).astype(jnp.bfloat16)
    turned = turned.transpose(0, 3, 2, 1, 4).reshape(2 * inner, count, outer, lanes)
    return split_product("ab,bskc->askc", inner_table(inner, 1.0), turned, exact=False)


def fft_inverse(spectrum, length):
    twice, count, outer, lanes = spectrum.shape
    inner = twice // 2
    size = outer * inner
    half = outer // 2
    stage = split_product("ab,bskc->askc", inner_table(inner, -1.0), spectrum, exact=False)
    real_part, imag_part = stage[:inner], stage[inner:]
    cosine, sine = twiddles(outer, inner, size)
    cosine, sine = cosine.transpose(2, 0, 1, 3), sine.transpose(2, 0, 1, 3)
    turned = jnp.stack(
        [real_part * cosine - imag_part * sine, imag_part * cosine + real_part * sine]
    ).astype(jnp.bfloat16)
    turned = turned.transpose(0, 3, 2, 1, 4).reshape(2 * outer, count, inner, lanes)
    phase = 2.0 * np.pi * np.outer(np.arange(half), np.arange(outer)) / outer
    last = np.concatenate([np.cos(phase), -np.sin(phase)], 1) / size
    result = split_product("nk,ksqb->nsqb", last, turned, exact=False)
    return result.transpose(1, 0, 2, 3).reshape(count, length, lanes)


def spectral_products(spectra):
    inner = spectra.shape[0] // 2
    parts = [(spectra[:inner, i], spectra[inner:, i]) for i in range(3)]
    (f_re, f_im), (m_re, m_im), (g_re, g_im) = parts
    conv = jnp.concatenate([m_re * f_re - m_im * f_im, m_re * f_im + m_im * f_re], 0)
    back = jnp.concatenate([g_re * f_re + g_im * f_im, g_im * f_re - g_re * f_im], 0)
    cross = jnp.concatenate([g_re * m_re + g_im * m_im, g_im * m_re - g_re * m_im], 0)
    return jnp.stack([conv, back, cross], 1)


def all_sum(data, axis):
    size = lax.axis_size(axis)
    total = data
    for step in range(1, size):
        total = total + lax.ppermute(data, axis, [(i, (i + step) % size) for i in range(size)])
    return total


def mesh_sum(data, axes):
    count = 1
    for axis in axes:
        count *= lax.axis_size(axis)
    rows, chans = data.shape
    pieces = data.reshape(rows, count, chans // count).transpose(1, 0, 2)
    mine = jnp.sum(lax.all_to_all(pieces, axes, 0, 0, tiled=True), axis=0)
    spread = jnp.broadcast_to(mine[None], (count,) + mine.shape)
    gathered = lax.all_to_all(spread, axes, 0, 0, tiled=True)
    return gathered.transpose(1, 0, 2).reshape(rows, chans)


def halving_rows(data, axis):
    size = lax.axis_size(axis)
    index = lax.axis_index(axis)
    blocks = data.reshape(size, data.shape[0] // size, data.shape[1])
    step = size // 2
    while step >= 1:
        half = blocks.shape[0] // 2
        upper = (index // step) % 2 == 1
        keep = jnp.where(upper, blocks[half:], blocks[:half])
        give = jnp.where(upper, blocks[:half], blocks[half:])
        blocks = keep + lax.ppermute(give, axis, [(i, i ^ step) for i in range(size)])
        step //= 2
    return blocks.reshape(-1, data.shape[1])


def route_filter_grad(block, rows):
    parts = lax.axis_size("ctx")
    groups = lax.axis_size("dp")
    ratio = parts // groups
    pieces = block.reshape(ratio, rows, block.shape[1])
    columns = []
    for lane_block in range(ratio):
        total = None
        for piece in range(ratio):
            pairs = [
                (sd * parts + sc, (sc // ratio) * parts + sd * ratio + piece)
                for sd in range(groups)
                for sc in range(lane_block, parts, ratio)
            ]
            got = lax.ppermute(pieces[piece], ("dp", "ctx"), pairs)
            total = got if total is None else total + got
        columns.append(total)
    return jnp.concatenate(columns, 1)


def halving_scatter(data, axis):
    size = lax.axis_size(axis)
    index = lax.axis_index(axis)
    rows, chans = data.shape
    blocks = data.reshape(rows, size, chans // size)
    step = size // 2
    while step >= 1:
        half = blocks.shape[1] // 2
        upper = (index // step) % 2 == 1
        keep = jnp.where(upper, blocks[:, half:], blocks[:, :half])
        give = jnp.where(upper, blocks[:, :half], blocks[:, half:])
        blocks = keep + lax.ppermute(give, axis, [(i, i ^ step) for i in range(size)])
        step //= 2
    return blocks.reshape(rows, chans // size)


def epilogue_kernel(conv_ref, back_ref, src_ref, up_ref, mask_ref, w_ref, skip_ref, *outputs, want_stats):
    out_ref, stats_ref = (None, outputs[0]) if want_stats else (outputs[0], None)
    wide, narrow = jnp.float32, jnp.bfloat16
    taps = w_ref.shape[1]
    head = taps - 1
    frame = src_ref.shape[1]
    rows = out_ref.shape[1] if out_ref is not None else frame - 4 * head

    def mask(i):
        return mask_ref[i] > 0.5

    def down(x, by):
        return pltpu.roll(x, by, 0) if by else x

    def lift(x, by):
        return pltpu.roll(x, frame - by, 0) if by else x

    sources = [src_ref[i].astype(wide) for i in range(3)]
    weights = w_ref[...]
    shorts = []
    for i in range(3):
        total = weights[i, 0:1] * sources[i]
        for off in range(1, taps):
            total = total + jnp.where(mask(off), weights[i, off : off + 1] * down(sources[i], off), 0.0)
        shorts.append(total.astype(narrow).astype(wide))
    q_short, k_short, v_short = shorts
    upstream = up_ref[...].astype(wide)
    skip = skip_ref[...]
    mixed = (k_short * v_short).astype(narrow).astype(wide)
    grad_conv = (upstream * q_short).astype(narrow).astype(wide)
    conv = conv_ref[...].astype(wide) + skip * mixed
    grad_mixed = back_ref[...].astype(wide) + skip * grad_conv
    own = mask(2 * taps)
    grads = [upstream * conv, grad_mixed * v_short, grad_mixed * k_short]
    if not want_stats:
        out_ref[0] = lift(q_short * conv, head)[:rows].astype(narrow)
        for i in range(3):
            grad = grads[i]
            acc = weights[i, 0:1] * grad
            for off in range(1, taps):
                later = lift(jnp.where(mask(taps + off), grad, 0.0), off)
                acc = acc + weights[i, off : off + 1] * later
            out_ref[1 + i] = lift(acc, head)[:rows].astype(narrow)
        return
    stats = []
    for i in range(3):
        grad = grads[i]
        stats.append(jnp.sum(jnp.where(own, sources[i] * grad, 0.0), axis=0, keepdims=True))
        for off in range(1, taps):
            lagged = jnp.where(own & mask(off), down(sources[i], off) * grad, 0.0)
            stats.append(jnp.sum(lagged, axis=0, keepdims=True))
    stats.append(jnp.sum(jnp.where(own, grad_conv * mixed, 0.0), axis=0, keepdims=True))
    width = stats[0].shape[1]
    stats.append(jnp.zeros((stats_ref.shape[0] - len(stats), width), wide))
    stats_ref[...] = jnp.concatenate(stats, 0)


def epilogue(back, sources, upstream, masks, short_weights, skip, rows, want_stats):
    _, frame, chans = back.shape
    taps = short_weights.shape[1]
    block = 256 if chans % 256 == 0 else chans
    grid = (chans // block,)
    stat_rows = 16
    if want_stats:
        out_specs = pl.BlockSpec((stat_rows, block), lambda c: (0, c))
        out_shape = jax.ShapeDtypeStruct((stat_rows, chans), jnp.float32)
    else:
        out_specs = pl.BlockSpec((4, rows, block), lambda c: (0, 0, c))
        out_shape = jax.ShapeDtypeStruct((4, rows, chans), jnp.bfloat16)
    return pl.pallas_call(
        functools.partial(epilogue_kernel, want_stats=want_stats),
        grid=grid,
        in_specs=[
            pl.BlockSpec((None, frame, block), lambda c: (0, 0, c)),
            pl.BlockSpec((None, frame, block), lambda c: (1, 0, c)),
            pl.BlockSpec((3, frame, block), lambda c: (0, 0, c)),
            pl.BlockSpec((frame, block), lambda c: (0, c)),
            pl.BlockSpec(masks.shape, lambda c: (0, 0, 0)),
            pl.BlockSpec((3, taps, block), lambda c: (0, 0, c)),
            pl.BlockSpec((1, block), lambda c: (0, c)),
        ],
        out_specs=out_specs,
        out_shape=out_shape,
    )(back, back, sources, upstream, masks, short_weights, skip[None])


def local(query, keys, values, cotangent, long_filter, short_weights, skip, lengths):
    parts = lax.axis_size("ctx")
    index = lax.axis_index("ctx")
    groups = lax.axis_size("dp")
    q_rows, k_rows, v_rows, c_rows = query[0], keys[0], values[0], cotangent[0]
    rows, chans = q_rows.shape
    taps = short_weights.shape[1]
    head = taps - 1
    seq_len = rows * parts
    lanes = chans // parts
    ext = rows + head
    frame = -(-(rows + 2 * head) // 8) * 8
    doc_len = lengths[0]
    starts = jnp.cumsum(doc_len) - doc_len

    position = index * rows + jnp.arange(ext, dtype=jnp.int32)
    begin = jnp.max(jnp.where(starts[None, :] <= position[:, None], starts[None, :], 0), axis=1)
    valid = position[None, :] - jnp.arange(taps, dtype=jnp.int32)[:, None] >= begin[None, :]
    valid_after = valid & (position < seq_len)[None, :]

    prev = shifted(jnp.stack([a[rows - head :] for a in (q_rows, k_rows, v_rows)]), "ctx", 1)
    nxt = shifted(jnp.stack([a[:head] for a in (q_rows, k_rows, v_rows, c_rows)]), "ctx", -1)
    padded = [
        jnp.concatenate([prev[i], src, nxt[i]], 0).astype(jnp.float32)
        for i, src in enumerate((q_rows, k_rows, v_rows))
    ]

    def short_forward(wide, weights):
        summed = weights[0] * wide[head : head + ext]
        for offset in range(1, taps):
            begin_at = head - offset
            summed = summed + jnp.where(
                valid[offset][:, None], weights[offset] * wide[begin_at : begin_at + ext], 0.0
            )
        return summed.astype(jnp.bfloat16).astype(jnp.float32)

    q_short = short_forward(padded[0], short_weights[0])
    k_short = short_forward(padded[1], short_weights[1])
    v_short = short_forward(padded[2], short_weights[2])
    upstream = jnp.concatenate([c_rows, nxt[3]], 0).astype(jnp.float32)
    mixed = (k_short * v_short).astype(jnp.bfloat16)
    grad_conv = (upstream * q_short).astype(jnp.bfloat16)
    mixed_wide = mixed.astype(jnp.float32)
    grad_wide = grad_conv.astype(jnp.float32)

    chunks = 2 if lanes % 2 == 0 else 1
    width = lanes // chunks

    def to_columns(data, part):
        count = data.shape[0]
        split = data.reshape(count, rows, parts, chunks, width)[:, :, :, part]
        moved = lax.all_to_all(split.transpose(0, 2, 1, 3), "ctx", 1, 1, tiled=True)
        return moved.reshape(count, seq_len, width)

    sent = jnp.stack([long_filter, mixed[:rows], grad_conv[:rows]])
    returned = []
    lagged_parts = []
    previous = None
    for part in range(chunks):
        columns = to_columns(sent, part)
        if previous is not None:
            columns, previous = lax.optimization_barrier((columns, previous))
            returned.append(lax.all_to_all(previous, "ctx", 1, 1, tiled=True))
        spectra = fft_forward(columns)
        raw = fft_inverse(spectral_products(spectra), seq_len)
        lagged_parts.append(raw[2])
        raw = raw[:2].astype(jnp.bfloat16)
        raw = jnp.concatenate(
            [jnp.zeros((2, head, width), raw.dtype), raw, jnp.zeros((2, frame - rows - head, width), raw.dtype)], 1
        )
        blocks = jnp.stack([raw[:, j * rows : j * rows + frame] for j in range(parts)], 1)
        previous = blocks
    returned.append(lax.all_to_all(previous, "ctx", 1, 1, tiled=True))
    back = jnp.stack(returned, 3).transpose(0, 2, 1, 3, 4).reshape(2, frame, chans)
    lagged = halving_rows(jnp.concatenate(lagged_parts, 1), "dp")
    filter_part = route_filter_grad(lagged, rows)

    spot = index * rows - head + jnp.arange(frame, dtype=jnp.int32)
    spot_begin = jnp.max(jnp.where(starts[None, :] <= spot[:, None], starts[None, :], 0), axis=1)
    spot_valid = spot[None, :] - jnp.arange(taps, dtype=jnp.int32)[:, None] >= spot_begin[None, :]
    spot_after = spot_valid & ((spot >= 0) & (spot < seq_len))[None, :]
    spot_own = ((spot >= index * rows) & (spot < index * rows + rows))[None, :]
    masks = jnp.concatenate([spot_valid, spot_after, spot_own], 0).astype(jnp.float32)
    masks = jnp.concatenate([masks, jnp.zeros(((-masks.shape[0]) % 8, frame), jnp.float32)], 0)
    tail = frame - rows - 2 * head
    sources = jnp.stack([
        jnp.concatenate([prev[i], src, nxt[i], jnp.zeros((tail, chans), src.dtype)], 0)
        for i, src in enumerate((q_rows, k_rows, v_rows))
    ])
    framed_up = jnp.concatenate(
        [jnp.zeros((head, chans), c_rows.dtype), c_rows, nxt[3], jnp.zeros((tail, chans), c_rows.dtype)], 0
    )
    operands = (back, sources, framed_up, masks[:, :, None], short_weights, skip, rows)
    stats = epilogue(*operands, True)
    summed = mesh_sum(stats[: 3 * taps + 1], ("dp", "ctx"))
    outs = epilogue(*operands, False)
    gated, grad_q, grad_k, grad_v = outs[0], outs[1], outs[2], outs[3]
    scale = 1.0 / (groups * seq_len)
    return (
        gated[None],
        grad_q.astype(jnp.bfloat16)[None],
        grad_k.astype(jnp.bfloat16)[None],
        grad_v.astype(jnp.bfloat16)[None],
        filter_part * scale,
        summed[: 3 * taps].reshape(3, taps, chans) * scale,
        summed[3 * taps] * scale,
    )


def solution(mesh):
    in_specs = (
        P("dp", "ctx", None),
        P("dp", "ctx", None),
        P("dp", "ctx", None),
        P("dp", "ctx", None),
        P("ctx", None),
        P(),
        P(),
        P("dp", None),
    )
    out_specs = (
        P("dp", "ctx", None),
        P("dp", "ctx", None),
        P("dp", "ctx", None),
        P("dp", "ctx", None),
        P("ctx", "dp"),
        P(),
        P(),
    )
    return jax.shard_map(local, mesh=mesh, in_specs=in_specs, out_specs=out_specs, check_vma=False)
```

```python
import math

import jax
import jax.numpy as jnp
import ml_dtypes
import numpy as np
from jax import lax
from jax.experimental import pallas as pl
from jax.experimental.pallas import tpu as pltpu
from jax.sharding import PartitionSpec as P


def shifted(x, axis, by):
    length = lax.axis_size(axis)
    pairs = [(i, i + by) for i in range(length) if 0 <= i + by < length]
    return lax.ppermute(x, axis, pairs)


def table_halves(table):
    upper = table.astype(ml_dtypes.bfloat16)
    lower = (table - upper.astype(np.float64)).astype(ml_dtypes.bfloat16)
    return jnp.asarray(upper), jnp.asarray(lower)


def split_product(form, table, data, exact=True):
    upper, lower = table_halves(table)
    wide = jnp.float32
    if not exact:
        return jnp.einsum(form, upper, data.astype(jnp.bfloat16), preferred_element_type=wide)
    if data.dtype == jnp.bfloat16:
        total = jnp.einsum(form, upper, data, preferred_element_type=wide)
        return total + jnp.einsum(form, lower, data, preferred_element_type=wide)
    data_upper = lax.optimization_barrier(data.astype(jnp.bfloat16))
    data_lower = (data - data_upper.astype(wide)).astype(jnp.bfloat16)
    total = jnp.einsum(form, upper, data_upper, preferred_element_type=wide)
    total = total + jnp.einsum(form, lower, data_upper, preferred_element_type=wide)
    return total + jnp.einsum(form, upper, data_lower, preferred_element_type=wide)


def batched_product(table, data):
    count, outer, twice, lanes = data.shape
    upper = jnp.asarray(table.astype(ml_dtypes.bfloat16))
    upper = jnp.broadcast_to(upper, (count, outer, twice, twice))
    return jnp.einsum(
        "skab,skbc->skac", upper, data.astype(jnp.bfloat16), preferred_element_type=jnp.float32
    )


def factors(size):
    bits = size.bit_length() - 1
    inner = 1 << (bits // 2)
    return size // inner, inner


def twiddles(outer, inner, size):
    phase = 2.0 * np.pi * np.outer(np.arange(outer), np.arange(inner)) / size
    cosine = jnp.asarray(np.cos(phase), jnp.float32)[None, :, :, None]
    sine = jnp.asarray(np.sin(phase), jnp.float32)[None, :, :, None]
    return cosine, sine


def inner_table(inner, sign):
    phase = 2.0 * np.pi * np.outer(np.arange(inner), np.arange(inner)) / inner
    cosine, sine = np.cos(phase), sign * np.sin(phase)
    return np.block([[cosine, sine], [-sine, cosine]])


def fft_forward(signal):
    count, length, lanes = signal.shape
    size = 2 * length
    outer, inner = factors(size)
    half = outer // 2
    phase = 2.0 * np.pi * np.outer(np.arange(outer), np.arange(half)) / outer
    first = np.concatenate([np.cos(phase), -np.sin(phase)], 0)
    blocks = signal.reshape(count, half, inner, lanes).transpose(1, 0, 2, 3)
    stage = split_product("kn,nsqb->ksqb", first, blocks)
    real_part, imag_part = stage[:outer], stage[outer:]
    cosine, sine = twiddles(outer, inner, size)
    cosine, sine = cosine.transpose(1, 0, 2, 3), sine.transpose(1, 0, 2, 3)
    turned = jnp.stack(
        [real_part * cosine + imag_part * sine, imag_part * cosine - real_part * sine]
    ).astype(jnp.bfloat16)
    turned = turned.transpose(0, 3, 2, 1, 4).reshape(2 * inner, count, outer, lanes)
    return split_product("ab,bskc->askc", inner_table(inner, 1.0), turned, exact=False)


def fft_inverse(spectrum, length):
    twice, count, outer, lanes = spectrum.shape
    inner = twice // 2
    size = outer * inner
    half = outer // 2
    stage = split_product("ab,bskc->askc", inner_table(inner, -1.0), spectrum, exact=False)
    real_part, imag_part = stage[:inner], stage[inner:]
    cosine, sine = twiddles(outer, inner, size)
    cosine, sine = cosine.transpose(2, 0, 1, 3), sine.transpose(2, 0, 1, 3)
    turned = jnp.stack(
        [real_part * cosine - imag_part * sine, imag_part * cosine + real_part * sine]
    ).astype(jnp.bfloat16)
    turned = turned.transpose(0, 3, 2, 1, 4).reshape(2 * outer, count, inner, lanes)
    phase = 2.0 * np.pi * np.outer(np.arange(half), np.arange(outer)) / outer
    last = np.concatenate([np.cos(phase), -np.sin(phase)], 1) / size
    result = split_product("nk,ksqb->nsqb", last, turned, exact=False)
    return result.transpose(1, 0, 2, 3).reshape(count, length, lanes)


def spectral_products(spectra):
    inner = spectra.shape[0] // 2
    parts = [(spectra[:inner, i], spectra[inner:, i]) for i in range(3)]
    (f_re, f_im), (m_re, m_im), (g_re, g_im) = parts
    conv = jnp.concatenate([m_re * f_re - m_im * f_im, m_re * f_im + m_im * f_re], 0)
    back = jnp.concatenate([g_re * f_re + g_im * f_im, g_im * f_re - g_re * f_im], 0)
    cross = jnp.concatenate([g_re * m_re + g_im * m_im, g_im * m_re - g_re * m_im], 0)
    return jnp.stack([conv, back, cross], 1)


def all_sum(data, axis):
    size = lax.axis_size(axis)
    total = data
    for step in range(1, size):
        total = total + lax.ppermute(data, axis, [(i, (i + step) % size) for i in range(size)])
    return total


def mesh_sum(data, axes):
    count = 1
    for axis in axes:
        count *= lax.axis_size(axis)
    rows, chans = data.shape
    pieces = data.reshape(rows, count, chans // count).transpose(1, 0, 2)
    mine = jnp.sum(lax.all_to_all(pieces, axes, 0, 0, tiled=True), axis=0)
    spread = jnp.broadcast_to(mine[None], (count,) + mine.shape)
    gathered = lax.all_to_all(spread, axes, 0, 0, tiled=True)
    return gathered.transpose(1, 0, 2).reshape(rows, chans)


def halving_rows(data, axis):
    size = lax.axis_size(axis)
    index = lax.axis_index(axis)
    blocks = data.reshape(size, data.shape[0] // size, data.shape[1])
    step = size // 2
    while step >= 1:
        half = blocks.shape[0] // 2
        upper = (index // step) % 2 == 1
        keep = jnp.where(upper, blocks[half:], blocks[:half])
        give = jnp.where(upper, blocks[:half], blocks[half:])
        blocks = keep + lax.ppermute(give, axis, [(i, i ^ step) for i in range(size)])
        step //= 2
    return blocks.reshape(-1, data.shape[1])


def route_filter_grad(block, rows):
    parts = lax.axis_size("ctx")
    groups = lax.axis_size("dp")
    ratio = parts // groups
    pieces = block.reshape(ratio, rows, block.shape[1])
    columns = []
    for lane_block in range(ratio):
        total = None
        for piece in range(ratio):
            pairs = [
                (sd * parts + sc, (sc // ratio) * parts + sd * ratio + piece)
                for sd in range(groups)
                for sc in range(lane_block, parts, ratio)
            ]
            got = lax.ppermute(pieces[piece], ("dp", "ctx"), pairs)
            total = got if total is None else total + got
        columns.append(total)
    return jnp.concatenate(columns, 1)


def halving_scatter(data, axis):
    size = lax.axis_size(axis)
    index = lax.axis_index(axis)
    rows, chans = data.shape
    blocks = data.reshape(rows, size, chans // size)
    step = size // 2
    while step >= 1:
        half = blocks.shape[1] // 2
        upper = (index // step) % 2 == 1
        keep = jnp.where(upper, blocks[:, half:], blocks[:, :half])
        give = jnp.where(upper, blocks[:, :half], blocks[:, half:])
        blocks = keep + lax.ppermute(give, axis, [(i, i ^ step) for i in range(size)])
        step //= 2
    return blocks.reshape(rows, chans // size)


def epilogue_kernel(conv_ref, back_ref, src_ref, up_ref, mask_ref, w_ref, skip_ref, out_ref, stats_ref):
    wide, narrow = jnp.float32, jnp.bfloat16
    taps = w_ref.shape[1]
    head = taps - 1
    frame = src_ref.shape[1]
    rows = out_ref.shape[1]

    def mask(i):
        return mask_ref[i] > 0.5

    def down(x, by):
        return pltpu.roll(x, by, 0) if by else x

    def lift(x, by):
        return pltpu.roll(x, frame - by, 0) if by else x

    sources = [src_ref[i].astype(wide) for i in range(3)]
    weights = w_ref[...]
    shorts = []
    for i in range(3):
        total = weights[i, 0:1] * sources[i]
        for off in range(1, taps):
            total = total + jnp.where(mask(off), weights[i, off : off + 1] * down(sources[i], off), 0.0)
        shorts.append(total.astype(narrow).astype(wide))
    q_short, k_short, v_short = shorts
    upstream = up_ref[...].astype(wide)
    skip = skip_ref[...]
    mixed = (k_short * v_short).astype(narrow).astype(wide)
    grad_conv = (upstream * q_short).astype(narrow).astype(wide)
    conv = conv_ref[...].astype(wide) + skip * mixed
    grad_mixed = back_ref[...].astype(wide) + skip * grad_conv
    own = mask(2 * taps)
    out_ref[0] = lift(q_short * conv, head)[:rows].astype(narrow)
    grads = [upstream * conv, grad_mixed * v_short, grad_mixed * k_short]
    stats = []
    for i in range(3):
        grad = grads[i]
        acc = weights[i, 0:1] * grad
        stats.append(jnp.sum(jnp.where(own, sources[i] * grad, 0.0), axis=0, keepdims=True))
        for off in range(1, taps):
            later = lift(jnp.where(mask(taps + off), grad, 0.0), off)
            acc = acc + weights[i, off : off + 1] * later
            lagged = jnp.where(own & mask(off), down(sources[i], off) * grad, 0.0)
            stats.append(jnp.sum(lagged, axis=0, keepdims=True))
        out_ref[1 + i] = lift(acc, head)[:rows].astype(narrow)
    stats.append(jnp.sum(jnp.where(own, grad_conv * mixed, 0.0), axis=0, keepdims=True))
    width = stats[0].shape[1]
    stats.append(jnp.zeros((stats_ref.shape[0] - len(stats), width), wide))
    stats_ref[...] = jnp.concatenate(stats, 0)


def epilogue(back, sources, upstream, masks, short_weights, skip, rows):
    _, frame, chans = back.shape
    taps = short_weights.shape[1]
    block = 256 if chans % 256 == 0 else chans
    grid = (chans // block,)
    stat_rows = 16
    return pl.pallas_call(
        epilogue_kernel,
        grid=grid,
        in_specs=[
            pl.BlockSpec((None, frame, block), lambda c: (0, 0, c)),
            pl.BlockSpec((None, frame, block), lambda c: (1, 0, c)),
            pl.BlockSpec((3, frame, block), lambda c: (0, 0, c)),
            pl.BlockSpec((frame, block), lambda c: (0, c)),
            pl.BlockSpec(masks.shape, lambda c: (0, 0, 0)),
            pl.BlockSpec((3, taps, block), lambda c: (0, 0, c)),
            pl.BlockSpec((1, block), lambda c: (0, c)),
        ],
        out_specs=[
            pl.BlockSpec((4, rows, block), lambda c: (0, 0, c)),
            pl.BlockSpec((stat_rows, block), lambda c: (0, c)),
        ],
        out_shape=[
            jax.ShapeDtypeStruct((4, rows, chans), jnp.bfloat16),
            jax.ShapeDtypeStruct((stat_rows, chans), jnp.float32),
        ],
    )(back, back, sources, upstream, masks, short_weights, skip[None])


def local(query, keys, values, cotangent, long_filter, short_weights, skip, lengths):
    parts = lax.axis_size("ctx")
    index = lax.axis_index("ctx")
    groups = lax.axis_size("dp")
    q_rows, k_rows, v_rows, c_rows = query[0], keys[0], values[0], cotangent[0]
    rows, chans = q_rows.shape
    taps = short_weights.shape[1]
    head = taps - 1
    seq_len = rows * parts
    lanes = chans // parts
    ext = rows + head
    frame = -(-(rows + 2 * head) // 8) * 8
    doc_len = lengths[0]
    starts = jnp.cumsum(doc_len) - doc_len

    position = index * rows + jnp.arange(ext, dtype=jnp.int32)
    begin = jnp.max(jnp.where(starts[None, :] <= position[:, None], starts[None, :], 0), axis=1)
    valid = position[None, :] - jnp.arange(taps, dtype=jnp.int32)[:, None] >= begin[None, :]
    valid_after = valid & (position < seq_len)[None, :]

    prev = shifted(jnp.stack([a[rows - head :] for a in (q_rows, k_rows, v_rows)]), "ctx", 1)
    nxt = shifted(jnp.stack([a[:head] for a in (q_rows, k_rows, v_rows, c_rows)]), "ctx", -1)
    padded = [
        jnp.concatenate([prev[i], src, nxt[i]], 0).astype(jnp.float32)
        for i, src in enumerate((q_rows, k_rows, v_rows))
    ]

    def short_forward(wide, weights):
        summed = weights[0] * wide[head : head + ext]
        for offset in range(1, taps):
            begin_at = head - offset
            summed = summed + jnp.where(
                valid[offset][:, None], weights[offset] * wide[begin_at : begin_at + ext], 0.0
            )
        return summed.astype(jnp.bfloat16).astype(jnp.float32)

    q_short = short_forward(padded[0], short_weights[0])
    k_short = short_forward(padded[1], short_weights[1])
    v_short = short_forward(padded[2], short_weights[2])
    upstream = jnp.concatenate([c_rows, nxt[3]], 0).astype(jnp.float32)
    mixed = (k_short * v_short).astype(jnp.bfloat16)
    grad_conv = (upstream * q_short).astype(jnp.bfloat16)
    mixed_wide = mixed.astype(jnp.float32)
    grad_wide = grad_conv.astype(jnp.float32)

    chunks = 2 if lanes % 2 == 0 else 1
    width = lanes // chunks

    def to_columns(data, part):
        count = data.shape[0]
        split = data.reshape(count, rows, parts, chunks, width)[:, :, :, part]
        moved = lax.all_to_all(split.transpose(0, 2, 1, 3), "ctx", 1, 1, tiled=True)
        return moved.reshape(count, seq_len, width)

    sent = jnp.stack([long_filter, mixed[:rows], grad_conv[:rows]])
    returned = []
    lagged_parts = []
    previous = None
    for part in range(chunks):
        columns = to_columns(sent, part)
        if previous is not None:
            columns, previous = lax.optimization_barrier((columns, previous))
            returned.append(lax.all_to_all(previous, "ctx", 1, 1, tiled=True))
        spectra = fft_forward(columns)
        raw = fft_inverse(spectral_products(spectra), seq_len)
        lagged_parts.append(raw[2])
        raw = raw[:2].astype(jnp.bfloat16)
        raw = jnp.concatenate(
            [jnp.zeros((2, head, width), raw.dtype), raw, jnp.zeros((2, frame - rows - head, width), raw.dtype)], 1
        )
        blocks = jnp.stack([raw[:, j * rows : j * rows + frame] for j in range(parts)], 1)
        previous = blocks
    returned.append(lax.all_to_all(previous, "ctx", 1, 1, tiled=True))
    back = jnp.stack(returned, 3).transpose(0, 2, 1, 3, 4).reshape(2, frame, chans)
    lagged, back = lax.optimization_barrier((jnp.concatenate(lagged_parts, 1), back))
    lagged = halving_rows(lagged, "dp")
    filter_part = route_filter_grad(lagged, rows)

    spot = index * rows - head + jnp.arange(frame, dtype=jnp.int32)
    spot_begin = jnp.max(jnp.where(starts[None, :] <= spot[:, None], starts[None, :], 0), axis=1)
    spot_valid = spot[None, :] - jnp.arange(taps, dtype=jnp.int32)[:, None] >= spot_begin[None, :]
    spot_after = spot_valid & ((spot >= 0) & (spot < seq_len))[None, :]
    spot_own = ((spot >= index * rows) & (spot < index * rows + rows))[None, :]
    masks = jnp.concatenate([spot_valid, spot_after, spot_own], 0).astype(jnp.float32)
    masks = jnp.concatenate([masks, jnp.zeros(((-masks.shape[0]) % 8, frame), jnp.float32)], 0)
    tail = frame - rows - 2 * head
    sources = jnp.stack([
        jnp.concatenate([prev[i], src, nxt[i], jnp.zeros((tail, chans), src.dtype)], 0)
        for i, src in enumerate((q_rows, k_rows, v_rows))
    ])
    framed_up = jnp.concatenate(
        [jnp.zeros((head, chans), c_rows.dtype), c_rows, nxt[3], jnp.zeros((tail, chans), c_rows.dtype)], 0
    )
    outs, stats = epilogue(back, sources, framed_up, masks[:, :, None], short_weights, skip, rows)
    summed = mesh_sum(stats[: 3 * taps + 1], ("dp", "ctx"))
    gated, grad_q, grad_k, grad_v = outs[0], outs[1], outs[2], outs[3]
    scale = 1.0 / (groups * seq_len)
    return (
        gated[None],
        grad_q.astype(jnp.bfloat16)[None],
        grad_k.astype(jnp.bfloat16)[None],
        grad_v.astype(jnp.bfloat16)[None],
        filter_part * scale,
        summed[: 3 * taps].reshape(3, taps, chans) * scale,
        summed[3 * taps] * scale,
    )


def solution(mesh):
    in_specs = (
        P("dp", "ctx", None),
        P("dp", "ctx", None),
        P("dp", "ctx", None),
        P("dp", "ctx", None),
        P("ctx", None),
        P(),
        P(),
        P("dp", None),
    )
    out_specs = (
        P("dp", "ctx", None),
        P("dp", "ctx", None),
        P("dp", "ctx", None),
        P("dp", "ctx", None),
        P("ctx", "dp"),
        P(),
        P(),
    )
    return jax.shard_map(local, mesh=mesh, in_specs=in_specs, out_specs=out_specs, check_vma=False)
```

```python
import math

import jax
import jax.numpy as jnp
import ml_dtypes
import numpy as np
from jax import lax
from jax.experimental import pallas as pl
from jax.experimental.pallas import tpu as pltpu
from jax.sharding import PartitionSpec as P


def shifted(x, axis, by):
    length = lax.axis_size(axis)
    pairs = [(i, i + by) for i in range(length) if 0 <= i + by < length]
    return lax.ppermute(x, axis, pairs)


def table_halves(table):
    upper = table.astype(ml_dtypes.bfloat16)
    lower = (table - upper.astype(np.float64)).astype(ml_dtypes.bfloat16)
    return jnp.asarray(upper), jnp.asarray(lower)


def split_product(form, table, data, exact=True):
    upper, lower = table_halves(table)
    wide = jnp.float32
    if not exact:
        return jnp.einsum(form, upper, data.astype(jnp.bfloat16), preferred_element_type=wide)
    if data.dtype == jnp.bfloat16:
        total = jnp.einsum(form, upper, data, preferred_element_type=wide)
        return total + jnp.einsum(form, lower, data, preferred_element_type=wide)
    data_upper = lax.optimization_barrier(data.astype(jnp.bfloat16))
    data_lower = (data - data_upper.astype(wide)).astype(jnp.bfloat16)
    total = jnp.einsum(form, upper, data_upper, preferred_element_type=wide)
    total = total + jnp.einsum(form, lower, data_upper, preferred_element_type=wide)
    return total + jnp.einsum(form, upper, data_lower, preferred_element_type=wide)


def batched_product(table, data):
    count, outer, twice, lanes = data.shape
    upper = jnp.asarray(table.astype(ml_dtypes.bfloat16))
    upper = jnp.broadcast_to(upper, (count, outer, twice, twice))
    return jnp.einsum(
        "skab,skbc->skac", upper, data.astype(jnp.bfloat16), preferred_element_type=jnp.float32
    )


def factors(size):
    bits = size.bit_length() - 1
    inner = 1 << (bits // 2)
    return size // inner, inner


def twiddles(outer, inner, size):
    phase = 2.0 * np.pi * np.outer(np.arange(outer), np.arange(inner)) / size
    cosine = jnp.asarray(np.cos(phase), jnp.float32)[None, :, :, None]
    sine = jnp.asarray(np.sin(phase), jnp.float32)[None, :, :, None]
    return cosine, sine


def inner_table(inner, sign):
    phase = 2.0 * np.pi * np.outer(np.arange(inner), np.arange(inner)) / inner
    cosine, sine = np.cos(phase), sign * np.sin(phase)
    return np.block([[cosine, sine], [-sine, cosine]])


def fft_forward(signal):
    count, length, lanes = signal.shape
    size = 2 * length
    outer, inner = factors(size)
    half = outer // 2
    phase = 2.0 * np.pi * np.outer(np.arange(outer), np.arange(half)) / outer
    first = np.concatenate([np.cos(phase), -np.sin(phase)], 0)
    blocks = signal.reshape(count, half, inner, lanes).transpose(1, 0, 2, 3)
    stage = split_product("kn,nsqb->ksqb", first, blocks, exact=False)
    real_part, imag_part = stage[:outer], stage[outer:]
    cosine, sine = twiddles(outer, inner, size)
    cosine, sine = cosine.transpose(1, 0, 2, 3), sine.transpose(1, 0, 2, 3)
    turned = jnp.stack(
        [real_part * cosine + imag_part * sine, imag_part * cosine - real_part * sine]
    ).astype(jnp.bfloat16)
    turned = turned.transpose(0, 3, 2, 1, 4).reshape(2 * inner, count, outer, lanes)
    return split_product("ab,bskc->askc", inner_table(inner, 1.0), turned, exact=False)


def fft_inverse(spectrum, length):
    twice, count, outer, lanes = spectrum.shape
    inner = twice // 2
    size = outer * inner
    half = outer // 2
    stage = split_product("ab,bskc->askc", inner_table(inner, -1.0), spectrum, exact=False)
    real_part, imag_part = stage[:inner], stage[inner:]
    cosine, sine = twiddles(outer, inner, size)
    cosine, sine = cosine.transpose(2, 0, 1, 3), sine.transpose(2, 0, 1, 3)
    turned = jnp.stack(
        [real_part * cosine - imag_part * sine, imag_part * cosine + real_part * sine]
    ).astype(jnp.bfloat16)
    turned = turned.transpose(0, 3, 2, 1, 4).reshape(2 * outer, count, inner, lanes)
    phase = 2.0 * np.pi * np.outer(np.arange(half), np.arange(outer)) / outer
    last = np.concatenate([np.cos(phase), -np.sin(phase)], 1) / size
    result = split_product("nk,ksqb->nsqb", last, turned, exact=False)
    return result.transpose(1, 0, 2, 3).reshape(count, length, lanes)


def spectral_products(spectra):
    inner = spectra.shape[0] // 2
    parts = [(spectra[:inner, i], spectra[inner:, i]) for i in range(3)]
    (f_re, f_im), (m_re, m_im), (g_re, g_im) = parts
    conv = jnp.concatenate([m_re * f_re - m_im * f_im, m_re * f_im + m_im * f_re], 0)
    back = jnp.concatenate([g_re * f_re + g_im * f_im, g_im * f_re - g_re * f_im], 0)
    cross = jnp.concatenate([g_re * m_re + g_im * m_im, g_im * m_re - g_re * m_im], 0)
    return jnp.stack([conv, back, cross], 1)


def all_sum(data, axis):
    size = lax.axis_size(axis)
    total = data
    for step in range(1, size):
        total = total + lax.ppermute(data, axis, [(i, (i + step) % size) for i in range(size)])
    return total


def mesh_sum(data, axes):
    count = 1
    for axis in axes:
        count *= lax.axis_size(axis)
    rows, chans = data.shape
    pieces = data.reshape(rows, count, chans // count).transpose(1, 0, 2)
    mine = jnp.sum(lax.all_to_all(pieces, axes, 0, 0, tiled=True), axis=0)
    spread = jnp.broadcast_to(mine[None], (count,) + mine.shape)
    gathered = lax.all_to_all(spread, axes, 0, 0, tiled=True)
    return gathered.transpose(1, 0, 2).reshape(rows, chans)


def halving_rows(data, axis):
    size = lax.axis_size(axis)
    index = lax.axis_index(axis)
    blocks = data.reshape(size, data.shape[0] // size, data.shape[1])
    step = size // 2
    while step >= 1:
        half = blocks.shape[0] // 2
        upper = (index // step) % 2 == 1
        keep = jnp.where(upper, blocks[half:], blocks[:half])
        give = jnp.where(upper, blocks[:half], blocks[half:])
        blocks = keep + lax.ppermute(give, axis, [(i, i ^ step) for i in range(size)])
        step //= 2
    return blocks.reshape(-1, data.shape[1])


def route_filter_grad(block, rows):
    parts = lax.axis_size("ctx")
    groups = lax.axis_size("dp")
    ratio = parts // groups
    pieces = block.reshape(ratio, rows, block.shape[1])
    columns = []
    for lane_block in range(ratio):
        total = None
        for piece in range(ratio):
            pairs = [
                (sd * parts + sc, (sc // ratio) * parts + sd * ratio + piece)
                for sd in range(groups)
                for sc in range(lane_block, parts, ratio)
            ]
            got = lax.ppermute(pieces[piece], ("dp", "ctx"), pairs)
            total = got if total is None else total + got
        columns.append(total)
    return jnp.concatenate(columns, 1)


def halving_scatter(data, axis):
    size = lax.axis_size(axis)
    index = lax.axis_index(axis)
    rows, chans = data.shape
    blocks = data.reshape(rows, size, chans // size)
    step = size // 2
    while step >= 1:
        half = blocks.shape[1] // 2
        upper = (index // step) % 2 == 1
        keep = jnp.where(upper, blocks[:, half:], blocks[:, :half])
        give = jnp.where(upper, blocks[:, :half], blocks[:, half:])
        blocks = keep + lax.ppermute(give, axis, [(i, i ^ step) for i in range(size)])
        step //= 2
    return blocks.reshape(rows, chans // size)


def epilogue_kernel(conv_ref, back_ref, src_ref, up_ref, mask_ref, w_ref, skip_ref, out_ref, stats_ref):
    wide, narrow = jnp.float32, jnp.bfloat16
    taps = w_ref.shape[1]
    head = taps - 1
    frame = src_ref.shape[1]
    rows = out_ref.shape[1]

    def mask(i):
        return mask_ref[i] > 0.5

    def down(x, by):
        return pltpu.roll(x, by, 0) if by else x

    def lift(x, by):
        return pltpu.roll(x, frame - by, 0) if by else x

    sources = [src_ref[i].astype(wide) for i in range(3)]
    weights = w_ref[...]
    shorts = []
    for i in range(3):
        total = weights[i, 0:1] * sources[i]
        for off in range(1, taps):
            total = total + jnp.where(mask(off), weights[i, off : off + 1] * down(sources[i], off), 0.0)
        shorts.append(total.astype(narrow).astype(wide))
    q_short, k_short, v_short = shorts
    upstream = up_ref[...].astype(wide)
    skip = skip_ref[...]
    mixed = (k_short * v_short).astype(narrow).astype(wide)
    grad_conv = (upstream * q_short).astype(narrow).astype(wide)
    conv = conv_ref[...].astype(wide) + skip * mixed
    grad_mixed = back_ref[...].astype(wide) + skip * grad_conv
    own = mask(2 * taps)
    out_ref[0] = lift(q_short * conv, head)[:rows].astype(narrow)
    grads = [upstream * conv, grad_mixed * v_short, grad_mixed * k_short]
    stats = []
    for i in range(3):
        grad = grads[i]
        acc = weights[i, 0:1] * grad
        stats.append(jnp.sum(jnp.where(own, sources[i] * grad, 0.0), axis=0, keepdims=True))
        for off in range(1, taps):
            later = lift(jnp.where(mask(taps + off), grad, 0.0), off)
            acc = acc + weights[i, off : off + 1] * later
            lagged = jnp.where(own & mask(off), down(sources[i], off) * grad, 0.0)
            stats.append(jnp.sum(lagged, axis=0, keepdims=True))
        out_ref[1 + i] = lift(acc, head)[:rows].astype(narrow)
    stats.append(jnp.sum(jnp.where(own, grad_conv * mixed, 0.0), axis=0, keepdims=True))
    width = stats[0].shape[1]
    stats.append(jnp.zeros((stats_ref.shape[0] - len(stats), width), wide))
    stats_ref[...] = jnp.concatenate(stats, 0)


def epilogue(back, sources, upstream, masks, short_weights, skip, rows):
    _, frame, chans = back.shape
    taps = short_weights.shape[1]
    block = 256 if chans % 256 == 0 else chans
    grid = (chans // block,)
    stat_rows = 16
    return pl.pallas_call(
        epilogue_kernel,
        grid=grid,
        in_specs=[
            pl.BlockSpec((None, frame, block), lambda c: (0, 0, c)),
            pl.BlockSpec((None, frame, block), lambda c: (1, 0, c)),
            pl.BlockSpec((3, frame, block), lambda c: (0, 0, c)),
            pl.BlockSpec((frame, block), lambda c: (0, c)),
            pl.BlockSpec(masks.shape, lambda c: (0, 0, 0)),
            pl.BlockSpec((3, taps, block), lambda c: (0, 0, c)),
            pl.BlockSpec((1, block), lambda c: (0, c)),
        ],
        out_specs=[
            pl.BlockSpec((4, rows, block), lambda c: (0, 0, c)),
            pl.BlockSpec((stat_rows, block), lambda c: (0, c)),
        ],
        out_shape=[
            jax.ShapeDtypeStruct((4, rows, chans), jnp.bfloat16),
            jax.ShapeDtypeStruct((stat_rows, chans), jnp.float32),
        ],
    )(back, back, sources, upstream, masks, short_weights, skip[None])


def local(query, keys, values, cotangent, long_filter, short_weights, skip, lengths):
    parts = lax.axis_size("ctx")
    index = lax.axis_index("ctx")
    groups = lax.axis_size("dp")
    q_rows, k_rows, v_rows, c_rows = query[0], keys[0], values[0], cotangent[0]
    rows, chans = q_rows.shape
    taps = short_weights.shape[1]
    head = taps - 1
    seq_len = rows * parts
    lanes = chans // parts
    ext = rows + head
    frame = -(-(rows + 2 * head) // 8) * 8
    doc_len = lengths[0]
    starts = jnp.cumsum(doc_len) - doc_len

    position = index * rows + jnp.arange(ext, dtype=jnp.int32)
    begin = jnp.max(jnp.where(starts[None, :] <= position[:, None], starts[None, :], 0), axis=1)
    valid = position[None, :] - jnp.arange(taps, dtype=jnp.int32)[:, None] >= begin[None, :]
    valid_after = valid & (position < seq_len)[None, :]

    prev = shifted(jnp.stack([a[rows - head :] for a in (q_rows, k_rows, v_rows)]), "ctx", 1)
    nxt = shifted(jnp.stack([a[:head] for a in (q_rows, k_rows, v_rows, c_rows)]), "ctx", -1)
    padded = [
        jnp.concatenate([prev[i], src, nxt[i]], 0).astype(jnp.float32)
        for i, src in enumerate((q_rows, k_rows, v_rows))
    ]

    def short_forward(wide, weights):
        summed = weights[0] * wide[head : head + ext]
        for offset in range(1, taps):
            begin_at = head - offset
            summed = summed + jnp.where(
                valid[offset][:, None], weights[offset] * wide[begin_at : begin_at + ext], 0.0
            )
        return summed.astype(jnp.bfloat16).astype(jnp.float32)

    q_short = short_forward(padded[0], short_weights[0])
    k_short = short_forward(padded[1], short_weights[1])
    v_short = short_forward(padded[2], short_weights[2])
    upstream = jnp.concatenate([c_rows, nxt[3]], 0).astype(jnp.float32)
    mixed = (k_short * v_short).astype(jnp.bfloat16)
    grad_conv = (upstream * q_short).astype(jnp.bfloat16)
    mixed_wide = mixed.astype(jnp.float32)
    grad_wide = grad_conv.astype(jnp.float32)

    chunks = 2 if lanes % 2 == 0 else 1
    width = lanes // chunks

    def to_columns(data, part):
        count = data.shape[0]
        split = data.reshape(count, rows, parts, chunks, width)[:, :, :, part]
        moved = lax.all_to_all(split.transpose(0, 2, 1, 3), "ctx", 1, 1, tiled=True)
        return moved.reshape(count, seq_len, width)

    sent = jnp.stack([long_filter, mixed[:rows], grad_conv[:rows]])
    returned = []
    lagged_parts = []
    previous = None
    for part in range(chunks):
        columns = to_columns(sent, part)
        if previous is not None:
            columns, previous = lax.optimization_barrier((columns, previous))
            returned.append(lax.all_to_all(previous, "ctx", 1, 1, tiled=True))
        spectra = fft_forward(columns)
        raw = fft_inverse(spectral_products(spectra), seq_len)
        lagged_parts.append(raw[2])
        raw = raw[:2].astype(jnp.bfloat16)
        raw = jnp.concatenate(
            [jnp.zeros((2, head, width), raw.dtype), raw, jnp.zeros((2, frame - rows - head, width), raw.dtype)], 1
        )
        blocks = jnp.stack([raw[:, j * rows : j * rows + frame] for j in range(parts)], 1)
        previous = blocks
    returned.append(lax.all_to_all(previous, "ctx", 1, 1, tiled=True))
    back = jnp.stack(returned, 3).transpose(0, 2, 1, 3, 4).reshape(2, frame, chans)
    lagged = halving_rows(jnp.concatenate(lagged_parts, 1), "dp")
    filter_part = route_filter_grad(lagged, rows)

    spot = index * rows - head + jnp.arange(frame, dtype=jnp.int32)
    spot_begin = jnp.max(jnp.where(starts[None, :] <= spot[:, None], starts[None, :], 0), axis=1)
    spot_valid = spot[None, :] - jnp.arange(taps, dtype=jnp.int32)[:, None] >= spot_begin[None, :]
    spot_after = spot_valid & ((spot >= 0) & (spot < seq_len))[None, :]
    spot_own = ((spot >= index * rows) & (spot < index * rows + rows))[None, :]
    masks = jnp.concatenate([spot_valid, spot_after, spot_own], 0).astype(jnp.float32)
    masks = jnp.concatenate([masks, jnp.zeros(((-masks.shape[0]) % 8, frame), jnp.float32)], 0)
    tail = frame - rows - 2 * head
    sources = jnp.stack([
        jnp.concatenate([prev[i], src, nxt[i], jnp.zeros((tail, chans), src.dtype)], 0)
        for i, src in enumerate((q_rows, k_rows, v_rows))
    ])
    framed_up = jnp.concatenate(
        [jnp.zeros((head, chans), c_rows.dtype), c_rows, nxt[3], jnp.zeros((tail, chans), c_rows.dtype)], 0
    )
    outs, stats = epilogue(back, sources, framed_up, masks[:, :, None], short_weights, skip, rows)
    summed = mesh_sum(stats[: 3 * taps + 1], ("dp", "ctx"))
    gated, grad_q, grad_k, grad_v = outs[0], outs[1], outs[2], outs[3]
    scale = 1.0 / (groups * seq_len)
    return (
        gated[None],
        grad_q.astype(jnp.bfloat16)[None],
        grad_k.astype(jnp.bfloat16)[None],
        grad_v.astype(jnp.bfloat16)[None],
        filter_part * scale,
        summed[: 3 * taps].reshape(3, taps, chans) * scale,
        summed[3 * taps] * scale,
    )


def solution(mesh):
    in_specs = (
        P("dp", "ctx", None),
        P("dp", "ctx", None),
        P("dp", "ctx", None),
        P("dp", "ctx", None),
        P("ctx", None),
        P(),
        P(),
        P("dp", None),
    )
    out_specs = (
        P("dp", "ctx", None),
        P("dp", "ctx", None),
        P("dp", "ctx", None),
        P("dp", "ctx", None),
        P("ctx", "dp"),
        P(),
        P(),
    )
    return jax.shard_map(local, mesh=mesh, in_specs=in_specs, out_specs=out_specs, check_vma=False)
```

```python
import math

import jax
import jax.numpy as jnp
import ml_dtypes
import numpy as np
from jax import lax
from jax.experimental import pallas as pl
from jax.experimental.pallas import tpu as pltpu
from jax.sharding import PartitionSpec as P


def shifted(x, axis, by):
    length = lax.axis_size(axis)
    pairs = [(i, i + by) for i in range(length) if 0 <= i + by < length]
    return lax.ppermute(x, axis, pairs)


def table_halves(table):
    upper = table.astype(ml_dtypes.bfloat16)
    lower = (table - upper.astype(np.float64)).astype(ml_dtypes.bfloat16)
    return jnp.asarray(upper), jnp.asarray(lower)


def split_product(form, table, data, exact=True):
    upper, lower = table_halves(table)
    wide = jnp.float32
    if not exact:
        return jnp.einsum(form, upper, data.astype(jnp.bfloat16), preferred_element_type=wide)
    if data.dtype == jnp.bfloat16:
        total = jnp.einsum(form, upper, data, preferred_element_type=wide)
        return total + jnp.einsum(form, lower, data, preferred_element_type=wide)
    data_upper = lax.optimization_barrier(data.astype(jnp.bfloat16))
    data_lower = (data - data_upper.astype(wide)).astype(jnp.bfloat16)
    total = jnp.einsum(form, upper, data_upper, preferred_element_type=wide)
    total = total + jnp.einsum(form, lower, data_upper, preferred_element_type=wide)
    return total + jnp.einsum(form, upper, data_lower, preferred_element_type=wide)


def batched_product(table, data):
    count, outer, twice, lanes = data.shape
    upper = jnp.asarray(table.astype(ml_dtypes.bfloat16))
    upper = jnp.broadcast_to(upper, (count, outer, twice, twice))
    return jnp.einsum(
        "skab,skbc->skac", upper, data.astype(jnp.bfloat16), preferred_element_type=jnp.float32
    )


def factors(size):
    bits = size.bit_length() - 1
    inner = 1 << (bits // 2)
    return size // inner, inner


def twiddles(outer, inner, size):
    phase = 2.0 * np.pi * np.outer(np.arange(outer), np.arange(inner)) / size
    cosine = jnp.asarray(np.cos(phase), jnp.float32)[None, :, :, None]
    sine = jnp.asarray(np.sin(phase), jnp.float32)[None, :, :, None]
    return cosine, sine


def inner_table(inner, sign):
    phase = 2.0 * np.pi * np.outer(np.arange(inner), np.arange(inner)) / inner
    cosine, sine = np.cos(phase), sign * np.sin(phase)
    return np.block([[cosine, sine], [-sine, cosine]])


def fft_forward(signal):
    count, length, lanes = signal.shape
    size = 2 * length
    outer, inner = factors(size)
    half = outer // 2
    phase = 2.0 * np.pi * np.outer(np.arange(outer), np.arange(half)) / outer
    first = np.concatenate([np.cos(phase), -np.sin(phase)], 0)
    blocks = signal.reshape(count, half, inner, lanes).transpose(1, 0, 2, 3)
    stage = split_product("kn,nsqb->ksqb", first, blocks, exact=False)
    real_part, imag_part = stage[:outer], stage[outer:]
    cosine, sine = twiddles(outer, inner, size)
    cosine, sine = cosine.transpose(1, 0, 2, 3), sine.transpose(1, 0, 2, 3)
    turned = jnp.stack(
        [real_part * cosine + imag_part * sine, imag_part * cosine - real_part * sine]
    ).astype(jnp.bfloat16)
    turned = turned.transpose(0, 3, 2, 1, 4).reshape(2 * inner, count, outer, lanes)
    return split_product("ab,bskc->askc", inner_table(inner, 1.0), turned, exact=False)


def fft_inverse(spectrum, length):
    twice, count, outer, lanes = spectrum.shape
    inner = twice // 2
    size = outer * inner
    half = outer // 2
    stage = split_product("ab,bskc->askc", inner_table(inner, -1.0), spectrum, exact=False)
    real_part, imag_part = stage[:inner], stage[inner:]
    cosine, sine = twiddles(outer, inner, size)
    cosine, sine = cosine.transpose(2, 0, 1, 3), sine.transpose(2, 0, 1, 3)
    turned = jnp.stack(
        [real_part * cosine - imag_part * sine, imag_part * cosine + real_part * sine]
    ).astype(jnp.bfloat16)
    turned = turned.transpose(0, 3, 2, 1, 4).reshape(2 * outer, count, inner, lanes)
    phase = 2.0 * np.pi * np.outer(np.arange(half), np.arange(outer)) / outer
    last = np.concatenate([np.cos(phase), -np.sin(phase)], 1) / size
    result = split_product("nk,ksqb->nsqb", last, turned, exact=False)
    return result.transpose(1, 0, 2, 3).reshape(count, length, lanes)


def spectral_products(spectra):
    inner = spectra.shape[0] // 2
    parts = [(spectra[:inner, i], spectra[inner:, i]) for i in range(3)]
    (f_re, f_im), (m_re, m_im), (g_re, g_im) = parts
    conv = jnp.concatenate([m_re * f_re - m_im * f_im, m_re * f_im + m_im * f_re], 0)
    back = jnp.concatenate([g_re * f_re + g_im * f_im, g_im * f_re - g_re * f_im], 0)
    cross = jnp.concatenate([g_re * m_re + g_im * m_im, g_im * m_re - g_re * m_im], 0)
    return jnp.stack([conv, back, cross], 1)


def all_sum(data, axis):
    size = lax.axis_size(axis)
    total = data
    for step in range(1, size):
        total = total + lax.ppermute(data, axis, [(i, (i + step) % size) for i in range(size)])
    return total


def mesh_sum(data, axes):
    count = 1
    for axis in axes:
        count *= lax.axis_size(axis)
    rows, chans = data.shape
    pieces = data.reshape(rows, count, chans // count).transpose(1, 0, 2)
    mine = jnp.sum(lax.all_to_all(pieces, axes, 0, 0, tiled=True), axis=0)
    spread = jnp.broadcast_to(mine[None], (count,) + mine.shape)
    gathered = lax.all_to_all(spread, axes, 0, 0, tiled=True)
    return gathered.transpose(1, 0, 2).reshape(rows, chans)


def halving_rows(data, axis):
    size = lax.axis_size(axis)
    index = lax.axis_index(axis)
    blocks = data.reshape(size, data.shape[0] // size, data.shape[1])
    step = size // 2
    while step >= 1:
        half = blocks.shape[0] // 2
        upper = (index // step) % 2 == 1
        keep = jnp.where(upper, blocks[half:], blocks[:half])
        give = jnp.where(upper, blocks[:half], blocks[half:])
        blocks = keep + lax.ppermute(give, axis, [(i, i ^ step) for i in range(size)])
        step //= 2
    return blocks.reshape(-1, data.shape[1])


def route_filter_grad(block, rows):
    parts = lax.axis_size("ctx")
    groups = lax.axis_size("dp")
    ratio = parts // groups
    pieces = block.reshape(ratio, rows, block.shape[1])
    columns = []
    for lane_block in range(ratio):
        total = None
        for piece in range(ratio):
            pairs = [
                (sd * parts + sc, (sc // ratio) * parts + sd * ratio + piece)
                for sd in range(groups)
                for sc in range(lane_block, parts, ratio)
            ]
            got = lax.ppermute(pieces[piece], ("dp", "ctx"), pairs)
            total = got if total is None else total + got
        columns.append(total)
    return jnp.concatenate(columns, 1)


def halving_scatter(data, axis):
    size = lax.axis_size(axis)
    index = lax.axis_index(axis)
    rows, chans = data.shape
    blocks = data.reshape(rows, size, chans // size)
    step = size // 2
    while step >= 1:
        half = blocks.shape[1] // 2
        upper = (index // step) % 2 == 1
        keep = jnp.where(upper, blocks[:, half:], blocks[:, :half])
        give = jnp.where(upper, blocks[:, :half], blocks[:, half:])
        blocks = keep + lax.ppermute(give, axis, [(i, i ^ step) for i in range(size)])
        step //= 2
    return blocks.reshape(rows, chans // size)


def epilogue_kernel(conv_ref, back_ref, src_ref, up_ref, mask_ref, w_ref, skip_ref, out_ref, stats_ref):
    wide, narrow = jnp.float32, jnp.bfloat16
    taps = w_ref.shape[1]
    head = taps - 1
    frame = src_ref.shape[1]
    rows = out_ref.shape[1]

    def mask(i):
        return mask_ref[i] > 0.5

    def down(x, by):
        return pltpu.roll(x, by, 0) if by else x

    def lift(x, by):
        return pltpu.roll(x, frame - by, 0) if by else x

    sources = [src_ref[i].astype(wide) for i in range(3)]
    weights = w_ref[...]
    shorts = []
    for i in range(3):
        total = weights[i, 0:1] * sources[i]
        for off in range(1, taps):
            total = total + jnp.where(mask(off), weights[i, off : off + 1] * down(sources[i], off), 0.0)
        shorts.append(total.astype(narrow).astype(wide))
    q_short, k_short, v_short = shorts
    upstream = up_ref[...].astype(wide)
    skip = skip_ref[...]
    mixed = (k_short * v_short).astype(narrow).astype(wide)
    grad_conv = (upstream * q_short).astype(narrow).astype(wide)
    conv = conv_ref[...].astype(wide) + skip * mixed
    grad_mixed = back_ref[...].astype(wide) + skip * grad_conv
    own = mask(2 * taps)
    out_ref[0] = lift(q_short * conv, head)[:rows].astype(narrow)
    grads = [upstream * conv, grad_mixed * v_short, grad_mixed * k_short]
    stats = []
    for i in range(3):
        grad = grads[i]
        acc = weights[i, 0:1] * grad
        stats.append(jnp.sum(jnp.where(own, sources[i] * grad, 0.0), axis=0, keepdims=True))
        for off in range(1, taps):
            later = lift(jnp.where(mask(taps + off), grad, 0.0), off)
            acc = acc + weights[i, off : off + 1] * later
            lagged = jnp.where(own & mask(off), down(sources[i], off) * grad, 0.0)
            stats.append(jnp.sum(lagged, axis=0, keepdims=True))
        out_ref[1 + i] = lift(acc, head)[:rows].astype(narrow)
    stats.append(jnp.sum(jnp.where(own, grad_conv * mixed, 0.0), axis=0, keepdims=True))
    width = stats[0].shape[1]
    stats.append(jnp.zeros((stats_ref.shape[0] - len(stats), width), wide))
    stats_ref[...] = jnp.concatenate(stats, 0)


def epilogue(back, sources, upstream, masks, short_weights, skip, rows):
    _, frame, chans = back.shape
    taps = short_weights.shape[1]
    block = 512 if chans % 512 == 0 else chans
    grid = (chans // block,)
    stat_rows = 16
    return pl.pallas_call(
        epilogue_kernel,
        grid=grid,
        in_specs=[
            pl.BlockSpec((None, frame, block), lambda c: (0, 0, c)),
            pl.BlockSpec((None, frame, block), lambda c: (1, 0, c)),
            pl.BlockSpec((3, frame, block), lambda c: (0, 0, c)),
            pl.BlockSpec((frame, block), lambda c: (0, c)),
            pl.BlockSpec(masks.shape, lambda c: (0, 0, 0)),
            pl.BlockSpec((3, taps, block), lambda c: (0, 0, c)),
            pl.BlockSpec((1, block), lambda c: (0, c)),
        ],
        out_specs=[
            pl.BlockSpec((4, rows, block), lambda c: (0, 0, c)),
            pl.BlockSpec((stat_rows, block), lambda c: (0, c)),
        ],
        out_shape=[
            jax.ShapeDtypeStruct((4, rows, chans), jnp.bfloat16),
            jax.ShapeDtypeStruct((stat_rows, chans), jnp.float32),
        ],
    )(back, back, sources, upstream, masks, short_weights, skip[None])


def local(query, keys, values, cotangent, long_filter, short_weights, skip, lengths):
    parts = lax.axis_size("ctx")
    index = lax.axis_index("ctx")
    groups = lax.axis_size("dp")
    q_rows, k_rows, v_rows, c_rows = query[0], keys[0], values[0], cotangent[0]
    rows, chans = q_rows.shape
    taps = short_weights.shape[1]
    head = taps - 1
    seq_len = rows * parts
    lanes = chans // parts
    ext = rows + head
    frame = -(-(rows + 2 * head) // 8) * 8
    doc_len = lengths[0]
    starts = jnp.cumsum(doc_len) - doc_len

    position = index * rows + jnp.arange(ext, dtype=jnp.int32)
    begin = jnp.max(jnp.where(starts[None, :] <= position[:, None], starts[None, :], 0), axis=1)
    valid = position[None, :] - jnp.arange(taps, dtype=jnp.int32)[:, None] >= begin[None, :]
    valid_after = valid & (position < seq_len)[None, :]

    prev = shifted(jnp.stack([a[rows - head :] for a in (q_rows, k_rows, v_rows)]), "ctx", 1)
    nxt = shifted(jnp.stack([a[:head] for a in (q_rows, k_rows, v_rows, c_rows)]), "ctx", -1)
    padded = [
        jnp.concatenate([prev[i], src, nxt[i]], 0).astype(jnp.float32)
        for i, src in enumerate((q_rows, k_rows, v_rows))
    ]

    def short_forward(wide, weights):
        summed = weights[0] * wide[head : head + ext]
        for offset in range(1, taps):
            begin_at = head - offset
            summed = summed + jnp.where(
                valid[offset][:, None], weights[offset] * wide[begin_at : begin_at + ext], 0.0
            )
        return summed.astype(jnp.bfloat16).astype(jnp.float32)

    q_short = short_forward(padded[0], short_weights[0])
    k_short = short_forward(padded[1], short_weights[1])
    v_short = short_forward(padded[2], short_weights[2])
    upstream = jnp.concatenate([c_rows, nxt[3]], 0).astype(jnp.float32)
    mixed = (k_short * v_short).astype(jnp.bfloat16)
    grad_conv = (upstream * q_short).astype(jnp.bfloat16)
    mixed_wide = mixed.astype(jnp.float32)
    grad_wide = grad_conv.astype(jnp.float32)

    chunks = 2 if lanes % 2 == 0 else 1
    width = lanes // chunks

    def to_columns(data, part):
        count = data.shape[0]
        split = data.reshape(count, rows, parts, chunks, width)[:, :, :, part]
        moved = lax.all_to_all(split.transpose(0, 2, 1, 3), "ctx", 1, 1, tiled=True)
        return moved.reshape(count, seq_len, width)

    sent = jnp.stack([long_filter, mixed[:rows], grad_conv[:rows]])
    returned = []
    lagged_parts = []
    previous = None
    for part in range(chunks):
        columns = to_columns(sent, part)
        if previous is not None:
            columns, previous = lax.optimization_barrier((columns, previous))
            returned.append(lax.all_to_all(previous, "ctx", 1, 1, tiled=True))
        spectra = fft_forward(columns)
        raw = fft_inverse(spectral_products(spectra), seq_len)
        lagged_parts.append(raw[2])
        raw = raw[:2].astype(jnp.bfloat16)
        raw = jnp.concatenate(
            [jnp.zeros((2, head, width), raw.dtype), raw, jnp.zeros((2, frame - rows - head, width), raw.dtype)], 1
        )
        blocks = jnp.stack([raw[:, j * rows : j * rows + frame] for j in range(parts)], 1)
        previous = blocks
    returned.append(lax.all_to_all(previous, "ctx", 1, 1, tiled=True))
    back = jnp.stack(returned, 3).transpose(0, 2, 1, 3, 4).reshape(2, frame, chans)
    lagged = halving_rows(jnp.concatenate(lagged_parts, 1), "dp")
    filter_part = route_filter_grad(lagged, rows)

    spot = index * rows - head + jnp.arange(frame, dtype=jnp.int32)
    spot_begin = jnp.max(jnp.where(starts[None, :] <= spot[:, None], starts[None, :], 0), axis=1)
    spot_valid = spot[None, :] - jnp.arange(taps, dtype=jnp.int32)[:, None] >= spot_begin[None, :]
    spot_after = spot_valid & ((spot >= 0) & (spot < seq_len))[None, :]
    spot_own = ((spot >= index * rows) & (spot < index * rows + rows))[None, :]
    masks = jnp.concatenate([spot_valid, spot_after, spot_own], 0).astype(jnp.float32)
    masks = jnp.concatenate([masks, jnp.zeros(((-masks.shape[0]) % 8, frame), jnp.float32)], 0)
    tail = frame - rows - 2 * head
    sources = jnp.stack([
        jnp.concatenate([prev[i], src, nxt[i], jnp.zeros((tail, chans), src.dtype)], 0)
        for i, src in enumerate((q_rows, k_rows, v_rows))
    ])
    framed_up = jnp.concatenate(
        [jnp.zeros((head, chans), c_rows.dtype), c_rows, nxt[3], jnp.zeros((tail, chans), c_rows.dtype)], 0
    )
    outs, stats = epilogue(back, sources, framed_up, masks[:, :, None], short_weights, skip, rows)
    summed = mesh_sum(stats[: 3 * taps + 1], ("dp", "ctx"))
    gated, grad_q, grad_k, grad_v = outs[0], outs[1], outs[2], outs[3]
    scale = 1.0 / (groups * seq_len)
    return (
        gated[None],
        grad_q.astype(jnp.bfloat16)[None],
        grad_k.astype(jnp.bfloat16)[None],
        grad_v.astype(jnp.bfloat16)[None],
        filter_part * scale,
        summed[: 3 * taps].reshape(3, taps, chans) * scale,
        summed[3 * taps] * scale,
    )


def solution(mesh):
    in_specs = (
        P("dp", "ctx", None),
        P("dp", "ctx", None),
        P("dp", "ctx", None),
        P("dp", "ctx", None),
        P("ctx", None),
        P(),
        P(),
        P("dp", None),
    )
    out_specs = (
        P("dp", "ctx", None),
        P("dp", "ctx", None),
        P("dp", "ctx", None),
        P("dp", "ctx", None),
        P("ctx", "dp"),
        P(),
        P(),
    )
    return jax.shard_map(local, mesh=mesh, in_specs=in_specs, out_specs=out_specs, check_vma=False)
```

```python
import math

import jax
import jax.numpy as jnp
import ml_dtypes
import numpy as np
from jax import lax
from jax.experimental import pallas as pl
from jax.experimental.pallas import tpu as pltpu
from jax.sharding import PartitionSpec as P


def shifted(x, axis, by):
    length = lax.axis_size(axis)
    pairs = [(i, i + by) for i in range(length) if 0 <= i + by < length]
    return lax.ppermute(x, axis, pairs)


def table_halves(table):
    upper = table.astype(ml_dtypes.bfloat16)
    lower = (table - upper.astype(np.float64)).astype(ml_dtypes.bfloat16)
    return jnp.asarray(upper), jnp.asarray(lower)


def split_product(form, table, data, exact=True):
    upper, lower = table_halves(table)
    wide = jnp.float32
    if not exact:
        return jnp.einsum(form, upper, data.astype(jnp.bfloat16), preferred_element_type=wide)
    if data.dtype == jnp.bfloat16:
        total = jnp.einsum(form, upper, data, preferred_element_type=wide)
        return total + jnp.einsum(form, lower, data, preferred_element_type=wide)
    data_upper = lax.optimization_barrier(data.astype(jnp.bfloat16))
    data_lower = (data - data_upper.astype(wide)).astype(jnp.bfloat16)
    total = jnp.einsum(form, upper, data_upper, preferred_element_type=wide)
    total = total + jnp.einsum(form, lower, data_upper, preferred_element_type=wide)
    return total + jnp.einsum(form, upper, data_lower, preferred_element_type=wide)


def batched_product(table, data):
    count, outer, twice, lanes = data.shape
    upper = jnp.asarray(table.astype(ml_dtypes.bfloat16))
    upper = jnp.broadcast_to(upper, (count, outer, twice, twice))
    return jnp.einsum(
        "skab,skbc->skac", upper, data.astype(jnp.bfloat16), preferred_element_type=jnp.float32
    )


def factors(size):
    bits = size.bit_length() - 1
    inner = 1 << (bits // 2)
    return size // inner, inner


def twiddles(outer, inner, size):
    phase = 2.0 * np.pi * np.outer(np.arange(outer), np.arange(inner)) / size
    cosine = jnp.asarray(np.cos(phase), jnp.float32)[None, :, :, None]
    sine = jnp.asarray(np.sin(phase), jnp.float32)[None, :, :, None]
    return cosine, sine


def inner_table(inner, sign):
    phase = 2.0 * np.pi * np.outer(np.arange(inner), np.arange(inner)) / inner
    cosine, sine = np.cos(phase), sign * np.sin(phase)
    return np.block([[cosine, sine], [-sine, cosine]])


def fft_forward(signal):
    count, length, lanes = signal.shape
    size = 2 * length
    outer, inner = factors(size)
    half = outer // 2
    phase = 2.0 * np.pi * np.outer(np.arange(outer), np.arange(half)) / outer
    first = np.concatenate([np.cos(phase), -np.sin(phase)], 0)
    blocks = signal.reshape(count, half, inner, lanes).transpose(1, 0, 2, 3)
    stage = split_product("kn,nsqb->ksqb", first, blocks, exact=False)
    real_part, imag_part = stage[:outer], stage[outer:]
    cosine, sine = twiddles(outer, inner, size)
    cosine, sine = cosine.transpose(1, 0, 2, 3), sine.transpose(1, 0, 2, 3)
    turned = jnp.stack(
        [real_part * cosine + imag_part * sine, imag_part * cosine - real_part * sine]
    ).astype(jnp.bfloat16)
    turned = turned.transpose(0, 3, 2, 1, 4).reshape(2 * inner, count, outer, lanes)
    return split_product("ab,bskc->askc", inner_table(inner, 1.0), turned, exact=False)


def fft_inverse(spectrum, length):
    twice, count, outer, lanes = spectrum.shape
    inner = twice // 2
    size = outer * inner
    half = outer // 2
    stage = split_product("ab,bskc->askc", inner_table(inner, -1.0), spectrum, exact=False)
    real_part, imag_part = stage[:inner], stage[inner:]
    cosine, sine = twiddles(outer, inner, size)
    cosine, sine = cosine.transpose(2, 0, 1, 3), sine.transpose(2, 0, 1, 3)
    turned = jnp.stack(
        [real_part * cosine - imag_part * sine, imag_part * cosine + real_part * sine]
    ).astype(jnp.bfloat16)
    turned = turned.transpose(0, 3, 2, 1, 4).reshape(2 * outer, count, inner, lanes)
    phase = 2.0 * np.pi * np.outer(np.arange(half), np.arange(outer)) / outer
    last = np.concatenate([np.cos(phase), -np.sin(phase)], 1) / size
    result = split_product("nk,ksqb->nsqb", last, turned, exact=False)
    return result.transpose(1, 0, 2, 3).reshape(count, length, lanes)


def spectral_products(spectra):
    inner = spectra.shape[0] // 2
    parts = [(spectra[:inner, i], spectra[inner:, i]) for i in range(3)]
    (f_re, f_im), (m_re, m_im), (g_re, g_im) = parts
    conv = jnp.concatenate([m_re * f_re - m_im * f_im, m_re * f_im + m_im * f_re], 0)
    back = jnp.concatenate([g_re * f_re + g_im * f_im, g_im * f_re - g_re * f_im], 0)
    cross = jnp.concatenate([g_re * m_re + g_im * m_im, g_im * m_re - g_re * m_im], 0)
    return jnp.stack([conv, back, cross], 1)


def all_sum(data, axis):
    size = lax.axis_size(axis)
    total = data
    for step in range(1, size):
        total = total + lax.ppermute(data, axis, [(i, (i + step) % size) for i in range(size)])
    return total


def mesh_sum(data, axes):
    count = 1
    for axis in axes:
        count *= lax.axis_size(axis)
    rows, chans = data.shape
    pieces = data.reshape(rows, count, chans // count).transpose(1, 0, 2)
    mine = jnp.sum(lax.all_to_all(pieces, axes, 0, 0, tiled=True), axis=0)
    spread = jnp.broadcast_to(mine[None], (count,) + mine.shape)
    gathered = lax.all_to_all(spread, axes, 0, 0, tiled=True)
    return gathered.transpose(1, 0, 2).reshape(rows, chans)


def halving_rows(data, axis):
    size = lax.axis_size(axis)
    index = lax.axis_index(axis)
    blocks = data.reshape(size, data.shape[0] // size, data.shape[1])
    step = size // 2
    while step >= 1:
        half = blocks.shape[0] // 2
        upper = (index // step) % 2 == 1
        keep = jnp.where(upper, blocks[half:], blocks[:half])
        give = jnp.where(upper, blocks[:half], blocks[half:])
        blocks = keep + lax.ppermute(give, axis, [(i, i ^ step) for i in range(size)])
        step //= 2
    return blocks.reshape(-1, data.shape[1])


def route_filter_grad(block, rows):
    parts = lax.axis_size("ctx")
    groups = lax.axis_size("dp")
    ratio = parts // groups
    pieces = block.reshape(ratio, rows, block.shape[1])
    columns = []
    for lane_block in range(ratio):
        total = None
        for piece in range(ratio):
            pairs = [
                (sd * parts + sc, (sc // ratio) * parts + sd * ratio + piece)
                for sd in range(groups)
                for sc in range(lane_block, parts, ratio)
            ]
            got = lax.ppermute(pieces[piece], ("dp", "ctx"), pairs)
            total = got if total is None else total + got
        columns.append(total)
    return jnp.concatenate(columns, 1)


def halving_scatter(data, axis):
    size = lax.axis_size(axis)
    index = lax.axis_index(axis)
    rows, chans = data.shape
    blocks = data.reshape(rows, size, chans // size)
    step = size // 2
    while step >= 1:
        half = blocks.shape[1] // 2
        upper = (index // step) % 2 == 1
        keep = jnp.where(upper, blocks[:, half:], blocks[:, :half])
        give = jnp.where(upper, blocks[:, :half], blocks[:, half:])
        blocks = keep + lax.ppermute(give, axis, [(i, i ^ step) for i in range(size)])
        step //= 2
    return blocks.reshape(rows, chans // size)


def epilogue_kernel(conv_ref, back_ref, src_ref, up_ref, mask_ref, w_ref, skip_ref, out_ref, stats_ref):
    wide, narrow = jnp.float32, jnp.bfloat16
    taps = w_ref.shape[1]
    head = taps - 1
    frame = src_ref.shape[1]
    rows = out_ref.shape[1]

    def mask(i):
        return mask_ref[i] > 0.5

    def down(x, by):
        return pltpu.roll(x, by, 0) if by else x

    def lift(x, by):
        return pltpu.roll(x, frame - by, 0) if by else x

    sources = [src_ref[i].astype(wide) for i in range(3)]
    weights = w_ref[...]
    shorts = []
    for i in range(3):
        total = weights[i, 0:1] * sources[i]
        for off in range(1, taps):
            total = total + jnp.where(mask(off), weights[i, off : off + 1] * down(sources[i], off), 0.0)
        shorts.append(total.astype(narrow).astype(wide))
    q_short, k_short, v_short = shorts
    upstream = up_ref[...].astype(wide)
    skip = skip_ref[...]
    mixed = (k_short * v_short).astype(narrow).astype(wide)
    grad_conv = (upstream * q_short).astype(narrow).astype(wide)
    conv = conv_ref[...].astype(wide) + skip * mixed
    grad_mixed = back_ref[...].astype(wide) + skip * grad_conv
    own = mask(2 * taps)
    out_ref[0] = lift(q_short * conv, head)[:rows].astype(narrow)
    grads = [upstream * conv, grad_mixed * v_short, grad_mixed * k_short]
    stats = []
    for i in range(3):
        grad = grads[i]
        acc = weights[i, 0:1] * grad
        stats.append(jnp.sum(jnp.where(own, sources[i] * grad, 0.0), axis=0, keepdims=True))
        for off in range(1, taps):
            later = lift(jnp.where(mask(taps + off), grad, 0.0), off)
            acc = acc + weights[i, off : off + 1] * later
            lagged = jnp.where(own & mask(off), down(sources[i], off) * grad, 0.0)
            stats.append(jnp.sum(lagged, axis=0, keepdims=True))
        out_ref[1 + i] = lift(acc, head)[:rows].astype(narrow)
    stats.append(jnp.sum(jnp.where(own, grad_conv * mixed, 0.0), axis=0, keepdims=True))
    width = stats[0].shape[1]
    stats.append(jnp.zeros((stats_ref.shape[0] - len(stats), width), wide))
    stats_ref[...] = jnp.concatenate(stats, 0)


def epilogue(back, sources, upstream, masks, short_weights, skip, rows):
    _, frame, chans = back.shape
    taps = short_weights.shape[1]
    block = 512 if chans % 512 == 0 else chans
    grid = (chans // block,)
    stat_rows = 16
    return pl.pallas_call(
        epilogue_kernel,
        grid=grid,
        in_specs=[
            pl.BlockSpec((None, frame, block), lambda c: (0, 0, c)),
            pl.BlockSpec((None, frame, block), lambda c: (1, 0, c)),
            pl.BlockSpec((3, frame, block), lambda c: (0, 0, c)),
            pl.BlockSpec((frame, block), lambda c: (0, c)),
            pl.BlockSpec(masks.shape, lambda c: (0, 0, 0)),
            pl.BlockSpec((3, taps, block), lambda c: (0, 0, c)),
            pl.BlockSpec((1, block), lambda c: (0, c)),
        ],
        out_specs=[
            pl.BlockSpec((4, rows, block), lambda c: (0, 0, c)),
            pl.BlockSpec((stat_rows, block), lambda c: (0, c)),
        ],
        out_shape=[
            jax.ShapeDtypeStruct((4, rows, chans), jnp.bfloat16),
            jax.ShapeDtypeStruct((stat_rows, chans), jnp.float32),
        ],
    )(back, back, sources, upstream, masks, short_weights, skip[None])


def local(query, keys, values, cotangent, long_filter, short_weights, skip, lengths):
    parts = lax.axis_size("ctx")
    index = lax.axis_index("ctx")
    groups = lax.axis_size("dp")
    q_rows, k_rows, v_rows, c_rows = query[0], keys[0], values[0], cotangent[0]
    rows, chans = q_rows.shape
    taps = short_weights.shape[1]
    head = taps - 1
    seq_len = rows * parts
    lanes = chans // parts
    ext = rows + head
    frame = -(-(rows + 2 * head) // 8) * 8
    doc_len = lengths[0]
    starts = jnp.cumsum(doc_len) - doc_len

    position = index * rows + jnp.arange(ext, dtype=jnp.int32)
    begin = jnp.max(jnp.where(starts[None, :] <= position[:, None], starts[None, :], 0), axis=1)
    valid = position[None, :] - jnp.arange(taps, dtype=jnp.int32)[:, None] >= begin[None, :]
    valid_after = valid & (position < seq_len)[None, :]

    prev = shifted(jnp.stack([a[rows - head :] for a in (q_rows, k_rows, v_rows)]), "ctx", 1)
    nxt = shifted(jnp.stack([a[:head] for a in (q_rows, k_rows, v_rows, c_rows)]), "ctx", -1)
    padded = [
        jnp.concatenate([prev[i], src], 0).astype(jnp.float32)
        for i, src in enumerate((q_rows, k_rows, v_rows))
    ]

    def short_forward(wide, weights):
        summed = weights[0] * wide[head : head + rows]
        for offset in range(1, taps):
            begin_at = head - offset
            summed = summed + jnp.where(
                valid[offset, :rows][:, None], weights[offset] * wide[begin_at : begin_at + rows], 0.0
            )
        return summed.astype(jnp.bfloat16).astype(jnp.float32)

    q_short = short_forward(padded[0], short_weights[0])
    k_short = short_forward(padded[1], short_weights[1])
    v_short = short_forward(padded[2], short_weights[2])
    mixed = (k_short * v_short).astype(jnp.bfloat16)
    grad_conv = (c_rows.astype(jnp.float32) * q_short).astype(jnp.bfloat16)

    chunks = 2 if lanes % 2 == 0 else 1
    width = lanes // chunks

    def to_columns(data, part):
        count = data.shape[0]
        split = data.reshape(count, rows, parts, chunks, width)[:, :, :, part]
        moved = lax.all_to_all(split.transpose(0, 2, 1, 3), "ctx", 1, 1, tiled=True)
        return moved.reshape(count, seq_len, width)

    sent = jnp.stack([long_filter, mixed, grad_conv])
    returned = []
    lagged_parts = []
    previous = None
    for part in range(chunks):
        columns = to_columns(sent, part)
        if previous is not None:
            columns, previous = lax.optimization_barrier((columns, previous))
            returned.append(lax.all_to_all(previous, "ctx", 1, 1, tiled=True))
        spectra = fft_forward(columns)
        raw = fft_inverse(spectral_products(spectra), seq_len)
        lagged_parts.append(raw[2])
        raw = raw[:2].astype(jnp.bfloat16)
        raw = jnp.concatenate(
            [jnp.zeros((2, head, width), raw.dtype), raw, jnp.zeros((2, frame - rows - head, width), raw.dtype)], 1
        )
        blocks = jnp.stack([raw[:, j * rows : j * rows + frame] for j in range(parts)], 1)
        previous = blocks
    returned.append(lax.all_to_all(previous, "ctx", 1, 1, tiled=True))
    back = jnp.stack(returned, 3).transpose(0, 2, 1, 3, 4).reshape(2, frame, chans)
    lagged = halving_rows(jnp.concatenate(lagged_parts, 1), "dp")
    filter_part = route_filter_grad(lagged, rows)

    spot = index * rows - head + jnp.arange(frame, dtype=jnp.int32)
    spot_begin = jnp.max(jnp.where(starts[None, :] <= spot[:, None], starts[None, :], 0), axis=1)
    spot_valid = spot[None, :] - jnp.arange(taps, dtype=jnp.int32)[:, None] >= spot_begin[None, :]
    spot_after = spot_valid & ((spot >= 0) & (spot < seq_len))[None, :]
    spot_own = ((spot >= index * rows) & (spot < index * rows + rows))[None, :]
    masks = jnp.concatenate([spot_valid, spot_after, spot_own], 0).astype(jnp.float32)
    masks = jnp.concatenate([masks, jnp.zeros(((-masks.shape[0]) % 8, frame), jnp.float32)], 0)
    tail = frame - rows - 2 * head
    sources = jnp.stack([
        jnp.concatenate([prev[i], src, nxt[i], jnp.zeros((tail, chans), src.dtype)], 0)
        for i, src in enumerate((q_rows, k_rows, v_rows))
    ])
    framed_up = jnp.concatenate(
        [jnp.zeros((head, chans), c_rows.dtype), c_rows, nxt[3], jnp.zeros((tail, chans), c_rows.dtype)], 0
    )
    outs, stats = epilogue(back, sources, framed_up, masks[:, :, None], short_weights, skip, rows)
    summed = mesh_sum(stats[: 3 * taps + 1], ("dp", "ctx"))
    gated, grad_q, grad_k, grad_v = outs[0], outs[1], outs[2], outs[3]
    scale = 1.0 / (groups * seq_len)
    return (
        gated[None],
        grad_q.astype(jnp.bfloat16)[None],
        grad_k.astype(jnp.bfloat16)[None],
        grad_v.astype(jnp.bfloat16)[None],
        filter_part * scale,
        summed[: 3 * taps].reshape(3, taps, chans) * scale,
        summed[3 * taps] * scale,
    )


def solution(mesh):
    in_specs = (
        P("dp", "ctx", None),
        P("dp", "ctx", None),
        P("dp", "ctx", None),
        P("dp", "ctx", None),
        P("ctx", None),
        P(),
        P(),
        P("dp", None),
    )
    out_specs = (
        P("dp", "ctx", None),
        P("dp", "ctx", None),
        P("dp", "ctx", None),
        P("dp", "ctx", None),
        P("ctx", "dp"),
        P(),
        P(),
    )
    return jax.shard_map(local, mesh=mesh, in_specs=in_specs, out_specs=out_specs, check_vma=False)
```

```python
import math

import jax
import jax.numpy as jnp
import ml_dtypes
import numpy as np
from jax import lax
from jax.experimental import pallas as pl
from jax.experimental.pallas import tpu as pltpu
from jax.sharding import PartitionSpec as P


def shifted(x, axis, by):
    length = lax.axis_size(axis)
    pairs = [(i, i + by) for i in range(length) if 0 <= i + by < length]
    return lax.ppermute(x, axis, pairs)


def table_halves(table):
    upper = table.astype(ml_dtypes.bfloat16)
    lower = (table - upper.astype(np.float64)).astype(ml_dtypes.bfloat16)
    return jnp.asarray(upper), jnp.asarray(lower)


def split_product(form, table, data, exact=True):
    upper, lower = table_halves(table)
    wide = jnp.float32
    if not exact:
        return jnp.einsum(form, upper, data.astype(jnp.bfloat16), preferred_element_type=wide)
    if data.dtype == jnp.bfloat16:
        total = jnp.einsum(form, upper, data, preferred_element_type=wide)
        return total + jnp.einsum(form, lower, data, preferred_element_type=wide)
    data_upper = lax.optimization_barrier(data.astype(jnp.bfloat16))
    data_lower = (data - data_upper.astype(wide)).astype(jnp.bfloat16)
    total = jnp.einsum(form, upper, data_upper, preferred_element_type=wide)
    total = total + jnp.einsum(form, lower, data_upper, preferred_element_type=wide)
    return total + jnp.einsum(form, upper, data_lower, preferred_element_type=wide)


def batched_product(table, data):
    count, outer, twice, lanes = data.shape
    upper = jnp.asarray(table.astype(ml_dtypes.bfloat16))
    upper = jnp.broadcast_to(upper, (count, outer, twice, twice))
    return jnp.einsum(
        "skab,skbc->skac", upper, data.astype(jnp.bfloat16), preferred_element_type=jnp.float32
    )


def factors(size):
    bits = size.bit_length() - 1
    inner = 1 << (bits // 2)
    return size // inner, inner


def twiddles(outer, inner, size):
    phase = 2.0 * np.pi * np.outer(np.arange(outer), np.arange(inner)) / size
    cosine = jnp.asarray(np.cos(phase), jnp.float32)[None, :, :, None]
    sine = jnp.asarray(np.sin(phase), jnp.float32)[None, :, :, None]
    return cosine, sine


def inner_table(inner, sign):
    phase = 2.0 * np.pi * np.outer(np.arange(inner), np.arange(inner)) / inner
    cosine, sine = np.cos(phase), sign * np.sin(phase)
    return np.block([[cosine, sine], [-sine, cosine]])


def fft_forward(signal):
    count, length, lanes = signal.shape
    size = 2 * length
    outer, inner = factors(size)
    half = outer // 2
    phase = 2.0 * np.pi * np.outer(np.arange(outer), np.arange(half)) / outer
    first = np.concatenate([np.cos(phase), -np.sin(phase)], 0)
    blocks = signal.reshape(count, half, inner, lanes).transpose(1, 0, 2, 3)
    stage = split_product("kn,nsqb->ksqb", first, blocks, exact=False)
    real_part, imag_part = stage[:outer], stage[outer:]
    cosine, sine = twiddles(outer, inner, size)
    cosine, sine = cosine.transpose(1, 0, 2, 3), sine.transpose(1, 0, 2, 3)
    turned = jnp.stack(
        [real_part * cosine + imag_part * sine, imag_part * cosine - real_part * sine]
    ).astype(jnp.bfloat16)
    turned = turned.transpose(0, 3, 2, 1, 4).reshape(2 * inner, count, outer, lanes)
    return split_product("ab,bskc->askc", inner_table(inner, 1.0), turned, exact=False)


def fft_inverse(spectrum, length):
    twice, count, outer, lanes = spectrum.shape
    inner = twice // 2
    size = outer * inner
    half = outer // 2
    stage = split_product("ab,bskc->askc", inner_table(inner, -1.0), spectrum, exact=False)
    real_part, imag_part = stage[:inner], stage[inner:]
    cosine, sine = twiddles(outer, inner, size)
    cosine, sine = cosine.transpose(2, 0, 1, 3), sine.transpose(2, 0, 1, 3)
    turned = jnp.stack(
        [real_part * cosine - imag_part * sine, imag_part * cosine + real_part * sine]
    ).astype(jnp.bfloat16)
    turned = turned.transpose(0, 3, 2, 1, 4).reshape(2 * outer, count, inner, lanes)
    phase = 2.0 * np.pi * np.outer(np.arange(half), np.arange(outer)) / outer
    last = np.concatenate([np.cos(phase), -np.sin(phase)], 1) / size
    result = split_product("nk,ksqb->nsqb", last, turned, exact=False)
    return result.transpose(1, 0, 2, 3).reshape(count, length, lanes)


def spectral_products(spectra):
    inner = spectra.shape[0] // 2
    parts = [(spectra[:inner, i], spectra[inner:, i]) for i in range(3)]
    (f_re, f_im), (m_re, m_im), (g_re, g_im) = parts
    conv = jnp.concatenate([m_re * f_re - m_im * f_im, m_re * f_im + m_im * f_re], 0)
    back = jnp.concatenate([g_re * f_re + g_im * f_im, g_im * f_re - g_re * f_im], 0)
    cross = jnp.concatenate([g_re * m_re + g_im * m_im, g_im * m_re - g_re * m_im], 0)
    return jnp.stack([conv, back, cross], 1)


def all_sum(data, axis):
    size = lax.axis_size(axis)
    total = data
    for step in range(1, size):
        total = total + lax.ppermute(data, axis, [(i, (i + step) % size) for i in range(size)])
    return total


def mesh_sum(data, axes):
    count = 1
    for axis in axes:
        count *= lax.axis_size(axis)
    rows, chans = data.shape
    pieces = data.reshape(rows, count, chans // count).transpose(1, 0, 2)
    mine = jnp.sum(lax.all_to_all(pieces, axes, 0, 0, tiled=True), axis=0)
    spread = jnp.broadcast_to(mine[None], (count,) + mine.shape)
    gathered = lax.all_to_all(spread, axes, 0, 0, tiled=True)
    return gathered.transpose(1, 0, 2).reshape(rows, chans)


def halving_rows(data, axis):
    size = lax.axis_size(axis)
    index = lax.axis_index(axis)
    blocks = data.reshape(size, data.shape[0] // size, data.shape[1])
    step = size // 2
    while step >= 1:
        half = blocks.shape[0] // 2
        upper = (index // step) % 2 == 1
        keep = jnp.where(upper, blocks[half:], blocks[:half])
        give = jnp.where(upper, blocks[:half], blocks[half:])
        blocks = keep + lax.ppermute(give, axis, [(i, i ^ step) for i in range(size)])
        step //= 2
    return blocks.reshape(-1, data.shape[1])


def route_filter_grad(block, rows):
    parts = lax.axis_size("ctx")
    groups = lax.axis_size("dp")
    ratio = parts // groups
    pieces = block.reshape(ratio, rows, block.shape[1])
    columns = []
    for lane_block in range(ratio):
        total = None
        for piece in range(ratio):
            pairs = [
                (sd * parts + sc, (sc // ratio) * parts + sd * ratio + piece)
                for sd in range(groups)
                for sc in range(lane_block, parts, ratio)
            ]
            got = lax.ppermute(pieces[piece], ("dp", "ctx"), pairs)
            total = got if total is None else total + got
        columns.append(total)
    return jnp.concatenate(columns, 1)


def halving_scatter(data, axis):
    size = lax.axis_size(axis)
    index = lax.axis_index(axis)
    rows, chans = data.shape
    blocks = data.reshape(rows, size, chans // size)
    step = size // 2
    while step >= 1:
        half = blocks.shape[1] // 2
        upper = (index // step) % 2 == 1
        keep = jnp.where(upper, blocks[:, half:], blocks[:, :half])
        give = jnp.where(upper, blocks[:, :half], blocks[:, half:])
        blocks = keep + lax.ppermute(give, axis, [(i, i ^ step) for i in range(size)])
        step //= 2
    return blocks.reshape(rows, chans // size)


def epilogue_kernel(conv_ref, back_ref, src_ref, up_ref, mask_ref, w_ref, skip_ref, out_ref, stats_ref):
    wide, narrow = jnp.float32, jnp.bfloat16
    taps = w_ref.shape[1]
    head = taps - 1
    frame = src_ref.shape[1]
    rows = out_ref.shape[1]

    def mask(i):
        return mask_ref[i] > 0.5

    def down(x, by):
        return pltpu.roll(x, by, 0) if by else x

    def lift(x, by):
        return pltpu.roll(x, frame - by, 0) if by else x

    sources = [src_ref[i].astype(wide) for i in range(3)]
    weights = w_ref[...]
    shorts = []
    for i in range(3):
        total = weights[i, 0:1] * sources[i]
        for off in range(1, taps):
            total = total + jnp.where(mask(off), weights[i, off : off + 1] * down(sources[i], off), 0.0)
        shorts.append(total.astype(narrow).astype(wide))
    q_short, k_short, v_short = shorts
    upstream = up_ref[...].astype(wide)
    skip = skip_ref[...]
    mixed = (k_short * v_short).astype(narrow).astype(wide)
    grad_conv = (upstream * q_short).astype(narrow).astype(wide)
    conv = conv_ref[...].astype(wide) + skip * mixed
    grad_mixed = back_ref[...].astype(wide) + skip * grad_conv
    own = mask(2 * taps)
    out_ref[0] = lift(q_short * conv, head)[:rows].astype(narrow)
    grads = [upstream * conv, grad_mixed * v_short, grad_mixed * k_short]
    stats = []
    for i in range(3):
        grad = grads[i]
        acc = weights[i, 0:1] * grad
        stats.append(jnp.sum(jnp.where(own, sources[i] * grad, 0.0), axis=0, keepdims=True))
        for off in range(1, taps):
            later = lift(jnp.where(mask(taps + off), grad, 0.0), off)
            acc = acc + weights[i, off : off + 1] * later
            lagged = jnp.where(own & mask(off), down(sources[i], off) * grad, 0.0)
            stats.append(jnp.sum(lagged, axis=0, keepdims=True))
        out_ref[1 + i] = lift(acc, head)[:rows].astype(narrow)
    stats.append(jnp.sum(jnp.where(own, grad_conv * mixed, 0.0), axis=0, keepdims=True))
    width = stats[0].shape[1]
    stats.append(jnp.zeros((stats_ref.shape[0] - len(stats), width), wide))
    stats_ref[...] = jnp.concatenate(stats, 0)


def epilogue(back, sources, upstream, masks, short_weights, skip, rows):
    _, frame, chans = back.shape
    taps = short_weights.shape[1]
    block = 512 if chans % 512 == 0 else chans
    grid = (chans // block,)
    stat_rows = 16
    return pl.pallas_call(
        epilogue_kernel,
        grid=grid,
        in_specs=[
            pl.BlockSpec((None, frame, block), lambda c: (0, 0, c)),
            pl.BlockSpec((None, frame, block), lambda c: (1, 0, c)),
            pl.BlockSpec((3, frame, block), lambda c: (0, 0, c)),
            pl.BlockSpec((frame, block), lambda c: (0, c)),
            pl.BlockSpec(masks.shape, lambda c: (0, 0, 0)),
            pl.BlockSpec((3, taps, block), lambda c: (0, 0, c)),
            pl.BlockSpec((1, block), lambda c: (0, c)),
        ],
        out_specs=[
            pl.BlockSpec((4, rows, block), lambda c: (0, 0, c)),
            pl.BlockSpec((stat_rows, block), lambda c: (0, c)),
        ],
        out_shape=[
            jax.ShapeDtypeStruct((4, rows, chans), jnp.bfloat16),
            jax.ShapeDtypeStruct((stat_rows, chans), jnp.float32),
        ],
    )(back, back, sources, upstream, masks, short_weights, skip[None])


def local(query, keys, values, cotangent, long_filter, short_weights, skip, lengths):
    parts = lax.axis_size("ctx")
    index = lax.axis_index("ctx")
    groups = lax.axis_size("dp")
    q_rows, k_rows, v_rows, c_rows = query[0], keys[0], values[0], cotangent[0]
    rows, chans = q_rows.shape
    taps = short_weights.shape[1]
    head = taps - 1
    seq_len = rows * parts
    lanes = chans // parts
    ext = rows + head
    frame = -(-(rows + 2 * head) // 8) * 8
    doc_len = lengths[0]
    starts = jnp.cumsum(doc_len) - doc_len

    position = index * rows + jnp.arange(ext, dtype=jnp.int32)
    begin = jnp.max(jnp.where(starts[None, :] <= position[:, None], starts[None, :], 0), axis=1)
    valid = position[None, :] - jnp.arange(taps, dtype=jnp.int32)[:, None] >= begin[None, :]
    valid_after = valid & (position < seq_len)[None, :]

    prev = shifted(jnp.stack([a[rows - head :] for a in (q_rows, k_rows, v_rows)]), "ctx", 1)
    padded = [
        jnp.concatenate([prev[i], src], 0).astype(jnp.float32)
        for i, src in enumerate((q_rows, k_rows, v_rows))
    ]

    def short_forward(wide, weights):
        summed = weights[0] * wide[head : head + rows]
        for offset in range(1, taps):
            begin_at = head - offset
            summed = summed + jnp.where(
                valid[offset, :rows][:, None], weights[offset] * wide[begin_at : begin_at + rows], 0.0
            )
        return summed.astype(jnp.bfloat16).astype(jnp.float32)

    q_short = short_forward(padded[0], short_weights[0])
    k_short = short_forward(padded[1], short_weights[1])
    v_short = short_forward(padded[2], short_weights[2])
    mixed = (k_short * v_short).astype(jnp.bfloat16)
    grad_conv = (c_rows.astype(jnp.float32) * q_short).astype(jnp.bfloat16)

    chunks = 2 if lanes % 2 == 0 else 1
    width = lanes // chunks

    def to_columns(data, part):
        count = data.shape[0]
        split = data.reshape(count, rows, parts, chunks, width)[:, :, :, part]
        moved = lax.all_to_all(split.transpose(0, 2, 1, 3), "ctx", 1, 1, tiled=True)
        return moved.reshape(count, seq_len, width)

    sent = jnp.stack([long_filter, mixed, grad_conv])
    returned = []
    lagged_parts = []
    previous = None
    for part in range(chunks):
        columns = to_columns(sent, part)
        if previous is not None:
            columns, previous = lax.optimization_barrier((columns, previous))
            returned.append(lax.all_to_all(previous, "ctx", 1, 1, tiled=True))
        spectra = fft_forward(columns)
        raw = fft_inverse(spectral_products(spectra), seq_len)
        lagged_parts.append(raw[2])
        raw = raw[:2].astype(jnp.bfloat16)
        raw = jnp.concatenate(
            [jnp.zeros((2, head, width), raw.dtype), raw, jnp.zeros((2, frame - rows - head, width), raw.dtype)], 1
        )
        blocks = jnp.stack([raw[:, j * rows : j * rows + frame] for j in range(parts)], 1)
        previous = blocks
    following = jnp.stack([a[:head] for a in (q_rows, k_rows, v_rows, c_rows)])
    following, previous = lax.optimization_barrier((following, previous))
    returned.append(lax.all_to_all(previous, "ctx", 1, 1, tiled=True))
    nxt = shifted(following, "ctx", -1)
    back = jnp.stack(returned, 3).transpose(0, 2, 1, 3, 4).reshape(2, frame, chans)
    lagged = halving_rows(jnp.concatenate(lagged_parts, 1), "dp")
    filter_part = route_filter_grad(lagged, rows)

    spot = index * rows - head + jnp.arange(frame, dtype=jnp.int32)
    spot_begin = jnp.max(jnp.where(starts[None, :] <= spot[:, None], starts[None, :], 0), axis=1)
    spot_valid = spot[None, :] - jnp.arange(taps, dtype=jnp.int32)[:, None] >= spot_begin[None, :]
    spot_after = spot_valid & ((spot >= 0) & (spot < seq_len))[None, :]
    spot_own = ((spot >= index * rows) & (spot < index * rows + rows))[None, :]
    masks = jnp.concatenate([spot_valid, spot_after, spot_own], 0).astype(jnp.float32)
    masks = jnp.concatenate([masks, jnp.zeros(((-masks.shape[0]) % 8, frame), jnp.float32)], 0)
    tail = frame - rows - 2 * head
    sources = jnp.stack([
        jnp.concatenate([prev[i], src, nxt[i], jnp.zeros((tail, chans), src.dtype)], 0)
        for i, src in enumerate((q_rows, k_rows, v_rows))
    ])
    framed_up = jnp.concatenate(
        [jnp.zeros((head, chans), c_rows.dtype), c_rows, nxt[3], jnp.zeros((tail, chans), c_rows.dtype)], 0
    )
    outs, stats = epilogue(back, sources, framed_up, masks[:, :, None], short_weights, skip, rows)
    summed = mesh_sum(stats[: 3 * taps + 1], ("dp", "ctx"))
    gated, grad_q, grad_k, grad_v = outs[0], outs[1], outs[2], outs[3]
    scale = 1.0 / (groups * seq_len)
    return (
        gated[None],
        grad_q.astype(jnp.bfloat16)[None],
        grad_k.astype(jnp.bfloat16)[None],
        grad_v.astype(jnp.bfloat16)[None],
        filter_part * scale,
        summed[: 3 * taps].reshape(3, taps, chans) * scale,
        summed[3 * taps] * scale,
    )


def solution(mesh):
    in_specs = (
        P("dp", "ctx", None),
        P("dp", "ctx", None),
        P("dp", "ctx", None),
        P("dp", "ctx", None),
        P("ctx", None),
        P(),
        P(),
        P("dp", None),
    )
    out_specs = (
        P("dp", "ctx", None),
        P("dp", "ctx", None),
        P("dp", "ctx", None),
        P("dp", "ctx", None),
        P("ctx", "dp"),
        P(),
        P(),
    )
    return jax.shard_map(local, mesh=mesh, in_specs=in_specs, out_specs=out_specs, check_vma=False)
```

```python
import math

import jax
import jax.numpy as jnp
import ml_dtypes
import numpy as np
from jax import lax
from jax.experimental import pallas as pl
from jax.experimental.pallas import tpu as pltpu
from jax.sharding import PartitionSpec as P


def shifted(x, axis, by):
    length = lax.axis_size(axis)
    pairs = [(i, i + by) for i in range(length) if 0 <= i + by < length]
    return lax.ppermute(x, axis, pairs)


def table_halves(table):
    upper = table.astype(ml_dtypes.bfloat16)
    lower = (table - upper.astype(np.float64)).astype(ml_dtypes.bfloat16)
    return jnp.asarray(upper), jnp.asarray(lower)


def split_product(form, table, data, exact=True):
    upper, lower = table_halves(table)
    wide = jnp.float32
    if not exact:
        return jnp.einsum(form, upper, data.astype(jnp.bfloat16), preferred_element_type=wide)
    if data.dtype == jnp.bfloat16:
        total = jnp.einsum(form, upper, data, preferred_element_type=wide)
        return total + jnp.einsum(form, lower, data, preferred_element_type=wide)
    data_upper = lax.optimization_barrier(data.astype(jnp.bfloat16))
    data_lower = (data - data_upper.astype(wide)).astype(jnp.bfloat16)
    total = jnp.einsum(form, upper, data_upper, preferred_element_type=wide)
    total = total + jnp.einsum(form, lower, data_upper, preferred_element_type=wide)
    return total + jnp.einsum(form, upper, data_lower, preferred_element_type=wide)


def batched_product(table, data):
    count, outer, twice, lanes = data.shape
    upper = jnp.asarray(table.astype(ml_dtypes.bfloat16))
    upper = jnp.broadcast_to(upper, (count, outer, twice, twice))
    return jnp.einsum(
        "skab,skbc->skac", upper, data.astype(jnp.bfloat16), preferred_element_type=jnp.float32
    )


def factors(size):
    bits = size.bit_length() - 1
    inner = 1 << (bits // 2)
    return size // inner, inner


def twiddles(outer, inner, size):
    phase = 2.0 * np.pi * np.outer(np.arange(outer), np.arange(inner)) / size
    cosine = jnp.asarray(np.cos(phase), jnp.float32)[None, :, :, None]
    sine = jnp.asarray(np.sin(phase), jnp.float32)[None, :, :, None]
    return cosine, sine


def inner_table(inner, sign):
    phase = 2.0 * np.pi * np.outer(np.arange(inner), np.arange(inner)) / inner
    cosine, sine = np.cos(phase), sign * np.sin(phase)
    return np.block([[cosine, sine], [-sine, cosine]])


def fft_forward(signal):
    count, length, lanes = signal.shape
    size = 2 * length
    outer, inner = factors(size)
    half = outer // 2
    phase = 2.0 * np.pi * np.outer(np.arange(outer), np.arange(half)) / outer
    first = np.concatenate([np.cos(phase), -np.sin(phase)], 0)
    blocks = signal.reshape(count, half, inner, lanes).transpose(1, 0, 2, 3)
    stage = split_product("kn,nsqb->ksqb", first, blocks, exact=False)
    real_part, imag_part = stage[:outer], stage[outer:]
    cosine, sine = twiddles(outer, inner, size)
    cosine, sine = cosine.transpose(1, 0, 2, 3), sine.transpose(1, 0, 2, 3)
    turned = jnp.stack(
        [real_part * cosine + imag_part * sine, imag_part * cosine - real_part * sine]
    ).astype(jnp.bfloat16)
    turned = turned.transpose(0, 3, 2, 1, 4).reshape(2 * inner, count, outer, lanes)
    return split_product("ab,bskc->askc", inner_table(inner, 1.0), turned, exact=False)


def fft_inverse(spectrum, length):
    twice, count, outer, lanes = spectrum.shape
    inner = twice // 2
    size = outer * inner
    half = outer // 2
    stage = split_product("ab,bskc->askc", inner_table(inner, -1.0), spectrum, exact=False)
    real_part, imag_part = stage[:inner], stage[inner:]
    cosine, sine = twiddles(outer, inner, size)
    cosine, sine = cosine.transpose(2, 0, 1, 3), sine.transpose(2, 0, 1, 3)
    turned = jnp.stack(
        [real_part * cosine - imag_part * sine, imag_part * cosine + real_part * sine]
    ).astype(jnp.bfloat16)
    turned = turned.transpose(0, 3, 2, 1, 4).reshape(2 * outer, count, inner, lanes)
    phase = 2.0 * np.pi * np.outer(np.arange(half), np.arange(outer)) / outer
    last = np.concatenate([np.cos(phase), -np.sin(phase)], 1) / size
    result = split_product("nk,ksqb->nsqb", last, turned, exact=False)
    return result.transpose(1, 0, 2, 3).reshape(count, length, lanes)


def spectral_products(spectra):
    inner = spectra.shape[0] // 2
    parts = [(spectra[:inner, i], spectra[inner:, i]) for i in range(3)]
    (f_re, f_im), (m_re, m_im), (g_re, g_im) = parts
    conv = jnp.concatenate([m_re * f_re - m_im * f_im, m_re * f_im + m_im * f_re], 0)
    back = jnp.concatenate([g_re * f_re + g_im * f_im, g_im * f_re - g_re * f_im], 0)
    cross = jnp.concatenate([g_re * m_re + g_im * m_im, g_im * m_re - g_re * m_im], 0)
    return jnp.stack([conv, back, cross], 1)


def all_sum(data, axis):
    size = lax.axis_size(axis)
    total = data
    for step in range(1, size):
        total = total + lax.ppermute(data, axis, [(i, (i + step) % size) for i in range(size)])
    return total


def mesh_sum(data, axes):
    count = 1
    for axis in axes:
        count *= lax.axis_size(axis)
    rows, chans = data.shape
    pieces = data.reshape(rows, count, chans // count).transpose(1, 0, 2)
    mine = jnp.sum(lax.all_to_all(pieces, axes, 0, 0, tiled=True), axis=0)
    spread = jnp.broadcast_to(mine[None], (count,) + mine.shape)
    gathered = lax.all_to_all(spread, axes, 0, 0, tiled=True)
    return gathered.transpose(1, 0, 2).reshape(rows, chans)


def halving_rows(data, axis):
    size = lax.axis_size(axis)
    index = lax.axis_index(axis)
    blocks = data.reshape(size, data.shape[0] // size, data.shape[1])
    step = size // 2
    while step >= 1:
        half = blocks.shape[0] // 2
        upper = (index // step) % 2 == 1
        keep = jnp.where(upper, blocks[half:], blocks[:half])
        give = jnp.where(upper, blocks[:half], blocks[half:])
        blocks = keep + lax.ppermute(give, axis, [(i, i ^ step) for i in range(size)])
        step //= 2
    return blocks.reshape(-1, data.shape[1])


def route_filter_grad(block, rows):
    parts = lax.axis_size("ctx")
    groups = lax.axis_size("dp")
    ratio = parts // groups
    pieces = block.reshape(ratio, rows, block.shape[1])
    columns = []
    for lane_block in range(ratio):
        total = None
        for piece in range(ratio):
            pairs = [
                (sd * parts + sc, (sc // ratio) * parts + sd * ratio + piece)
                for sd in range(groups)
                for sc in range(lane_block, parts, ratio)
            ]
            got = lax.ppermute(pieces[piece], ("dp", "ctx"), pairs)
            total = got if total is None else total + got
        columns.append(total)
    return jnp.concatenate(columns, 1)


def halving_scatter(data, axis):
    size = lax.axis_size(axis)
    index = lax.axis_index(axis)
    rows, chans = data.shape
    blocks = data.reshape(rows, size, chans // size)
    step = size // 2
    while step >= 1:
        half = blocks.shape[1] // 2
        upper = (index // step) % 2 == 1
        keep = jnp.where(upper, blocks[:, half:], blocks[:, :half])
        give = jnp.where(upper, blocks[:, :half], blocks[:, half:])
        blocks = keep + lax.ppermute(give, axis, [(i, i ^ step) for i in range(size)])
        step //= 2
    return blocks.reshape(rows, chans // size)


def epilogue_kernel(conv_ref, back_ref, src_ref, up_ref, mask_ref, w_ref, skip_ref, out_ref, stats_ref):
    wide, narrow = jnp.float32, jnp.bfloat16
    taps = w_ref.shape[1]
    head = taps - 1
    frame = src_ref.shape[1]
    rows = out_ref.shape[1]

    def mask(i):
        return mask_ref[i] > 0.5

    def down(x, by):
        return pltpu.roll(x, by, 0) if by else x

    def lift(x, by):
        return pltpu.roll(x, frame - by, 0) if by else x

    sources = [src_ref[i].astype(wide) for i in range(3)]
    weights = w_ref[...]
    shorts = []
    for i in range(3):
        total = weights[i, 0:1] * sources[i]
        for off in range(1, taps):
            total = total + jnp.where(mask(off), weights[i, off : off + 1] * down(sources[i], off), 0.0)
        shorts.append(total.astype(narrow).astype(wide))
    q_short, k_short, v_short = shorts
    upstream = up_ref[...].astype(wide)
    skip = skip_ref[...]
    mixed = (k_short * v_short).astype(narrow).astype(wide)
    grad_conv = (upstream * q_short).astype(narrow).astype(wide)
    conv = conv_ref[...].astype(wide) + skip * mixed
    grad_mixed = back_ref[...].astype(wide) + skip * grad_conv
    own = mask(2 * taps)
    out_ref[0] = lift(q_short * conv, head)[:rows].astype(narrow)
    grads = [upstream * conv, grad_mixed * v_short, grad_mixed * k_short]
    stats = []
    for i in range(3):
        grad = grads[i]
        acc = weights[i, 0:1] * grad
        stats.append(jnp.sum(jnp.where(own, sources[i] * grad, 0.0), axis=0, keepdims=True))
        for off in range(1, taps):
            later = lift(jnp.where(mask(taps + off), grad, 0.0), off)
            acc = acc + weights[i, off : off + 1] * later
            lagged = jnp.where(own & mask(off), down(sources[i], off) * grad, 0.0)
            stats.append(jnp.sum(lagged, axis=0, keepdims=True))
        out_ref[1 + i] = lift(acc, head)[:rows].astype(narrow)
    stats.append(jnp.sum(jnp.where(own, grad_conv * mixed, 0.0), axis=0, keepdims=True))
    width = stats[0].shape[1]
    stats.append(jnp.zeros((stats_ref.shape[0] - len(stats), width), wide))
    stats_ref[...] = jnp.concatenate(stats, 0)


def epilogue(back, sources, upstream, masks, short_weights, skip, rows):
    _, frame, chans = back.shape
    taps = short_weights.shape[1]
    block = 512 if chans % 512 == 0 else chans
    grid = (chans // block,)
    stat_rows = 16
    return pl.pallas_call(
        epilogue_kernel,
        grid=grid,
        in_specs=[
            pl.BlockSpec((None, frame, block), lambda c: (0, 0, c)),
            pl.BlockSpec((None, frame, block), lambda c: (1, 0, c)),
            pl.BlockSpec((3, frame, block), lambda c: (0, 0, c)),
            pl.BlockSpec((frame, block), lambda c: (0, c)),
            pl.BlockSpec(masks.shape, lambda c: (0, 0, 0)),
            pl.BlockSpec((3, taps, block), lambda c: (0, 0, c)),
            pl.BlockSpec((1, block), lambda c: (0, c)),
        ],
        out_specs=[
            pl.BlockSpec((4, rows, block), lambda c: (0, 0, c)),
            pl.BlockSpec((stat_rows, block), lambda c: (0, c)),
        ],
        out_shape=[
            jax.ShapeDtypeStruct((4, rows, chans), jnp.bfloat16),
            jax.ShapeDtypeStruct((stat_rows, chans), jnp.float32),
        ],
    )(back, back, sources, upstream, masks, short_weights, skip[None])


def local(query, keys, values, cotangent, long_filter, short_weights, skip, lengths):
    parts = lax.axis_size("ctx")
    index = lax.axis_index("ctx")
    groups = lax.axis_size("dp")
    q_rows, k_rows, v_rows, c_rows = query[0], keys[0], values[0], cotangent[0]
    rows, chans = q_rows.shape
    taps = short_weights.shape[1]
    head = taps - 1
    seq_len = rows * parts
    lanes = chans // parts
    ext = rows + head
    frame = -(-(rows + 2 * head) // 8) * 8
    doc_len = lengths[0]
    starts = jnp.cumsum(doc_len) - doc_len

    position = index * rows + jnp.arange(ext, dtype=jnp.int32)
    begin = jnp.max(jnp.where(starts[None, :] <= position[:, None], starts[None, :], 0), axis=1)
    valid = position[None, :] - jnp.arange(taps, dtype=jnp.int32)[:, None] >= begin[None, :]
    valid_after = valid & (position < seq_len)[None, :]

    prev = shifted(jnp.stack([a[rows - head :] for a in (q_rows, k_rows, v_rows)]), "ctx", 1)
    padded = [
        jnp.concatenate([prev[i], src], 0).astype(jnp.float32)
        for i, src in enumerate((q_rows, k_rows, v_rows))
    ]

    def short_forward(wide, weights):
        summed = weights[0] * wide[head : head + rows]
        for offset in range(1, taps):
            begin_at = head - offset
            summed = summed + jnp.where(
                valid[offset, :rows][:, None], weights[offset] * wide[begin_at : begin_at + rows], 0.0
            )
        return summed.astype(jnp.bfloat16).astype(jnp.float32)

    q_short = short_forward(padded[0], short_weights[0])
    k_short = short_forward(padded[1], short_weights[1])
    v_short = short_forward(padded[2], short_weights[2])
    mixed = (k_short * v_short).astype(jnp.bfloat16)
    grad_conv = (c_rows.astype(jnp.float32) * q_short).astype(jnp.bfloat16)

    chunks = 2 if lanes % 2 == 0 else 1
    width = lanes // chunks

    def to_columns(data, part):
        count = data.shape[0]
        split = data.reshape(count, rows, parts, chunks, width)[:, :, :, part]
        moved = lax.all_to_all(split.transpose(0, 2, 1, 3), "ctx", 1, 1, tiled=True)
        return moved.reshape(count, seq_len, width)

    sent = jnp.stack([long_filter, mixed, grad_conv])
    returned = []
    lagged_parts = []
    previous = None
    for part in range(chunks):
        columns = to_columns(sent, part)
        if previous is not None:
            columns, previous = lax.optimization_barrier((columns, previous))
            returned.append(lax.all_to_all(previous, "ctx", 1, 1, tiled=True))
        spectra = fft_forward(columns)
        raw = fft_inverse(spectral_products(spectra), seq_len)
        lagged_parts.append(raw[2])
        raw = raw[:2].astype(jnp.bfloat16)
        raw = jnp.concatenate(
            [jnp.zeros((2, head, width), raw.dtype), raw, jnp.zeros((2, frame - rows - head, width), raw.dtype)], 1
        )
        blocks = jnp.stack([raw[:, j * rows : j * rows + frame] for j in range(parts)], 1)
        previous = blocks
    following = jnp.stack([a[:head] for a in (q_rows, k_rows, v_rows, c_rows)])
    following, previous = lax.optimization_barrier((following, previous))
    returned.append(lax.all_to_all(previous, "ctx", 1, 1, tiled=True))
    nxt = shifted(following, "ctx", -1)
    back = jnp.stack(returned, 3).transpose(0, 2, 1, 3, 4).reshape(2, frame, chans)
    lagged = halving_rows(jnp.concatenate(lagged_parts, 1), "dp")
    filter_part = route_filter_grad(lagged, rows)

    spot = index * rows - head + jnp.arange(frame, dtype=jnp.int32)
    spot_begin = jnp.max(jnp.where(starts[None, :] <= spot[:, None], starts[None, :], 0), axis=1)
    spot_valid = spot[None, :] - jnp.arange(taps, dtype=jnp.int32)[:, None] >= spot_begin[None, :]
    spot_after = spot_valid & ((spot >= 0) & (spot < seq_len))[None, :]
    spot_own = ((spot >= index * rows) & (spot < index * rows + rows))[None, :]
    masks = jnp.concatenate([spot_valid, spot_after, spot_own], 0).astype(jnp.float32)
    masks = jnp.concatenate([masks, jnp.zeros(((-masks.shape[0]) % 8, frame), jnp.float32)], 0)
    tail = frame - rows - 2 * head
    sources = jnp.stack([
        jnp.concatenate([prev[i], src, jnp.zeros((head + tail, chans), src.dtype)], 0)
        for i, src in enumerate((q_rows, k_rows, v_rows))
    ])
    framed_up = jnp.concatenate(
        [jnp.zeros((head, chans), c_rows.dtype), c_rows, jnp.zeros((head + tail, chans), c_rows.dtype)], 0
    )
    sources = lax.dynamic_update_slice(sources, nxt[:3], (0, head + rows, 0))
    framed_up = lax.dynamic_update_slice(framed_up, nxt[3], (head + rows, 0))
    outs, stats = epilogue(back, sources, framed_up, masks[:, :, None], short_weights, skip, rows)
    summed = mesh_sum(stats[: 3 * taps + 1], ("dp", "ctx"))
    gated, grad_q, grad_k, grad_v = outs[0], outs[1], outs[2], outs[3]
    scale = 1.0 / (groups * seq_len)
    return (
        gated[None],
        grad_q.astype(jnp.bfloat16)[None],
        grad_k.astype(jnp.bfloat16)[None],
        grad_v.astype(jnp.bfloat16)[None],
        filter_part * scale,
        summed[: 3 * taps].reshape(3, taps, chans) * scale,
        summed[3 * taps] * scale,
    )


def solution(mesh):
    in_specs = (
        P("dp", "ctx", None),
        P("dp", "ctx", None),
        P("dp", "ctx", None),
        P("dp", "ctx", None),
        P("ctx", None),
        P(),
        P(),
        P("dp", None),
    )
    out_specs = (
        P("dp", "ctx", None),
        P("dp", "ctx", None),
        P("dp", "ctx", None),
        P("dp", "ctx", None),
        P("ctx", "dp"),
        P(),
        P(),
    )
    return jax.shard_map(local, mesh=mesh, in_specs=in_specs, out_specs=out_specs, check_vma=False)
```
